32 devices in a mesh: dp: 4 (over y, core), fsdp: 8 (over z, x).
Axes of the slice: x: 2, y: 2, z: 4, core: 2. Of those that a mesh axis runs over, the one named last changes fastest.
Arguments:
- tokens: bfloat16 [43520, 1024], P(('dp', 'fsdp')), may hold values from -6 to 6
- cond: bfloat16 [64, 1024], P(('dp', 'fsdp')), may hold values from -6 to 6
- stop_scale: int32 [64], P(('dp', 'fsdp')), may hold values from 5 to 9
- w_ada: bfloat16 [1024, 6144], P('fsdp'), may hold values from -0.1875 to 0.1875
- w_qkv: bfloat16 [1024, 3072], P('fsdp'), may hold values from -0.1875 to 0.1875
- w_proj: bfloat16 [1024, 1024], P('fsdp'), may hold values from -0.5 to 0.5
- w_fc1: bfloat16 [1024, 4096], P('fsdp'), may hold values from -0.1875 to 0.1875
- w_fc2: bfloat16 [4096, 1024], P('fsdp'), may hold values from -0.125 to 0.125
- head_log_scale: float32 [16], replicated, may hold values from 1.9 to 2.5
- cotangent: bfloat16 [43520, 1024], P(('dp', 'fsdp')), may hold values from -6 to 6
Outputs:
- out: bfloat16 [43520, 1024], P(('dp', 'fsdp'))
- grad_tokens: bfloat16 [43520, 1024], P(('dp', 'fsdp'))
- grad_cond: bfloat16 [64, 1024], P(('dp', 'fsdp'))
- grad_w_ada: float32 [1024, 6144], P('fsdp')
- grad_w_qkv: float32 [1024, 3072], P('fsdp')
- grad_w_proj: float32 [1024, 1024], P('fsdp')
- grad_w_fc1: float32 [1024, 4096], P('fsdp')
- grad_w_fc2: float32 [4096, 1024], P('fsdp')
- grad_head_log_scale: float32 [16], replicated
- rms: float32 [64, 3], P(('dp', 'fsdp'))
The draws below stay inside these ranges and needn't reach their ends.
Inputs may be any that keep to these rules, and one draw needn't show every extreme that they name: `stop_scale`: index of the last scale that holds real tokens of each item.
All inputs are finite; a program needn't handle non-finite values.
Results may differ from the reference program's by a relative error of at most 0.018.
Values may be sent and summed in bfloat16 or wider, within the bound.
No kernel may reach another device: no remote copies, remote signals or barrier semaphores. Data moves between devices by JAX's collectives and lax.ppermute only.
A program may use at most 384 MiB of HBM per device.

```python
import jax
import jax.numpy as jnp
from jax import lax

D = 1024
HEADS = 16
HEAD = 64
FF = 4096
SCALES = 10
SEQ = 680
ITEMS_DEV = 2
ITEMS = 64
TOKENS = 43520


def plant(entries, rng, smallest, largest):
    dims = entries.shape
    spot = [jax.random.randint(jax.random.fold_in(rng, axis), (), 0, dims[axis]) for axis in range(len(dims))]
    entries = entries.at[tuple(spot)].set(smallest)
    longest = dims.index(max(dims))
    spot[longest] = (spot[longest] + 1) % dims[longest]
    return entries.at[tuple(spot)].set(largest)


def levels(rng, shape, split, smallest, high):
    gain, own = 1.0, jax.random.fold_in(rng, 6)
    for dim, shards_of in split:
        steps = jnp.exp(jax.random.uniform(jax.random.fold_in(own, dim), (shards_of,), jnp.float32, smallest / len(split), high / len(split)))
        gain = gain * jnp.repeat(steps, shape[dim] // shards_of).reshape([-1 if axis == dim else 1 for axis in range(len(shape))])
    return gain


def normal_values(rng, dims, deviation, limit, shards=(), kind=jnp.bfloat16):
    level = levels(rng, dims, shards, -0.22, 0.18) if shards else 1.0
    entries = jax.random.normal(rng, dims, jnp.float32) * deviation * level
    return jnp.minimum(jnp.maximum(entries, -limit), limit).astype(kind)


def setup_inputs(seed: int = 0) -> dict:
    splits = jax.random.split(jax.random.key(seed), 11)
    return {
        "tokens": normal_values(splits[0], (TOKENS, D), 1.0, 6.0, ((0, 32),)),
        "cond": normal_values(splits[1], (ITEMS, D), 1.0, 6.0, ((0, 32),)),
        "stop_scale": plant(jax.random.randint(splits[2], (ITEMS,), SCALES // 2, SCALES), jax.random.fold_in(splits[2], 1), SCALES // 2, SCALES - 1).astype(jnp.int32),
        "w_ada": normal_values(splits[3], (D, 6 * D), D ** -0.5, 0.1875, ((0, 8),)),
        "w_qkv": normal_values(splits[4], (D, 3 * D), D ** -0.5, 0.1875, ((0, 8),)),
        "w_proj": normal_values(splits[5], (D, D), (D // 8) ** -0.5, 0.5, ((0, 8),)),
        "w_fc1": normal_values(splits[6], (D, FF), D ** -0.5, 0.1875, ((0, 8),)),
        "w_fc2": normal_values(splits[7], (FF, D), (FF // 2) ** -0.5, 0.125, ((0, 8),)),
        "head_log_scale": jnp.clip(jax.random.uniform(splits[8], (HEADS,), jnp.float32, 1.9, 2.5), 1.9, 2.5),
        "cotangent": normal_values(splits[9], (TOKENS, D), 1.0, 6.0, ((0, 32),)),
    }


PATCHES = (1, 2, 3, 4, 5, 6, 8, 10, 13, 16)
EPS = 1e-06
GELU_COEF = 0.7978845608028654

@jax.custom_vjp
def low(v):
    return lax.optimization_barrier(v.astype(jnp.bfloat16)).astype(jnp.float32)

@jax.custom_vjp
def low_back(v):
    return v

def low_keep(v):
    return (low(v), None)

def low_pass(kept, grad):
    return (grad,)

def back_keep(v):
    return (v, None)

def back_low(kept, grad):
    return (low(grad),)
low.defvjp(low_keep, low_pass)
low_back.defvjp(back_keep, back_low)

def scale_table(scale_total):
    pieces = [jnp.full((PATCHES[index] * PATCHES[index],), index, dtype=jnp.int32) for index in range(scale_total)]
    return jnp.concatenate(pieces).astype(jnp.int32)

def silu_act(values):
    return values * jax.nn.sigmoid(values)

def gelu_act(values):
    return 0.5 * values * (1.0 + jnp.tanh(GELU_COEF * (values + 0.044715 * values * values * values)))

def layer_norm(values):
    centred = values - lax.optimization_barrier(jnp.mean(values, -1, keepdims=True))
    return centred * lax.rsqrt(lax.optimization_barrier(jnp.mean(centred * centred, -1, keepdims=True)) + EPS)

def modulate(values, scale_term, shift_term):
    return layer_norm(values) * (1.0 + scale_term) + shift_term

def unit_rows(values):
    return values * lax.rsqrt(lax.optimization_barrier(jnp.sum(values * values, -1, keepdims=True)) + EPS)

def forward_pass(tokens, cond, w_ada, w_qkv, w_proj, w_fc1, w_fc2, head_log_scale, valid, allowed):
    highest = lax.Precision.HIGHEST
    group_size = tokens.shape[0]
    silu_cond = low(silu_act(cond))
    modulation = low_back(jnp.dot(silu_cond, w_ada, precision=highest))
    blocks = [modulation[:, None, portion * D:(portion + 1) * D] for portion in range(6)]
    gamma_one, gamma_two, scale_one, scale_two, shift_one, shift_two = blocks
    normed_one = low(modulate(tokens, scale_one, shift_one))
    projected = low_back(jnp.einsum('gnd,de->gne', normed_one, w_qkv, precision=highest))
    split_heads = projected.reshape(group_size, SEQ, 3, HEADS, HEAD)
    query_rows = low(unit_rows(split_heads[:, :, 0]) * jnp.exp(head_log_scale)[:, None])
    key_rows = low(unit_rows(split_heads[:, :, 1]))
    value_rows = low(split_heads[:, :, 2])
    scores = low_back(jnp.einsum('gqhc,gkhc->ghqk', query_rows, key_rows, precision=highest))
    key_allowed = allowed[:, None]
    zero = jnp.zeros((), scores.dtype)
    log_total = jnp.log(lax.optimization_barrier(jnp.sum(jnp.where(key_allowed, jnp.exp(scores), zero), -1)))
    weights_low = low(jnp.where(key_allowed, jnp.exp(scores - log_total[..., None]), zero))
    attended = jnp.einsum('ghqk,gkhc->gqhc', weights_low, value_rows, precision=highest)
    attended = low(low_back(attended)).reshape(group_size, SEQ, D)
    attn_out = low_back(jnp.einsum('gnd,de->gne', attended, w_proj, precision=highest))
    branch_one = valid * gamma_one * attn_out
    middle = tokens + branch_one
    normed_two = low(modulate(middle, scale_two, shift_two))
    hidden = low_back(jnp.einsum('gnd,df->gnf', normed_two, w_fc1, precision=highest))
    activated = low(gelu_act(hidden))
    mlp_out = low_back(jnp.einsum('gnf,fd->gnd', activated, w_fc2, precision=highest))
    branch_two = valid * gamma_two * mlp_out
    stream = middle + branch_two
    counted = lax.optimization_barrier(jnp.sum(valid[:, :, 0], 1)) * jnp.asarray(float(D), valid.dtype)

    def root_mean(field_rows):
        return jnp.sqrt(lax.optimization_barrier(jnp.sum(valid * field_rows * field_rows, (1, 2))) / counted + EPS)
    rms_rows = jnp.stack([root_mean(stream), root_mean(branch_one), root_mean(branch_two)], 1)
    return (stream, rms_rows)

def reference(tokens, cond, stop_scale, w_ada, w_qkv, w_proj, w_fc1, w_fc2, head_log_scale, cotangent):
    scale_ids = scale_table(SCALES)
    groups_count = ITEMS // ITEMS_DEV
    float_weights = (w_ada.astype(jnp.float32), w_qkv.astype(jnp.float32), w_proj.astype(jnp.float32), w_fc1.astype(jnp.float32), w_fc2.astype(jnp.float32), head_log_scale.astype(jnp.float32))
    stacked = (tokens.astype(jnp.float32).reshape(groups_count, ITEMS_DEV, SEQ, D), cond.astype(jnp.float32).reshape(groups_count, ITEMS_DEV, D), stop_scale.astype(jnp.int32).reshape(groups_count, ITEMS_DEV), cotangent.astype(jnp.float32).reshape(groups_count, ITEMS_DEV, SEQ, D))

    def one_group(carried, pieces):
        token_block, cond_block, stop_block, cot_block = pieces
        stop_int = stop_block.astype(jnp.int32)
        valid_bool = scale_ids[None, :] <= stop_int[:, None]
        allowed = (scale_ids[None, None, :] <= scale_ids[None, :, None]) & valid_bool[:, None, :]
        valid = valid_bool.astype(jnp.float32)[:, :, None]

        def wrapped(token_in, cond_in, ada_in, qkv_in, proj_in, fc1_in, fc2_in, scale_in):
            return forward_pass(token_in, cond_in, ada_in, qkv_in, proj_in, fc1_in, fc2_in, scale_in, valid, allowed)
        stream, pull, rms_rows = jax.vjp(wrapped, token_block, cond_block, float_weights[0], float_weights[1], float_weights[2], float_weights[3], float_weights[4], float_weights[5], has_aux=True)
        gradients = pull(cot_block)
        carried = tuple(((running_sum + new_grad).astype(jnp.float32) for running_sum, new_grad in zip(carried, gradients[2:])))
        return (carried, (stream.astype(jnp.bfloat16), gradients[0].astype(jnp.bfloat16), gradients[1].astype(jnp.bfloat16), rms_rows.astype(jnp.float32)))
    initial = tuple((jnp.zeros(weight_in.shape, jnp.float32) for weight_in in float_weights))
    totals, (out_blocks, grad_tok, grad_con, rms_blocks) = lax.scan(one_group, initial, stacked)
    return (out_blocks.reshape(TOKENS, D), grad_tok.reshape(TOKENS, D), grad_con.reshape(ITEMS, D), totals[0], totals[1], totals[2], totals[3], totals[4], totals[5], rms_blocks.reshape(ITEMS, 3))
```

```python
import functools

import jax
import jax.numpy as jnp
import numpy as np
from jax import lax
from jax.experimental import pallas as pl
from jax.experimental.pallas import tpu as pltpu
from jax.sharding import PartitionSpec as P

PATCHES = (1, 2, 3, 4, 5, 6, 8, 10, 13, 16)
EPS = 1e-06
GELU_COEF = 0.7978845608028654
AXES = ("dp", "fsdp")
LOW = jnp.bfloat16
WIDE = jnp.float32
NN = (((1,), (0,)), ((), ()))
NT = (((1,), (1,)), ((), ()))
TN = (((0,), (0,)), ((), ()))
VMEM_LIMIT = 56 << 20
BLOCKED = -30000.0


def dot(left, right, dims=NN):
    return lax.dot_general(left, right, dims, preferred_element_type=WIDE)


def two_parts(values):
    high = values.astype(LOW)
    return high, (values - high.astype(WIDE)).astype(LOW)


def split_dot(values, table):
    high, rest = two_parts(values)
    return dot(high, table) + dot(rest, table)


class Place:
    def __init__(self, dp_count, fsdp_count):
        self.grouped = dp_count == 4 and fsdp_count == 8
        self.dp_count = dp_count
        self.fsdp_count = fsdp_count
        dp_index = lax.axis_index("dp")
        fsdp_index = lax.axis_index("fsdp")
        self.dp_index, self.fsdp_index = dp_index, fsdp_index
        self.y, self.c = dp_index // 2, dp_index % 2
        self.z, self.x = fsdp_index // 2, fsdp_index % 2
        self.table = jnp.stack([self.y, self.c, self.z, self.x]).astype(jnp.int32)


def hop(values, dy=0, dc=0, dz=0, dx=0):
    pairs = [
        (d * 8 + f, (d ^ (2 * dy + dc)) * 8 + (f ^ (2 * dz + dx)))
        for d in range(4)
        for f in range(8)
    ]
    return lax.ppermute(values, AXES, pairs)


def gather_parts(place, shard, order, after=None):
    if not place.grouped:
        return [lax.all_gather(shard, "fsdp", axis=0, tiled=True)], None
    rows, columns = shard.shape
    quarter = columns // 4
    own = lax.dynamic_slice(shard, (0, (place.c * 2 + place.y) * quarter), (rows, quarter))
    if after is not None:
        own, _ = lax.optimization_barrier((own, after))
    stack = jnp.concatenate([own] + [hop(own, dz=k) for k in (1, 2, 3)], 0)
    if order == "xy":
        over_x = hop(stack, dx=1)
        over_y = hop(stack, dy=1)
        over_both = hop(over_x, dy=1)
    else:
        over_y = hop(stack, dy=1)
        over_x = hop(stack, dx=1)
        over_both = hop(over_y, dx=1)
    half = [stack, over_x, over_y, over_both]
    return half + [hop(piece, dc=1) for piece in half], stack


def load_weight(place_ref, pieces, buffer, sems):
    copies = []
    if len(pieces) == 1:
        copies.append(pltpu.make_async_copy(pieces[0], buffer, sems.at[0]))
    else:
        rows = pieces[0].shape[0] // 4
        quarter = pieces[0].shape[1]
        for number, piece in enumerate(pieces):
            core, side, across = number // 4, (number // 2) % 2, number % 2
            column = ((place_ref[1] ^ core) * 2 + (place_ref[0] ^ side)) * quarter
            for k in range(4):
                row = ((place_ref[2] ^ k) * 2 + (place_ref[3] ^ across)) * rows
                copies.append(
                    pltpu.make_async_copy(
                        piece.at[pl.ds(k * rows, rows), :],
                        buffer.at[
                            pl.ds(pl.multiple_of(row, 128), rows),
                            pl.ds(pl.multiple_of(column, 128), quarter),
                        ],
                        sems.at[number * 4 + k],
                    )
                )
    for copy in copies:
        copy.start()
    for copy in copies:
        copy.wait()


def add(left, right):
    return left.astype(WIDE) + right.astype(WIDE)


def reduce_rows(place, keep, send, rows, order):
    if not place.grouped:
        flip = place.c == 1
        full = jnp.concatenate([jnp.where(flip, send, keep), jnp.where(flip, keep, send)], 1)
        part = lax.psum_scatter(full, "fsdp", scatter_dimension=0, tiled=True)
        return lax.psum(part, "dp").astype(WIDE)
    quarter = keep.shape[1] // 2
    y, z, x = place.y, place.z, place.x

    def over_y(values):
        count = values.shape[0]
        mine = lax.dynamic_slice(values, (0, y * quarter), (count, quarter))
        other = lax.dynamic_slice(values, (0, (1 - y) * quarter), (count, quarter))
        return add(mine, hop(other, dy=1)).astype(LOW)

    def over_x(values):
        width = values.shape[1]
        values = values.reshape(4, 2, rows, width)
        size = (4, 1, rows, width)
        mine = lax.dynamic_slice(values, (0, x, 0, 0), size).reshape(4 * rows, width)
        other = lax.dynamic_slice(values, (0, 1 - x, 0, 0), size).reshape(4 * rows, width)
        return add(mine, hop(other, dx=1)).astype(LOW)

    values = add(keep, hop(send, dc=1)).astype(LOW)
    values = over_x(over_y(values)) if order == "yx" else over_y(over_x(values))
    total = lax.dynamic_slice(values, (z * rows, 0), (rows, quarter)).astype(WIDE)
    for k in (1, 2, 3):
        piece = lax.dynamic_slice(values, ((z ^ k) * rows, 0), (rows, quarter))
        total = total + hop(piece, dz=k).astype(WIDE)
    own = total.astype(LOW)
    from_y = hop(own, dy=1)
    from_c = hop(own, dc=1)
    from_both = hop(from_y, dc=1)
    here = place.c * 2 + y

    def pick(index):
        apart = index ^ here
        return jnp.where(
            apart == 0, own, jnp.where(apart == 1, from_y, jnp.where(apart == 2, from_c, from_both))
        )

    return jnp.concatenate([pick(index) for index in range(4)], 1).astype(WIDE)


def reorder(stack, count, flip):
    return jnp.concatenate(
        [lax.dynamic_slice_in_dim(stack, i ^ flip, 1, axis=0) for i in range(count)], 0
    )


def gather_small(place, values, whole):
    if not place.grouped:
        return lax.all_gather(values, AXES if whole else "fsdp", axis=0, tiled=True)
    count = values.shape[0]
    stack = jnp.stack([values] + [hop(values, dz=k) for k in (1, 2, 3)])
    stack = jnp.stack([stack, hop(stack, dx=1)], 1)
    stack = stack.reshape((8,) + values.shape)
    ordered = reorder(stack, 8, place.fsdp_index)
    ordered = ordered.reshape((8 * count,) + values.shape[1:])
    if not whole:
        return ordered
    stack = jnp.stack([ordered, hop(ordered, dc=1)])
    stack = jnp.concatenate([stack, hop(stack, dy=1)], 0)
    ordered = reorder(stack, 4, place.dp_index)
    return ordered.reshape((32 * count,) + values.shape[1:])


def scatter_small(place, values):
    if not place.grouped:
        return lax.psum_scatter(values, "fsdp", scatter_dimension=0, tiled=True)
    count = values.shape[0] // 8
    tail = values.shape[1:]
    values = values.reshape((4, 2, count) + tail)
    mine = lax.dynamic_index_in_dim(values, place.x, 1, keepdims=False)
    other = lax.dynamic_index_in_dim(values, 1 - place.x, 1, keepdims=False)
    values = mine + hop(other, dx=1)
    total = lax.dynamic_index_in_dim(values, place.z, 0, keepdims=False)
    for k in (1, 2, 3):
        total = total + hop(
            lax.dynamic_index_in_dim(values, place.z ^ k, 0, keepdims=False), dz=k
        )
    return total


def mask_tables(length):
    scale_ids = np.concatenate([np.full(side * side, i) for i, side in enumerate(PATCHES)])
    spare = np.arange(128) & 63
    slot = spare[None, :] - 2
    scale_column = scale_ids[:, None]
    later = (slot >= 0) & (slot < len(PATCHES)) & (slot > scale_column)
    query_side = np.where(later, BLOCKED, 0.0)
    key_side = np.where(slot == scale_column, 1.0, 0.0) + np.where(spare[None, :] < 2, 1.0, 0.0)
    return jnp.asarray(query_side, LOW), jnp.asarray(key_side, LOW)


FORWARD_BLOCKS = ((0, 240, 256), (240, 416, 512), (416, 680, 680))
BACKWARD_BLOCKS = ((424, 680, 680), (240, 424, 432), (0, 240, 256))


def attend_kernel(q_ref, k_ref, v_ref, qm_ref, km_ref, out_ref, extra_ref):
    query, key, value = q_ref[0], k_ref[0], v_ref[0]
    query_mask, key_mask = qm_ref[...], km_ref[...]
    lane = lax.broadcasted_iota(jnp.int32, query.shape, 1)
    even = lane < 64
    ones = jnp.ones_like(value)
    heads = (
        (jnp.where(even, query, query_mask), jnp.where(even, key, key_mask), jnp.where(even, value, ones)),
        (jnp.where(even, query_mask, query), jnp.where(even, key_mask, key), jnp.where(even, ones, value)),
    )
    for start, stop, keys in FORWARD_BLOCKS:
        sums = []
        for query_head, key_head, value_head in heads:
            scores = dot(query_head[start:stop], key_head[:keys], NT)
            sums.append(dot(jnp.exp(scores).astype(LOW), value_head[:keys]))
        side = even[start:stop]
        chosen = jnp.where(side, sums[0], sums[1])
        totals = jnp.where(side, sums[1], sums[0])
        out_ref[0, start:stop, :] = (chosen / pltpu.roll(totals, 64, 1)).astype(LOW)
        high, rest = two_parts(-jnp.log(totals))
        spare = lane[start:stop] & 63
        extra_ref[0, start:stop, :] = jnp.where(
            spare == 0, high, jnp.where(spare == 1, rest, query_mask[start:stop])
        )


def attend(query, key, value, query_mask, key_mask):
    items, length, width = query.shape
    pairs = width // 128
    block = pl.BlockSpec((1, length, 128), lambda i, p: (i, 0, p))
    table = pl.BlockSpec((length, 128), lambda i, p: (0, 0))
    return pl.pallas_call(
        attend_kernel,
        grid=(items, pairs),
        in_specs=[block, block, block, table, table],
        out_specs=[block, block],
        out_shape=[jax.ShapeDtypeStruct(query.shape, LOW)] * 2,
        compiler_params=pltpu.CompilerParams(vmem_limit_bytes=VMEM_LIMIT),
        cost_estimate=pl.CostEstimate(
            flops=items * pairs * length * length * 128 * 10,
            transcendentals=items * pairs * 2 * length * length,
            bytes_accessed=items * length * width * 10,
        ),
        name="attend",
    )(query, key, value, query_mask, key_mask)


def side_table(cross):
    first = lax.broadcasted_iota(jnp.int32, (128, 128), 0) < 64
    second = lax.broadcasted_iota(jnp.int32, (128, 128), 1) < 64
    return jnp.where((first != second) if cross else (first == second), 1.0, 0.0).astype(LOW)


def attend_back_kernel(
    q_ref, k_ref, v_ref, extra_ref, km_ref, out_ref, grad_ref, rq_ref, rk_ref, gain_ref,
    dq_ref, dk_ref, dv_ref, head_ref, value_sum, key_sum, query_sum,
):
    query, key, value, extra = q_ref[0], k_ref[0], v_ref[0], extra_ref[0]
    key_mask, grad = km_ref[...], grad_ref[0]
    lane = lax.broadcasted_iota(jnp.int32, query.shape, 1)
    even = lane < 64
    spare = lane & 63
    centre = split_dot(grad.astype(WIDE) * out_ref[0].astype(WIDE), side_table(True))
    high, rest = two_parts(-centre)
    grad_extra = jnp.where(spare == 0, high, jnp.where(spare == 1, rest, jnp.zeros_like(high)))
    ones = jnp.ones_like(value)
    key_rows = key.astype(WIDE).T.astype(LOW)
    heads = (
        (jnp.where(even, query, extra), jnp.where(even, key, key_mask),
         jnp.where(even, value, ones), jnp.where(even, grad, grad_extra)),
        (jnp.where(even, extra, query), jnp.where(even, key_mask, key),
         jnp.where(even, ones, value), jnp.where(even, grad_extra, grad)),
    )
    for head, (query_head, key_head, value_head, grad_head) in enumerate(heads):
        head_rows = key_rows[64 * head : 64 * head + 64]
        for number, (start, stop, keys) in enumerate(BACKWARD_BLOCKS):
            probs = jnp.exp(dot(key_head[:keys], query_head[start:stop], NT))
            grad_probs = dot(value_head[:keys], grad_head[start:stop], NT)
            grad_scores = (probs * grad_probs).astype(LOW)
            value_part = dot(probs.astype(LOW), grad[start:stop])
            key_part = dot(grad_scores, query[start:stop])
            if number == 0:
                value_sum[head] = value_part
                key_sum[head] = key_part
            else:
                value_sum[head, :keys] += value_part
                key_sum[head, :keys] += key_part
            query_sum[start:stop, 64 * head : 64 * head + 64] = dot(head_rows[:, :keys], grad_scores).T
    head_count = rq_ref.shape[2]
    head_row = lax.broadcasted_iota(jnp.int32, (head_count, 128), 0)
    head_lane = lax.broadcasted_iota(jnp.int32, (head_count, 128), 1)
    wanted = 2 * pl.program_id(1) + jnp.where(head_lane >= 64, 1, 0)
    table = jnp.where(head_row == wanted, 1.0, 0.0).astype(LOW)
    same = side_table(False)
    gain = gain_ref[...]
    grad_query = query_sum[...] * gain
    unit_query = query.astype(WIDE) / gain
    product = unit_query * grad_query
    head_ref[0] = jnp.sum(product, 0, keepdims=True)
    dq_ref[0] = (
        split_dot(rq_ref[0], table) * (grad_query - unit_query * split_dot(product, same))
    ).astype(LOW)
    grad_key = jnp.where(even, key_sum[0], key_sum[1])
    unit_key = key.astype(WIDE)
    dk_ref[0] = (
        split_dot(rk_ref[0], table) * (grad_key - unit_key * split_dot(unit_key * grad_key, same))
    ).astype(LOW)
    dv_ref[0] = jnp.where(even, value_sum[0], value_sum[1]).astype(LOW)


def attend_back(query, key, value, extra, key_mask, out, grad, rq, rk, gain):
    items, length, width = query.shape
    pairs = width // 128
    block = pl.BlockSpec((1, length, 128), lambda i, p: (i, 0, p))
    table = pl.BlockSpec((length, 128), lambda i, p: (0, 0))
    rows = pl.BlockSpec((1, length, rq.shape[2]), lambda i, p: (i, 0, 0))
    return pl.pallas_call(
        attend_back_kernel,
        grid=(items, pairs),
        in_specs=[block] * 4 + [table, block, block, rows, rows, pl.BlockSpec((1, 128), lambda i, p: (0, p))],
        out_specs=[block] * 3 + [pl.BlockSpec((1, 1, 128), lambda i, p: (i, 0, p))],
        out_shape=[jax.ShapeDtypeStruct(query.shape, LOW)] * 3
        + [jax.ShapeDtypeStruct((items, 1, width), WIDE)],
        scratch_shapes=[
            pltpu.VMEM((2, length, 128), WIDE),
            pltpu.VMEM((2, length, 128), WIDE),
            pltpu.VMEM((length, 128), WIDE),
        ],
        compiler_params=pltpu.CompilerParams(vmem_limit_bytes=VMEM_LIMIT),
        cost_estimate=pl.CostEstimate(
            flops=items * pairs * length * length * 128 * 26,
            transcendentals=items * pairs * 2 * length * length,
            bytes_accessed=items * length * width * 22,
        ),
        name="attend_back",
    )(query, key, value, extra, key_mask, out, grad, rq, rk, gain)


def row_facts(lengths_ref, block_rows, length):
    row = pl.program_id(0) * block_rows + lax.broadcasted_iota(jnp.int32, (block_rows, 1), 0)
    second = row >= length
    end = jnp.where(second, length + lengths_ref[1], lengths_ref[0])
    return second, row < end


def per_row(ref, second):
    return jnp.where(second, ref[1:2, :], ref[0:1, :])


def add_sums(ref, start, second, values):
    ref[start : start + 1, :] += jnp.sum(jnp.where(second, 0.0, values), 0, keepdims=True)
    ref[start + 1 : start + 2, :] += jnp.sum(jnp.where(second, values, 0.0), 0, keepdims=True)


def normalize(values):
    centred = values - jnp.mean(values, -1, keepdims=True)
    scale = lax.rsqrt(jnp.mean(centred * centred, -1, keepdims=True) + EPS)
    return centred * scale, scale


def token_call(kernel, place, rows, length, lengths, blocked, full, weights, outs, sums, flops, name, scratch=()):
    block_rows = 2 * length // 5
    grid = rows // block_rows
    parts = [part for pieces in weights for part in pieces[0]]
    counts = [len(pieces[0]) for pieces in weights]
    shapes = [pieces[1] for pieces in weights]
    blocked_count, full_count, out_count = len(blocked), len(full), len(outs)

    def body(place_ref, lengths_ref, *refs):
        refs = list(refs)
        token_refs = refs[:blocked_count]
        full_refs = refs[blocked_count : blocked_count + full_count]
        cursor = blocked_count + full_count
        groups = []
        for count in counts:
            groups.append(refs[cursor : cursor + count])
            cursor += count
        out_refs = refs[cursor : cursor + out_count]
        cursor += out_count
        sum_refs = refs[cursor : cursor + sums]
        cursor += sums
        buffers = refs[cursor : cursor + len(counts)]
        cursor += len(counts)
        sems = refs[cursor : cursor + len(counts)]
        cursor += len(counts)

        @pl.when(pl.program_id(0) == 0)
        def _():
            for ref in sum_refs:
                ref[...] = jnp.zeros_like(ref)
            for pieces, buffer, sem in zip(groups, buffers, sems):
                load_weight(place_ref, pieces, buffer, sem)

        second, real = row_facts(lengths_ref, block_rows, length)
        kernel(second, real, token_refs, full_refs, buffers, out_refs, sum_refs, *refs[cursor:])

    any_space = pl.BlockSpec(memory_space=pl.ANY)
    smem = pl.BlockSpec(memory_space=pltpu.SMEM)
    moved = sum(v.size * v.dtype.itemsize for v in blocked) + sum(
        rows * width * jnp.dtype(kind).itemsize for width, kind in outs
    )
    return pl.pallas_call(
        body,
        grid=(grid,),
        in_specs=[smem, smem]
        + [pl.BlockSpec((block_rows, v.shape[1]), lambda i: (i, 0)) for v in blocked]
        + [pl.BlockSpec(v.shape, lambda i: (0, 0)) for v in full]
        + [any_space] * len(parts),
        out_specs=[pl.BlockSpec((block_rows, width), lambda i: (i, 0)) for width, _ in outs]
        + [pl.BlockSpec((8, 1024), lambda i: (0, 0))] * sums,
        out_shape=[jax.ShapeDtypeStruct((rows, width), kind) for width, kind in outs]
        + [jax.ShapeDtypeStruct((8, 1024), WIDE)] * sums,
        scratch_shapes=[pltpu.VMEM(shape, LOW) for shape in shapes]
        + [pltpu.SemaphoreType.DMA((32,))] * len(shapes)
        + list(scratch),
        compiler_params=pltpu.CompilerParams(vmem_limit_bytes=VMEM_LIMIT),
        cost_estimate=pl.CostEstimate(
            flops=flops, transcendentals=0,
            bytes_accessed=moved + sum(2 * a * b for a, b in shapes),
        ),
        name=name,
    )(place.table, lengths, *blocked, *full, *parts)


def project_kernel(second, real, tokens, full, weights, outs, sums):
    (x_ref,) = tokens
    scale, shift, gain, spread, collect = full
    (weight,) = weights
    h_ref, q_ref, k_ref, v_ref, rq_ref, rk_ref = outs
    unit, _ = normalize(x_ref[...].astype(WIDE))
    hidden = (unit * (1.0 + per_row(scale, second)) + per_row(shift, second)).astype(LOW)
    h_ref[...] = hidden
    width = hidden.shape[1]
    for number, (ref, root_ref) in enumerate(((q_ref, rq_ref), (k_ref, rk_ref))):
        raw = dot(hidden, weight[:, number * width : (number + 1) * width])
        root = lax.rsqrt(split_dot(raw * raw, collect[...]) + EPS)
        root_ref[...] = root
        rows = raw * split_dot(root, spread[...])
        if number == 0:
            rows = rows * gain[...]
        ref[...] = rows.astype(LOW)
    v_ref[...] = dot(hidden, weight[:, 2 * width :]).astype(LOW)


def branch_kernel(second, real, tokens, full, weights, outs, sums):
    attended_ref, x_ref = tokens
    gamma, scale, shift = full
    proj, fc1 = weights
    attn_ref, h_ref, act_ref, slope_ref = outs
    (sum_ref,) = sums
    attn = dot(attended_ref[...], proj[...]).astype(LOW)
    attn_ref[...] = attn
    branch = jnp.where(real, per_row(gamma, second) * attn.astype(WIDE), 0.0)
    add_sums(sum_ref, 0, second, branch * branch)
    unit, _ = normalize(x_ref[...].astype(WIDE) + branch)
    hidden = (unit * (1.0 + per_row(scale, second)) + per_row(shift, second)).astype(LOW)
    h_ref[...] = hidden
    width = hidden.shape[1]
    for start in range(0, fc1.shape[1], width):
        span = slice(start, start + width)
        wide = dot(hidden, fc1[:, span])
        square = wide * wide
        bend = jnp.tanh(GELU_COEF * wide * (1.0 + 0.044715 * square))
        lift = 0.5 * (1.0 + bend)
        act_ref[:, span] = (wide * lift).astype(LOW)
        slope = lift + 0.5 * wide * (1.0 - bend * bend) * (
            GELU_COEF * (1.0 + 3.0 * 0.044715 * square)
        )
        slope_ref[:, span] = slope.astype(LOW)


def stream_kernel(second, real, tokens, full, weights, outs, sums):
    act_ref, x_ref, attn_ref, cot_ref = tokens
    gamma_one, gamma_two = full
    (fc2,) = weights
    out_ref, grad_ref = outs
    (sum_ref,) = sums
    mlp = dot(act_ref[...], fc2[...])
    branch_one = jnp.where(real, per_row(gamma_one, second) * attn_ref[...].astype(WIDE), 0.0)
    gate = per_row(gamma_two, second)
    branch_two = jnp.where(real, gate * mlp, 0.0)
    stream = x_ref[...].astype(WIDE) + branch_one + branch_two
    out_ref[...] = stream.astype(LOW)
    upstream = cot_ref[...].astype(WIDE)
    grad_ref[...] = jnp.where(real, gate * upstream, 0.0).astype(LOW)
    add_sums(sum_ref, 0, second, jnp.where(real, stream * stream, 0.0))
    add_sums(sum_ref, 2, second, branch_two * branch_two)
    add_sums(sum_ref, 4, second, jnp.where(real, mlp * upstream, 0.0))


def hidden_back_kernel(second, real, tokens, full, weights, outs, sums):
    grad_ref, slope_ref = tokens
    (fc2,) = weights
    (out_ref,) = outs
    grad = grad_ref[...]
    width = grad.shape[1]
    for start in range(0, fc2.shape[0], width):
        span = slice(start, start + width)
        out_ref[:, span] = (
            dot(grad, fc2[span, :], NT) * slope_ref[:, span].astype(WIDE)
        ).astype(LOW)


def middle_back_kernel(second, real, tokens, full, weights, outs, sums):
    grad_ref, x_ref, attn_ref, cot_ref = tokens
    gamma, scale = full
    fc1, proj = weights
    middle_ref, attn_grad_ref, attended_grad_ref = outs
    (sum_ref,) = sums
    grad = dot(grad_ref[...], fc1[...], NT)
    attn = attn_ref[...].astype(WIDE)
    gate = per_row(gamma, second)
    unit, root = normalize(x_ref[...].astype(WIDE) + jnp.where(real, gate * attn, 0.0))
    add_sums(sum_ref, 0, second, grad * unit)
    add_sums(sum_ref, 2, second, grad)
    scaled = grad * (1.0 + per_row(scale, second))
    middle = cot_ref[...].astype(WIDE) + root * (
        scaled - jnp.mean(scaled, -1, keepdims=True) - unit * jnp.mean(scaled * unit, -1, keepdims=True)
    )
    middle_ref[...] = middle.astype(LOW)
    add_sums(sum_ref, 4, second, jnp.where(real, attn * middle, 0.0))
    attn_grad = jnp.where(real, gate * middle, 0.0).astype(LOW)
    attn_grad_ref[...] = attn_grad
    attended_grad_ref[...] = dot(attn_grad, proj[...], NT).astype(LOW)


def token_back_kernel(second, real, tokens, full, weights, outs, sums):
    dq_ref, dk_ref, dv_ref, x_ref, middle_ref = tokens
    (scale,) = full
    (weight,) = weights
    (out_ref,) = outs
    (sum_ref,) = sums
    width = x_ref.shape[1]
    grad = dot(dq_ref[...], weight[:, :width], NT)
    grad = grad + dot(dk_ref[...], weight[:, width : 2 * width], NT)
    grad = grad + dot(dv_ref[...], weight[:, 2 * width :], NT)
    unit, root = normalize(x_ref[...].astype(WIDE))
    add_sums(sum_ref, 0, second, grad * unit)
    add_sums(sum_ref, 2, second, grad)
    scaled = grad * (1.0 + per_row(scale, second))
    total = middle_ref[...].astype(WIDE) + root * (
        scaled - jnp.mean(scaled, -1, keepdims=True) - unit * jnp.mean(scaled * unit, -1, keepdims=True)
    )
    out_ref[...] = total.astype(LOW)


def weight_grad(place, left, rights, own_half):
    half = place.c if own_half else 1 - place.c
    parts = []
    for right in rights:
        width = right.shape[1] // 2
        piece = lax.dynamic_slice(right, (0, half * width), (right.shape[0], width))
        parts.append(dot(left, piece, TN).astype(LOW))
    return parts[0] if len(parts) == 1 else jnp.concatenate(parts, 1)


def shards(place_counts, tokens, cond, stop_scale, w_ada, w_qkv, w_proj, w_fc1, w_fc2, head_log_scale, cotangent):
    place = Place(*place_counts)
    items, width = cond.shape
    rows = tokens.shape[0]
    length = rows // items
    heads = head_log_scale.shape[0]
    ends = jnp.asarray(np.cumsum([side * side for side in PATCHES]).astype(np.int32))
    lengths = jnp.sum(jnp.where(jnp.arange(len(PATCHES))[None, :] == stop_scale[:, None], ends[None, :], 0), 1)

    cond_wide = cond.astype(WIDE)
    silu_cond = (cond_wide * jax.nn.sigmoid(cond_wide)).astype(LOW)
    ada_rows = w_ada.shape[0]
    group_cond = gather_small(place, silu_cond, False)
    ada_columns = (0, place.fsdp_index * ada_rows)
    group_slice = lax.dynamic_slice(group_cond, ada_columns, (group_cond.shape[0], ada_rows))
    modulation = scatter_small(place, dot(group_slice, w_ada))
    gamma_one, gamma_two, scale_one, scale_two, shift_one, shift_two = [
        modulation[:, n * width : (n + 1) * width] for n in range(6)
    ]

    qkv_parts, mark = gather_parts(place, w_qkv, "xy")
    proj_parts, mark = gather_parts(place, w_proj, "yx", mark)
    fc1_parts, mark = gather_parts(place, w_fc1, "xy", mark)
    fc2_parts, mark = gather_parts(place, w_fc2, "yx", mark)
    qkv_weight = (qkv_parts, (width, 3 * width))
    proj_weight = (proj_parts, (width, width))
    fc1_weight = (fc1_parts, (width, w_fc1.shape[1]))
    fc2_weight = (fc2_parts, (w_fc1.shape[1], width))

    hidden_width = w_fc1.shape[1]
    base = 2 * rows * width * width
    gain = jnp.repeat(jnp.exp(head_log_scale), width // heads)[None, :]
    head_of = np.arange(width) // (width // heads)
    spread = jnp.asarray((np.arange(heads)[:, None] == head_of[None, :]).astype(np.float32), LOW)
    collect = jnp.asarray((head_of[:, None] == np.arange(heads)[None, :]).astype(np.float32), LOW)
    normed_one, query, key, value, root_query, root_key = token_call(
        project_kernel, place, rows, length, lengths, [tokens],
        [scale_one, shift_one, gain, spread, collect], [qkv_weight],
        [(width, LOW)] * 4 + [(heads, WIDE)] * 2, 0, 3 * base, "project",
    )
    cube = (items, length, width)
    query, key, value = query.reshape(cube), key.reshape(cube), value.reshape(cube)
    query_mask, key_mask = mask_tables(length)
    attended, extra = attend(query, key, value, query_mask, key_mask)

    attn, normed_two, act, slope, sum_one = token_call(
        branch_kernel, place, rows, length, lengths,
        [attended.reshape(rows, width), tokens], [gamma_one, scale_two, shift_two],
        [proj_weight, fc1_weight],
        [(width, LOW), (width, LOW), (hidden_width, LOW), (hidden_width, LOW)], 1, 5 * base, "branch",
    )
    result, grad_mlp, sum_two = token_call(
        stream_kernel, place, rows, length, lengths,
        [act, tokens, attn, cotangent], [gamma_one, gamma_two], [fc2_weight],
        [(width, LOW), (width, LOW)], 1, 4 * base, "stream",
    )
    fc2_send = weight_grad(place, act, [grad_mlp], False)
    fc2_keep = weight_grad(place, act, [grad_mlp], True)
    grad_fc2 = reduce_rows(place, fc2_keep, fc2_send, w_fc2.shape[0], "yx")
    (grad_hidden,) = token_call(
        hidden_back_kernel, place, rows, length, lengths, [grad_mlp, slope], [], [fc2_weight],
        [(hidden_width, LOW)], 0, 4 * base, "hidden_back",
    )
    fc1_send = weight_grad(place, normed_two, [grad_hidden], False)
    fc1_keep = weight_grad(place, normed_two, [grad_hidden], True)
    grad_fc1 = reduce_rows(place, fc1_keep, fc1_send, w_fc1.shape[0], "xy")
    grad_middle, grad_attn, grad_attended, sum_three = token_call(
        middle_back_kernel, place, rows, length, lengths,
        [grad_hidden, tokens, attn, cotangent], [gamma_one, scale_two], [fc1_weight, proj_weight],
        [(width, LOW)] * 3, 1, 5 * base, "middle_back",
    )
    flat_attended = attended.reshape(rows, width)
    proj_send = weight_grad(place, flat_attended, [grad_attn], False)
    proj_keep = weight_grad(place, flat_attended, [grad_attn], True)
    grad_proj = reduce_rows(place, proj_keep, proj_send, w_proj.shape[0], "yx")

    grad_query, grad_key, grad_value, head_sums = attend_back(
        query, key, value, extra, key_mask, attended, grad_attended.reshape(cube),
        root_query.reshape(items, length, heads), root_key.reshape(items, length, heads), gain,
    )
    grad_query, grad_key, grad_value = (
        v.reshape(rows, width) for v in (grad_query, grad_key, grad_value)
    )
    joined = jnp.concatenate([grad_query, grad_key, grad_value], 1)
    qkv_send = weight_grad(place, normed_one, [joined], False)
    qkv_keep = weight_grad(place, normed_one, [joined], True)
    grad_qkv = reduce_rows(place, qkv_keep, qkv_send, w_qkv.shape[0], "xy")

    grad_tokens, sum_four = token_call(
        token_back_kernel, place, rows, length, lengths,
        [grad_query, grad_key, grad_value, tokens, grad_middle], [scale_one], [qkv_weight],
        [(width, LOW)], 1, 3 * base, "token_back",
    )

    grad_modulation = jnp.concatenate(
        [sum_three[4:6], sum_two[4:6], sum_four[0:2], sum_three[0:2], sum_four[2:4], sum_three[2:4]], 1
    ).astype(LOW)
    all_cond = gather_small(place, silu_cond, True)
    all_slice = lax.dynamic_slice(all_cond, ada_columns, (all_cond.shape[0], ada_rows))
    all_modulation = gather_small(place, grad_modulation, True)
    grad_ada = dot(all_slice, all_modulation, TN)
    group_count = group_cond.shape[0]
    group_modulation = lax.dynamic_slice(
        all_modulation, (place.dp_index * group_count, 0), (group_count, all_modulation.shape[1])
    )
    grad_columns = dot(group_modulation, w_ada, NT)
    grad_parts = gather_small(place, grad_columns[None], False)
    own_items = lax.dynamic_slice(
        grad_parts, (0, place.fsdp_index * items, 0), (grad_parts.shape[0], items, ada_rows)
    )
    grad_silu = jnp.swapaxes(own_items, 0, 1).reshape(items, width)
    gate = jax.nn.sigmoid(cond_wide)
    grad_cond = (grad_silu * gate * (1.0 + cond_wide * (1.0 - gate))).astype(LOW)

    grad_head = lax.psum(head_sums.reshape(items, heads, width // heads).sum((0, 2)), AXES)

    counted = (lengths * width).astype(WIDE)
    squares = jnp.stack(
        [sum_two[0:2].sum(1), sum_one[0:2].sum(1), sum_two[2:4].sum(1)], 1
    )
    rms_rows = jnp.sqrt(squares / counted[:, None] + EPS)
    return (
        result, grad_tokens, grad_cond, grad_ada, grad_qkv, grad_proj, grad_fc1, grad_fc2,
        grad_head, rms_rows,
    )


def solution(mesh):
    both = P(("dp", "fsdp"), None)
    rows = P("fsdp", None)
    return jax.shard_map(
        functools.partial(shards, (mesh.shape["dp"], mesh.shape["fsdp"])),
        mesh=mesh,
        in_specs=(both, both, P(("dp", "fsdp")), rows, rows, rows, rows, rows, P(), both),
        out_specs=(both, both, both, rows, rows, rows, rows, rows, P(), both),
        check_vma=False,
    )
```

```python
import functools

import jax
import jax.numpy as jnp
import numpy as np
from jax import lax
from jax.experimental import pallas as pl
from jax.experimental.pallas import tpu as pltpu
from jax.sharding import PartitionSpec as P

PATCHES = (1, 2, 3, 4, 5, 6, 8, 10, 13, 16)
EPS = 1e-06
GELU_COEF = 0.7978845608028654
AXES = ("dp", "fsdp")
LOW = jnp.bfloat16
WIDE = jnp.float32
NN = (((1,), (0,)), ((), ()))
NT = (((1,), (1,)), ((), ()))
TN = (((0,), (0,)), ((), ()))
VMEM_LIMIT = 56 << 20
BLOCKED = -30000.0
LIGHT = pl.CostEstimate(flops=1024, transcendentals=0, bytes_accessed=1024)


def dot(left, right, dims=NN):
    return lax.dot_general(left, right, dims, preferred_element_type=WIDE)


def two_parts(values):
    high = values.astype(LOW)
    return high, (values - high.astype(WIDE)).astype(LOW)


def split_dot(values, table):
    high, rest = two_parts(values)
    return dot(high, table) + dot(rest, table)


class Place:
    def __init__(self, dp_count, fsdp_count):
        self.grouped = dp_count == 4 and fsdp_count == 8
        self.dp_count = dp_count
        self.fsdp_count = fsdp_count
        dp_index = lax.axis_index("dp")
        fsdp_index = lax.axis_index("fsdp")
        self.dp_index, self.fsdp_index = dp_index, fsdp_index
        self.y, self.c = dp_index // 2, dp_index % 2
        self.z, self.x = fsdp_index // 2, fsdp_index % 2
        self.table = jnp.stack([self.y, self.c, self.z, self.x]).astype(jnp.int32)


def hop(values, dy=0, dc=0, dz=0, dx=0):
    pairs = [
        (d * 8 + f, (d ^ (2 * dy + dc)) * 8 + (f ^ (2 * dz + dx)))
        for d in range(4)
        for f in range(8)
    ]
    return lax.ppermute(values, AXES, pairs)


def tie(*values):
    return lax.optimization_barrier(values)


class Gather:
    def __init__(self, own):
        self.own = own

    def over_z(self):
        self.stack = jnp.concatenate([self.own] + [hop(self.own, dz=k) for k in (1, 2, 3)], 0)

    def over_xy(self):
        self.from_x, self.from_y = hop(self.stack, dx=1), hop(self.stack, dy=1)

    def over_both(self):
        half = self.stack.shape[0] // 2
        self.from_both = [hop(self.from_x[:half], dy=1), hop(self.from_y[half:], dx=1)]

    def over_core_first(self):
        self.first = [self.stack, self.from_x, self.from_y]
        self.first_core = [hop(piece, dc=1) for piece in self.first]

    def over_core(self):
        self.last_core = [hop(piece, dc=1) for piece in self.from_both]
        return self.first + self.from_both + self.first_core + self.last_core


def own_quarter(place, shard):
    rows, columns = shard.shape
    quarter = columns // 4
    return lax.dynamic_slice(shard, (0, (place.c * 2 + place.y) * quarter), (rows, quarter))


def weight_copies(place_ref, pieces, sources, buffer, sem):
    copies = []
    if sources is None:
        return [pltpu.make_async_copy(pieces[0], buffer, sem.at[0])]
    for column_from, quarter, rows, column_to in sources:
        for number in range(10):
            core, kind = number // 5, number % 5
            across, side = (0, 1, 0, 1, 1)[kind], (0, 0, 1, 1, 1)[kind]
            column = column_to + ((place_ref[1] ^ core) * 2 + (place_ref[0] ^ side)) * quarter
            members = range(4) if kind < 3 else range(2 * (kind - 3), 2 * (kind - 3) + 2)
            for place_in, k in enumerate(members):
                row = ((place_ref[2] ^ k) * 2 + (place_ref[3] ^ across)) * rows
                copies.append(
                    pltpu.make_async_copy(
                        pieces[number].at[pl.ds(place_in * rows, rows), pl.ds(column_from, quarter)],
                        buffer.at[
                            pl.ds(pl.multiple_of(row, 128), rows),
                            pl.ds(pl.multiple_of(column, 128), quarter),
                        ],
                        sem.at[len(copies)],
                    )
                )
    return copies


def add(left, right):
    return left.astype(WIDE) + right.astype(WIDE)


def add_blocks(place, steps, block, outs, name):
    arrays, specs, plan = [], [], []
    for _, _, terms in outs:
        entry = []
        for array, where, when in terms:
            entry.append((len(arrays), when))
            arrays.append(array)
            specs.append(pl.BlockSpec(block, functools.partial(lambda where, n, p: where(n, p), where)))
        plan.append(entry)

    def body(place_ref, *refs):
        step = pl.program_id(0)
        for entry, out_ref in zip(plan, refs[len(arrays) :]):
            total = None
            for number, when in entry:
                value = refs[number][...].astype(WIDE)
                if when is not None:
                    value = jnp.where(when(step, place_ref), value, 0.0)
                total = value if total is None else total + value
            out_ref[...] = total.astype(LOW)

    return pl.pallas_call(
        body,
        grid_spec=pltpu.PrefetchScalarGridSpec(
            num_scalar_prefetch=1,
            grid=(steps,),
            in_specs=specs,
            out_specs=[
                pl.BlockSpec(block, functools.partial(lambda where, n, p: where(n, p), where))
                for _, where, _ in outs
            ],
        ),
        out_shape=[
            jax.ShapeDtypeStruct((blocks[0] * block[0], blocks[1] * block[1]), LOW) for blocks, _, _ in outs
        ],
        compiler_params=pltpu.CompilerParams(vmem_limit_bytes=VMEM_LIMIT),
        cost_estimate=LIGHT,
        name=name,
    )(place.table, *arrays)


class RowSum:
    def __init__(self, place, keep, arrived, rows, order):
        self.place, self.base = place, [keep, arrived]
        self.block = (rows, keep.shape[1] // 2)
        self.streams = (
            [{"z": 0, "count": 2, "order": "yx"}, {"z": 2, "count": 2, "order": "xy"}]
            if order == "mixed"
            else [{"z": 0, "count": 4, "order": order}]
        )

    def first(self):
        outs, steps = [], 2 * self.streams[0]["count"]
        for stream in self.streams:
            start, count = stream["z"], stream["count"]
            if stream["order"] == "yx":
                where = lambda n, p, start=start: (2 * start + n, 1 - p[0])
                outs.append(((2 * count, 1), lambda n, p: (n, 0), [(t, where, None) for t in self.base]))
            else:
                where = lambda n, p, start=start: (2 * (start + n // 2) + 1 - p[3], n % 2)
                outs.append(((count, 2), lambda n, p: (n // 2, n % 2), [(t, where, None) for t in self.base]))
        sent = add_blocks(self.place, steps, self.block, outs, "first_sums")
        return [(v, {"d" + s["order"][0]: 1}) for v, s in zip(sent, self.streams)]

    def second(self, arrived):
        outs, steps = [], self.streams[0]["count"]
        for stream, value in zip(self.streams, arrived):
            stream["first"] = value
            start, count = stream["z"], stream["count"]
            if stream["order"] == "yx":
                where = lambda n, p, start=start: (2 * (start + n) + 1 - p[3], p[0])
                terms = [(value, lambda n, p: (2 * n + 1 - p[3], 0), None)]
            else:
                where = lambda n, p, start=start: (2 * (start + n) + p[3], 1 - p[0])
                terms = [(value, lambda n, p: (n, 1 - p[0]), None)]
            outs.append(((count, 1), lambda n, p: (n, 0), [(t, where, None) for t in self.base] + terms))
        sent = add_blocks(self.place, steps, self.block, outs, "second_sums")
        return [(v, {"d" + s["order"][1]: 1}) for v, s in zip(sent, self.streams)]

    def terms(self, flip):
        out = [(t, lambda n, p: (2 * (p[2] ^ flip) + p[3], p[0]), None) for t in self.base]
        for stream in self.streams:
            mask = stream["count"] - 1
            when = None
            if stream["count"] == 2:
                when = lambda n, p, start=stream["z"]: (p[2] ^ flip) // 2 == start // 2
            if stream["order"] == "yx":
                first = lambda n, p, mask=mask: (2 * ((p[2] ^ flip) & mask) + p[3], 0)
            else:
                first = lambda n, p, mask=mask: ((p[2] ^ flip) & mask, p[0])
            out.append((stream["first"], first, when))
            out.append((stream["second"], lambda n, p, mask=mask: ((p[2] ^ flip) & mask, 0), when))
        return out

    def third(self, arrived):
        for stream, value in zip(self.streams, arrived):
            stream["second"] = value
        outs = [((1, 1), lambda n, p: (0, 0), self.terms(k)) for k in (1, 2, 3)]
        sent = add_blocks(self.place, 1, self.block, outs, "third_sums")
        return [(v, {"dz": k}) for v, k in zip(sent, (1, 2, 3))]

    def finish(self, arrived):
        terms = self.terms(0) + [(v, lambda n, p: (0, 0), None) for v in arrived]
        return add_blocks(self.place, 1, self.block, [((1, 1), lambda n, p: (0, 0), terms)], "last_sums")[0]


def beside(kernel, operand, moves):
    out = tie(operand, *(value for value, _ in moves))
    arrived = [hop(value, **axes) for value, (_, axes) in zip(out[1:], moves)]
    results = kernel(out[0])
    results = list(results) if isinstance(results, (list, tuple)) else [results]
    out = tie(*results, *arrived)
    results, arrived = list(out[: len(results)]), list(out[len(results) :])
    return (results[0] if len(results) == 1 else results), arrived


def lay_out_kernel(layout, place_ref, *refs):
    quarters, outs = refs[:4], refs[4:]
    here = place_ref[1] * 2 + place_ref[0]
    for apart, ref in enumerate(quarters):
        index = here ^ apart
        for number, column, width, row, to, stride in layout:
            rows = ref.shape[0]
            start = pl.multiple_of(to + index * stride, 128)
            outs[number][pl.ds(row, rows), pl.ds(start, width)] = ref[:, column : column + width].astype(WIDE)


def lay_out(place, quarters, layout, shapes, name):
    vmem = pl.BlockSpec(memory_space=pltpu.VMEM)
    return pl.pallas_call(
        functools.partial(lay_out_kernel, layout),
        in_specs=[pl.BlockSpec(memory_space=pltpu.SMEM)] + [vmem] * 4,
        out_specs=[vmem] * len(shapes),
        out_shape=[jax.ShapeDtypeStruct(shape, WIDE) for shape in shapes],
        compiler_params=pltpu.CompilerParams(vmem_limit_bytes=VMEM_LIMIT),
        cost_estimate=LIGHT,
        name=name,
    )(place.table, *quarters)


def spread(own):
    return [own, hop(own, dy=1), hop(own, dc=1), hop(own, dy=1, dc=1)]


def reorder(stack, count, flip):
    return jnp.concatenate(
        [lax.dynamic_slice_in_dim(stack, i ^ flip, 1, axis=0) for i in range(count)], 0
    )


def small_over_z(values):
    return jnp.stack([values] + [hop(values, dz=k) for k in (1, 2, 3)])


def small_over_x(place, stack):
    count, tail = stack.shape[1], stack.shape[2:]
    stack = jnp.stack([stack, hop(stack, dx=1)], 1).reshape((8, count) + tail)
    return reorder(stack, 8, place.fsdp_index).reshape((8 * count,) + tail)


def gather_small(place, values, whole):
    if not place.grouped:
        return lax.all_gather(values, AXES if whole else "fsdp", axis=0, tiled=True)
    ordered = small_over_x(place, small_over_z(values))
    return over_dp(place, ordered) if whole else ordered


def over_dp(place, values):
    if not place.grouped:
        return lax.all_gather(values, "dp", axis=0, tiled=True)
    stack = jnp.stack([values, hop(values, dc=1), hop(values, dy=1), hop(values, dy=1, dc=1)])
    return reorder(stack, 4, place.dp_index).reshape((4 * values.shape[0],) + values.shape[1:])


def scatter_over_x(place, values):
    values = values.reshape((4, 2, values.shape[0] // 8) + values.shape[1:])
    mine = lax.dynamic_index_in_dim(values, place.x, 1, keepdims=False)
    other = lax.dynamic_index_in_dim(values, 1 - place.x, 1, keepdims=False)
    return mine + hop(other, dx=1)


def scatter_over_z(place, values):
    total = lax.dynamic_index_in_dim(values, place.z, 0, keepdims=False)
    for k in (1, 2, 3):
        total = total + hop(
            lax.dynamic_index_in_dim(values, place.z ^ k, 0, keepdims=False), dz=k
        )
    return total


def mask_tables(length):
    scale_ids = np.concatenate([np.full(side * side, i) for i, side in enumerate(PATCHES)])
    spare = np.arange(128) & 63
    slot = spare[None, :] - 2
    scale_column = scale_ids[:, None]
    later = (slot >= 0) & (slot < len(PATCHES)) & (slot > scale_column)
    query_side = np.where(later, BLOCKED, 0.0)
    key_side = np.where(slot == scale_column, 1.0, 0.0) + np.where(spare[None, :] < 2, 1.0, 0.0)
    return jnp.asarray(query_side, LOW), jnp.asarray(key_side, LOW)


FORWARD_BLOCKS = ((0, 240, 256), (240, 416, 512), (416, 680, 680))
BACKWARD_BLOCKS = ((424, 680, 680), (240, 424, 432), (0, 240, 256))


def attend_kernel(qkv_ref, qm_ref, km_ref, out_ref, extra_ref):
    query, key, value = (qkv_ref[0, :, 128 * n : 128 * n + 128] for n in range(3))
    query_mask, key_mask = qm_ref[...], km_ref[...]
    lane = lax.broadcasted_iota(jnp.int32, query.shape, 1)
    even = lane < 64
    ones = jnp.ones_like(value)
    heads = (
        (jnp.where(even, query, query_mask), jnp.where(even, key, key_mask), jnp.where(even, value, ones)),
        (jnp.where(even, query_mask, query), jnp.where(even, key_mask, key), jnp.where(even, ones, value)),
    )
    for start, stop, keys in FORWARD_BLOCKS:
        sums = []
        for query_head, key_head, value_head in heads:
            scores = dot(query_head[start:stop], key_head[:keys], NT)
            sums.append(dot(jnp.exp(scores).astype(LOW), value_head[:keys]))
        side = even[start:stop]
        chosen = jnp.where(side, sums[0], sums[1])
        totals = jnp.where(side, sums[1], sums[0])
        out_ref[0, start:stop, :] = (chosen / pltpu.roll(totals, 64, 1)).astype(LOW)
        high, rest = two_parts(-jnp.log(totals))
        spare = lane[start:stop] & 63
        extra_ref[0, start:stop, :] = jnp.where(
            spare == 0, high, jnp.where(spare == 1, rest, query_mask[start:stop])
        )


def attend(qkv, query_mask, key_mask):
    items, length, triple = qkv.shape
    pairs = triple // 384
    block = pl.BlockSpec((1, length, 128), lambda i, p: (i, 0, p))
    table = pl.BlockSpec((length, 128), lambda i, p: (0, 0))
    return pl.pallas_call(
        attend_kernel,
        grid=(items, pairs),
        in_specs=[pl.BlockSpec((1, length, 384), lambda i, p: (i, 0, p)), table, table],
        out_specs=[block, block],
        out_shape=[jax.ShapeDtypeStruct((items, length, 128 * pairs), LOW)] * 2,
        compiler_params=pltpu.CompilerParams(vmem_limit_bytes=VMEM_LIMIT),
        cost_estimate=LIGHT,
        name="attend",
    )(qkv, query_mask, key_mask)


def side_table(cross, size=128):
    first = lax.broadcasted_iota(jnp.int32, (size, size), 0) // 64
    second = lax.broadcasted_iota(jnp.int32, (size, size), 1) // 64
    return jnp.where((first != second) if cross else (first == second), 1.0, 0.0).astype(LOW)


def attend_back_kernel(
    qkv_ref, extra_ref, km_ref, out_ref, grad_ref, root_ref, gain_ref,
    grad_qkv_ref, head_ref, value_sum, key_sum, query_sum,
):
    query, key, value = (qkv_ref[0, :, 128 * n : 128 * n + 128] for n in range(3))
    key_mask, grad, extra = km_ref[...], grad_ref[0], extra_ref[0]
    lane = lax.broadcasted_iota(jnp.int32, query.shape, 1)
    even = lane < 64
    spare = lane & 63
    centre = split_dot(grad.astype(WIDE) * out_ref[0].astype(WIDE), side_table(True))
    high, rest = two_parts(-centre)
    grad_extra = jnp.where(spare == 0, high, jnp.where(spare == 1, rest, jnp.zeros_like(high)))
    ones = jnp.ones_like(value)
    key_rows = key.astype(WIDE).T.astype(LOW)
    heads = (
        (jnp.where(even, query, extra), jnp.where(even, key, key_mask),
         jnp.where(even, value, ones), jnp.where(even, grad, grad_extra)),
        (jnp.where(even, extra, query), jnp.where(even, key_mask, key),
         jnp.where(even, ones, value), jnp.where(even, grad_extra, grad)),
    )
    for head, (query_head, key_head, value_head, grad_head) in enumerate(heads):
        head_rows = key_rows[64 * head : 64 * head + 64]
        for number, (start, stop, keys) in enumerate(BACKWARD_BLOCKS):
            probs = jnp.exp(dot(key_head[:keys], query_head[start:stop], NT))
            grad_probs = dot(value_head[:keys], grad_head[start:stop], NT)
            grad_scores = (probs * grad_probs).astype(LOW)
            value_part = dot(probs.astype(LOW), grad[start:stop])
            key_part = dot(grad_scores, query[start:stop])
            if number == 0:
                value_sum[head] = value_part
                key_sum[head] = key_part
            else:
                value_sum[head, :keys] += value_part
                key_sum[head, :keys] += key_part
            query_sum[start:stop, 64 * head : 64 * head + 64] = dot(head_rows[:, :keys], grad_scores).T
    row = lax.broadcasted_iota(jnp.int32, (128, 128), 0)
    wanted = jnp.where(lax.broadcasted_iota(jnp.int32, (128, 128), 1) >= 64, 64, 0)
    roots = root_ref[0]
    root_query = dot(roots, jnp.where(row == wanted, 1.0, 0.0).astype(LOW))
    root_key = dot(roots, jnp.where(row == wanted + 32, 1.0, 0.0).astype(LOW))
    same = side_table(False)
    gain = gain_ref[...]
    grad_query = query_sum[...] * gain
    unit_query = query.astype(WIDE) / gain
    product = unit_query * grad_query
    head_ref[0] = jnp.sum(product, 0, keepdims=True)
    grad_qkv_ref[0, :, :128] = (
        root_query * (grad_query - unit_query * split_dot(product, same))
    ).astype(LOW)
    grad_key = jnp.where(even, key_sum[0], key_sum[1])
    unit_key = key.astype(WIDE)
    grad_qkv_ref[0, :, 128:256] = (
        root_key * (grad_key - unit_key * split_dot(unit_key * grad_key, same))
    ).astype(LOW)
    grad_qkv_ref[0, :, 256:] = jnp.where(even, value_sum[0], value_sum[1]).astype(LOW)


def attend_back(qkv, extra, key_mask, out, grad, roots, gain, first, pairs):
    items, length, _ = qkv.shape
    block = pl.BlockSpec((1, length, 128), lambda i, p: (i, 0, p + first))
    table = pl.BlockSpec((length, 128), lambda i, p: (0, 0))
    return pl.pallas_call(
        attend_back_kernel,
        grid=(items, pairs),
        in_specs=[pl.BlockSpec((1, length, 384), lambda i, p: (i, 0, p + first))]
        + [block, table, block, block, block, pl.BlockSpec((1, 128), lambda i, p: (0, p + first))],
        out_specs=[
            pl.BlockSpec((1, length, 384), lambda i, p: (i, 0, p)),
            pl.BlockSpec((1, 1, 128), lambda i, p: (i, 0, p)),
        ],
        out_shape=[
            jax.ShapeDtypeStruct((items, length, 384 * pairs), LOW),
            jax.ShapeDtypeStruct((items, 1, 128 * pairs), WIDE),
        ],
        scratch_shapes=[
            pltpu.VMEM((2, length, 128), WIDE),
            pltpu.VMEM((2, length, 128), WIDE),
            pltpu.VMEM((length, 128), WIDE),
        ],
        compiler_params=pltpu.CompilerParams(vmem_limit_bytes=VMEM_LIMIT),
        cost_estimate=LIGHT,
        name="attend_back",
    )(qkv, extra, key_mask, out, grad, roots, gain)


def row_facts(lengths_ref, block_rows, length):
    row = pl.program_id(0) * block_rows + lax.broadcasted_iota(jnp.int32, (block_rows, 1), 0)
    second = row >= length
    end = jnp.where(second, length + lengths_ref[1], lengths_ref[0])
    return second, row < end


def per_row(ref, second):
    return jnp.where(second, ref[1:2, :], ref[0:1, :])


def add_sums(ref, start, second, values):
    ref[start : start + 1, :] += jnp.sum(jnp.where(second, 0.0, values), 0, keepdims=True)
    ref[start + 1 : start + 2, :] += jnp.sum(jnp.where(second, values, 0.0), 0, keepdims=True)


def normalize(values):
    centred = values - jnp.mean(values, -1, keepdims=True)
    scale = lax.rsqrt(jnp.mean(centred * centred, -1, keepdims=True) + EPS)
    return centred * scale, scale


def token_call(kernel, place, rows, length, lengths, blocked, full, weights, outs, sums, name):
    block_rows = 2 * length // 5
    grid = rows // block_rows
    parts, where = [], []
    for pieces, sources, _ in weights:
        start = len(parts)
        parts.extend(pieces)
        where.append((start, len(pieces), sources))
    shapes = [weight[2] for weight in weights]
    counts = [1 if sources is None else 32 * len(sources) for _, _, sources in where]
    blocked_count, full_count, out_count, weight_count = len(blocked), len(full), len(outs), len(weights)

    def body(place_ref, lengths_ref, *refs):
        cursor = 0

        def take(count):
            nonlocal cursor
            cursor += count
            return refs[cursor - count : cursor]

        token_refs, full_refs, part_refs = take(blocked_count), take(full_count), take(len(parts))
        out_refs, sum_refs = take(out_count), take(sums)
        buffers, sems = take(weight_count), take(weight_count)
        first = pl.program_id(0) == 0

        def copies(number):
            start, count, sources = where[number]
            return weight_copies(
                place_ref, part_refs[start : start + count], sources, buffers[number], sems[number]
            )

        @pl.when(first)
        def _():
            for number in range(weight_count):
                for copy in copies(number):
                    copy.start()
            for ref in sum_refs:
                ref[...] = jnp.zeros_like(ref)

        def ready(number):
            @pl.when(first)
            def _():
                for copy in copies(number):
                    copy.wait()

            return buffers[number]

        second, real = row_facts(lengths_ref, block_rows, length)
        kernel(second, real, token_refs, full_refs, ready, out_refs, sum_refs)

    any_space = pl.BlockSpec(memory_space=pl.ANY)
    smem = pl.BlockSpec(memory_space=pltpu.SMEM)
    return pl.pallas_call(
        body,
        grid=(grid,),
        in_specs=[smem, smem]
        + [pl.BlockSpec((block_rows, v.shape[1]), lambda i: (i, 0)) for v in blocked]
        + [pl.BlockSpec(v.shape, lambda i: (0, 0)) for v in full]
        + [any_space] * len(parts),
        out_specs=[pl.BlockSpec((block_rows, width), lambda i: (i, 0)) for width, _ in outs]
        + [pl.BlockSpec((8, 1024), lambda i: (0, 0))] * sums,
        out_shape=[jax.ShapeDtypeStruct((rows, width), kind) for width, kind in outs]
        + [jax.ShapeDtypeStruct((8, 1024), WIDE)] * sums,
        scratch_shapes=[pltpu.VMEM(shape, LOW) for shape in shapes]
        + [pltpu.SemaphoreType.DMA((count,)) for count in counts],
        compiler_params=pltpu.CompilerParams(vmem_limit_bytes=VMEM_LIMIT),
        cost_estimate=LIGHT,
        name=name,
    )(place.table, lengths, *blocked, *full, *parts)


def project_kernel(second, real, tokens, full, ready, outs, sums):
    (x_ref,) = tokens
    scale, shift, gain = full
    h_ref, qkv_ref, root_ref = outs
    unit, _ = normalize(x_ref[...].astype(WIDE))
    hidden = (unit * (1.0 + per_row(scale, second)) + per_row(shift, second)).astype(LOW)
    h_ref[...] = hidden
    same = side_table(False, 256)
    first_half = (lax.broadcasted_iota(jnp.int32, (hidden.shape[0], 128), 1) & 32) == 0
    weight = ready(0)
    for pair in range(weight.shape[1] // 384):
        start = 384 * pair
        raw = dot(hidden, weight[:, start : start + 384])
        both = raw[:, :256]
        root = lax.rsqrt(dot((both * both).astype(LOW), same) + EPS)
        root_ref[:, 128 * pair : 128 * pair + 128] = jnp.where(
            first_half, root[:, :128], root[:, 128:]
        ).astype(LOW)
        query = raw[:, :128] * (root[:, :128] * gain[:, 128 * pair : 128 * pair + 128])
        qkv_ref[:, start : start + 128] = query.astype(LOW)
        qkv_ref[:, start + 128 : start + 256] = (raw[:, 128:256] * root[:, 128:]).astype(LOW)
        qkv_ref[:, start + 256 : start + 384] = raw[:, 256:].astype(LOW)


def branch_kernel(second, real, tokens, full, ready, outs, sums):
    attended_ref, x_ref = tokens
    gamma, scale, shift = full
    attn_ref, h_ref, act_ref, slope_ref = outs
    (sum_ref,) = sums
    attn = dot(attended_ref[...], ready(0)[...]).astype(LOW)
    attn_ref[...] = attn
    branch = jnp.where(real, per_row(gamma, second) * attn.astype(WIDE), 0.0)
    add_sums(sum_ref, 0, second, branch * branch)
    unit, _ = normalize(x_ref[...].astype(WIDE) + branch)
    hidden = (unit * (1.0 + per_row(scale, second)) + per_row(shift, second)).astype(LOW)
    h_ref[...] = hidden
    width = 512
    fc1 = ready(1)
    for start in range(0, fc1.shape[1], width):
        span = slice(start, start + width)
        wide = dot(hidden, fc1[:, span])
        square = wide * wide
        lift = 0.5 + 0.5 * jnp.tanh(wide * (GELU_COEF + (GELU_COEF * 0.044715) * square))
        act_ref[:, span] = (wide * lift).astype(LOW)
        bend = wide * (2.0 * GELU_COEF + (6.0 * 0.044715 * GELU_COEF) * square)
        slope_ref[:, span] = (lift * (1.0 + bend * (1.0 - lift))).astype(LOW)


def stream_kernel(second, real, tokens, full, ready, outs, sums):
    act_ref, x_ref, attn_ref, cot_ref = tokens
    gamma_one, gamma_two = full
    out_ref, grad_ref = outs
    (sum_ref,) = sums
    mlp = dot(act_ref[...], ready(0)[...])
    branch_one = jnp.where(real, per_row(gamma_one, second) * attn_ref[...].astype(WIDE), 0.0)
    gate = per_row(gamma_two, second)
    branch_two = jnp.where(real, gate * mlp, 0.0)
    stream = x_ref[...].astype(WIDE) + branch_one + branch_two
    out_ref[...] = stream.astype(LOW)
    upstream = cot_ref[...].astype(WIDE)
    grad_ref[...] = jnp.where(real, gate * upstream, 0.0).astype(LOW)
    add_sums(sum_ref, 0, second, jnp.where(real, stream * stream, 0.0))
    add_sums(sum_ref, 2, second, branch_two * branch_two)
    add_sums(sum_ref, 4, second, jnp.where(real, mlp * upstream, 0.0))


def hidden_back_kernel(second, real, tokens, full, ready, outs, sums):
    grad_ref, slope_ref = tokens
    (out_ref,) = outs
    grad = grad_ref[...]
    width = 512
    fc2 = ready(0)
    for start in range(0, fc2.shape[0], width):
        span = slice(start, start + width)
        out_ref[:, span] = (
            dot(grad, fc2[span, :], NT) * slope_ref[:, span].astype(WIDE)
        ).astype(LOW)


def middle_back_kernel(second, real, tokens, full, ready, outs, sums):
    grad_ref, x_ref, attn_ref, cot_ref = tokens
    gamma, scale = full
    middle_ref, attn_grad_ref, attended_grad_ref = outs
    (sum_ref,) = sums
    grad = dot(grad_ref[...], ready(0)[...], NT)
    attn = attn_ref[...].astype(WIDE)
    gate = per_row(gamma, second)
    unit, root = normalize(x_ref[...].astype(WIDE) + jnp.where(real, gate * attn, 0.0))
    add_sums(sum_ref, 0, second, grad * unit)
    add_sums(sum_ref, 2, second, grad)
    scaled = grad * (1.0 + per_row(scale, second))
    middle = cot_ref[...].astype(WIDE) + root * (
        scaled - jnp.mean(scaled, -1, keepdims=True) - unit * jnp.mean(scaled * unit, -1, keepdims=True)
    )
    middle_ref[...] = middle.astype(LOW)
    add_sums(sum_ref, 4, second, jnp.where(real, attn * middle, 0.0))
    attn_grad = jnp.where(real, gate * middle, 0.0).astype(LOW)
    attn_grad_ref[...] = attn_grad
    attended_grad_ref[...] = dot(attn_grad, ready(1)[...], NT).astype(LOW)


def token_back_kernel(second, real, tokens, full, ready, outs, sums):
    *grad_refs, x_ref, middle_ref = tokens
    (scale,) = full
    (out_ref,) = outs
    (sum_ref,) = sums
    weight = ready(0)
    grad, column = 0.0, 0
    for ref in grad_refs:
        grad = grad + dot(ref[...], weight[:, column : column + ref.shape[1]], NT)
        column += ref.shape[1]
    unit, root = normalize(x_ref[...].astype(WIDE))
    add_sums(sum_ref, 0, second, grad * unit)
    add_sums(sum_ref, 2, second, grad)
    scaled = grad * (1.0 + per_row(scale, second))
    total = middle_ref[...].astype(WIDE) + root * (
        scaled - jnp.mean(scaled, -1, keepdims=True) - unit * jnp.mean(scaled * unit, -1, keepdims=True)
    )
    out_ref[...] = total.astype(LOW)


def outer_kernel(half_ref, left_ref, right_ref, out_ref):
    out_ref[...] = dot(left_ref[...], right_ref[...], TN).astype(LOW)


def outer(left, right, half=None):
    count, height = left.shape
    width = right.shape[1] if half is None else right.shape[1] // 2
    half = jnp.zeros((1,), jnp.int32) if half is None else half.reshape(1).astype(jnp.int32)
    tall = min(height, 1024)
    wide = min(width, 1024 if width % 1024 == 0 else 768 if width % 768 == 0 else 512)
    steps = width // wide
    return pl.pallas_call(
        outer_kernel,
        grid_spec=pltpu.PrefetchScalarGridSpec(
            num_scalar_prefetch=1,
            grid=(height // tall, steps),
            in_specs=[
                pl.BlockSpec((count, tall), lambda i, j, h: (0, i)),
                pl.BlockSpec((count, wide), lambda i, j, h: (0, h[0] * steps + j)),
            ],
            out_specs=pl.BlockSpec((tall, wide), lambda i, j, h: (i, j)),
        ),
        out_shape=jax.ShapeDtypeStruct((height, width), LOW),
        compiler_params=pltpu.CompilerParams(vmem_limit_bytes=VMEM_LIMIT),
        cost_estimate=LIGHT,
        name="outer",
    )(half, left, right)


def plain_sum(place, keep, send):
    flip = place.c == 1
    full = jnp.concatenate([jnp.where(flip, send, keep), jnp.where(flip, keep, send)], 1)
    part = lax.psum_scatter(full, "fsdp", scatter_dimension=0, tiled=True)
    return lax.psum(part, "dp").astype(WIDE)


def shards(place_counts, tokens, cond, stop_scale, w_ada, w_qkv, w_proj, w_fc1, w_fc2, head_log_scale, cotangent):
    place = Place(*place_counts)
    items, width = cond.shape
    rows = tokens.shape[0]
    length = rows // items
    heads = head_log_scale.shape[0]
    pairs = heads // 2
    hidden_width = w_fc1.shape[1]
    ends = jnp.asarray(np.cumsum([side * side for side in PATCHES]).astype(np.int32))
    lengths = jnp.sum(jnp.where(jnp.arange(len(PATCHES))[None, :] == stop_scale[:, None], ends[None, :], 0), 1)

    def by_pair(matrix):
        return jnp.swapaxes(matrix.reshape(matrix.shape[0], 3, pairs, 128), 1, 2).reshape(matrix.shape)

    def from_pair(matrix):
        return jnp.swapaxes(matrix.reshape(matrix.shape[0], pairs, 3, 128), 1, 2).reshape(matrix.shape)

    paired = by_pair(w_qkv)
    half = paired.shape[1] // 2
    cond_wide = cond.astype(WIDE)
    silu_cond = (cond_wide * jax.nn.sigmoid(cond_wide)).astype(LOW)
    ada_rows = w_ada.shape[0]
    group_count = items * place.fsdp_count
    ada_columns = (0, place.fsdp_index * ada_rows)

    def part_modulation(group_cond):
        return dot(lax.dynamic_slice(group_cond, ada_columns, (group_count, ada_rows)), w_ada)

    if place.grouped:
        unit_rows = w_qkv.shape[0]
        cond_stack = small_over_z(silu_cond)
        own_qkv, cond_stack = tie(own_quarter(place, paired), cond_stack)
        qkv = Gather(own_qkv)
        qkv.over_z()
        mixed = scatter_over_x(place, part_modulation(small_over_x(place, cond_stack)))
        qkv.stack, mixed = tie(qkv.stack, mixed)
        qkv.over_xy()
        modulation = scatter_over_z(place, mixed)
        own_rest = jnp.concatenate([own_quarter(place, w_proj), own_quarter(place, w_fc1)], 1)
        own_rest, modulation = tie(own_rest, modulation)
        rest = Gather(own_rest)
        rest.over_z()
        qkv.over_both()
        qkv.over_core_first()
        out = tie(rest.stack, *qkv.from_both)
        rest.stack, qkv.from_both = out[0], list(out[1:])
        rest.over_xy()
        qkv_parts = qkv.over_core()
        piece = w_fc2.shape[0] // place.dp_count
        fc2_piece = lax.dynamic_slice(w_fc2, (place.dp_index * piece, 0), (piece, width))
        fc2_piece, qkv_parts[-1] = tie(fc2_piece, qkv_parts[-1])
        fc2_full = lax.all_gather(fc2_piece, ("fsdp", "dp"), axis=0, tiled=True)
        quarter = half // 2
        qkv_weight = (qkv_parts, [(0, quarter, unit_rows, 0)], (width, 2 * half))
        fc2_weight = ([fc2_full], None, (hidden_width, width))
    else:
        qkv_weight, proj_weight, fc1_weight, fc2_weight = (
            ([lax.all_gather(w, "fsdp", axis=0, tiled=True)], None, (w.shape[0] * place.fsdp_count, w.shape[1]))
            for w in (paired, w_proj, w_fc1, w_fc2)
        )
        modulation = lax.psum_scatter(
            part_modulation(gather_small(place, silu_cond, False)), "fsdp", scatter_dimension=0, tiled=True
        )
    gamma_one, gamma_two, scale_one, scale_two, shift_one, shift_two = [
        modulation[:, n * width : (n + 1) * width] for n in range(6)
    ]

    gain = jnp.repeat(jnp.exp(head_log_scale), width // heads)[None, :]
    normed_one, projected, roots = token_call(
        project_kernel, place, rows, length, lengths, [tokens], [scale_one, shift_one, gain],
        [qkv_weight], [(width, LOW), (3 * width, LOW), (width, LOW)], 0, "project",
    )
    if place.grouped:
        rest.from_x, rest.from_y, projected = tie(rest.from_x, rest.from_y, projected)
        rest.over_both()
        rest.over_core_first()
    cube = (items, length, width)
    projected, roots = projected.reshape(items, length, 3 * width), roots.reshape(cube)
    query_mask, key_mask = mask_tables(length)
    attended, extra = attend(projected, query_mask, key_mask)
    if place.grouped:
        out = tie(attended, *rest.from_both)
        attended, rest.from_both = out[0], list(out[1:])
        rest_parts = rest.over_core()
        proj_weight = (rest_parts, [(0, width // 4, unit_rows, 0)], (width, width))
        fc1_weight = (
            rest_parts, [(width // 4, hidden_width // 4, unit_rows, 0)], (width, hidden_width)
        )
    flat_attended = attended.reshape(rows, width)
    attn, normed_two, act, slope, sum_one = token_call(
        branch_kernel, place, rows, length, lengths, [flat_attended, tokens],
        [gamma_one, scale_two, shift_two], [proj_weight, fc1_weight],
        [(width, LOW), (width, LOW), (hidden_width, LOW), (hidden_width, LOW)], 1, "branch",
    )
    result, grad_mlp, sum_two = token_call(
        stream_kernel, place, rows, length, lengths, [act, tokens, attn, cotangent],
        [gamma_one, gamma_two], [fc2_weight], [(width, LOW), (width, LOW)], 1, "stream",
    )

    def send_part(left, right):
        return outer(left, right, 1 - place.c)

    def keep_part(left, right):
        return outer(left, right, place.c)

    def hidden_back(grad):
        return token_call(
            hidden_back_kernel, place, rows, length, lengths, [grad, slope], [], [fc2_weight],
            [(hidden_width, LOW)], 0, "hidden_back",
        )[0]

    def middle_back(grad):
        return token_call(
            middle_back_kernel, place, rows, length, lengths, [grad, tokens, attn, cotangent],
            [gamma_one, scale_two], [fc1_weight, proj_weight], [(width, LOW)] * 3, 1, "middle_back",
        )

    def heads_back(grad, first):
        out, sums = attend_back(
            projected, extra, key_mask, attended, grad.reshape(cube), roots, gain, first, pairs // 2
        )
        return out.reshape(rows, half), sums

    def token_back(first, second):
        return token_call(
            token_back_kernel, place, rows, length, lengths, [first, second, tokens, grad_middle],
            [scale_one], [qkv_weight], [(width, LOW)], 1, "token_back",
        )

    if place.grouped:
        fc2_rows = w_fc2.shape[0]
        fc2_send = send_part(act, grad_mlp)
        fc2_keep, arrived = beside(lambda g: keep_part(act, g), grad_mlp, [(fc2_send, {"dc": 1})])
        fc2_sum = RowSum(place, fc2_keep, arrived[0], fc2_rows, "mixed")
        grad_hidden, arrived = beside(hidden_back, grad_mlp, fc2_sum.first())
        fc1_send, arrived = beside(lambda g: send_part(normed_two, g), grad_hidden, fc2_sum.second(arrived))
        fc2_moves = fc2_sum.third(arrived)
        fc1_keep, arrived = beside(lambda g: keep_part(normed_two, g), grad_hidden, [(fc1_send, {"dc": 1})])
        fc1_sum = RowSum(place, fc1_keep, arrived[0], unit_rows, "mixed")
        out, arrived = beside(middle_back, grad_hidden, fc1_sum.first() + fc2_moves)
        grad_middle, grad_attn, grad_attended, sum_three = out
        fc2_own = fc2_sum.finish(arrived[2:])
        fc1_moves = fc1_sum.second(arrived[:2])
        grad_attn, *tied = tie(grad_attn, fc2_own, *(v for v, _ in fc1_moves))
        fc2_own, fc1_moves = tied[0], [(v, axes) for v, (_, axes) in zip(tied[1:], fc1_moves)]
        proj_send = send_part(flat_attended, grad_attn)
        proj_keep, arrived = beside(lambda g: keep_part(flat_attended, g), grad_attn, [(proj_send, {"dc": 1})])
        proj_sum = RowSum(place, proj_keep, arrived[0], unit_rows, "yx")
        out, arrived = beside(
            lambda g: heads_back(g, 0), grad_attended, fc1_moves + proj_sum.first() + [(fc2_own, {"dy": 1})]
        )
        grad_first, heads_first = out
        fc1_moves = fc1_sum.third(arrived[:2])
        proj_moves = proj_sum.second(arrived[2:3])
        fc2_y = arrived[3]
        first_send, fc2_core = beside(
            lambda g: send_part(normed_one, g), grad_first, [(fc2_own, {"dc": 1}), (fc2_y, {"dc": 1})]
        )
        first_keep, arrived = beside(lambda g: keep_part(normed_one, g), grad_first, [(first_send, {"dc": 1})])
        first_sum = RowSum(place, first_keep, arrived[0], unit_rows, "yx")
        out, arrived = beside(
            lambda g: heads_back(g, pairs // 2), grad_attended, fc1_moves + first_sum.first() + proj_moves
        )
        grad_second, heads_second = out
        fc1_own = fc1_sum.finish(arrived[:3])
        first_moves = first_sum.second(arrived[3:4])
        proj_moves = proj_sum.third(arrived[4:])
        second_send, arrived = beside(
            lambda g: send_part(normed_one, g), grad_second, proj_moves + first_moves
        )
        proj_own = proj_sum.finish(arrived[:3])
        first_moves = first_sum.third(arrived[3:])
        second_keep, arrived = beside(
            lambda g: keep_part(normed_one, g), grad_second, [(second_send, {"dc": 1}), (fc1_own, {"dy": 1})]
        )
        fc1_y = arrived[1]
        second_sum = RowSum(place, second_keep, arrived[0], unit_rows, "xy")
        out, arrived = beside(
            lambda g: token_back(grad_first, g), grad_second, second_sum.first() + first_moves
        )
        grad_tokens, sum_four = out
        second_moves = second_sum.second(arrived[:1])
        first_own = first_sum.finish(arrived[1:])
        second_moves = second_sum.third([hop(v, **axes) for v, axes in second_moves])
        second_own = second_sum.finish([hop(v, **axes) for v, axes in second_moves])
        quarter = width // 4
        (grad_fc2,) = lay_out(
            place, [fc2_own, fc2_y] + fc2_core, [(0, 0, quarter, 0, 0, quarter)], [w_fc2.shape], "lay_out_fc2"
        )
        (grad_fc1,) = lay_out(
            place, [fc1_own, fc1_y, hop(fc1_own, dc=1), hop(fc1_y, dc=1)],
            [(0, 0, hidden_width // 4, 0, 0, hidden_width // 4)], [w_fc1.shape], "lay_out_fc1",
        )
        late = spread(jnp.concatenate([first_own, second_own, proj_own], 1))
        layout = [
            (0, 384 * side + 128 * n, 128, 0, n * width + 512 * side, 128) for side in range(2) for n in range(3)
        ]
        layout.append((1, 768, quarter, 0, 0, quarter))
        grad_qkv, grad_proj = lay_out(place, late, layout, [w_qkv.shape, w_proj.shape], "lay_out_late")
    else:
        def whole_sum(left, right):
            return plain_sum(place, keep_part(left, right), send_part(left, right))

        grad_fc2 = whole_sum(act, grad_mlp)
        grad_hidden = hidden_back(grad_mlp)
        grad_fc1 = whole_sum(normed_two, grad_hidden)
        grad_middle, grad_attn, grad_attended, sum_three = middle_back(grad_hidden)
        grad_proj = whole_sum(flat_attended, grad_attn)
        grad_first, heads_first = heads_back(grad_attended, 0)
        grad_second, heads_second = heads_back(grad_attended, pairs // 2)
        grad_qkv = from_pair(
            jnp.concatenate([whole_sum(normed_one, grad_first), whole_sum(normed_one, grad_second)], 1)
        )
        grad_tokens, sum_four = token_back(grad_first, grad_second)

    head_terms = jnp.concatenate([heads_first, heads_second], 2).reshape(items, heads, width // heads).sum(2)
    head_parts = jnp.concatenate([*two_parts(head_terms), jnp.zeros((items, 128 - 2 * heads), LOW)], 1)
    grad_modulation = jnp.concatenate(
        [sum_three[4:6], sum_two[4:6], sum_four[0:2], sum_three[0:2], sum_four[2:4], sum_three[2:4]], 1
    ).astype(LOW)
    group = gather_small(place, jnp.concatenate([grad_modulation, head_parts, silu_cond], 1), False)
    grad_columns = dot(group[:, : 6 * width], w_ada, NT)
    everything = over_dp(place, group)
    all_heads = everything[:, 6 * width : 6 * width + 2 * heads].astype(WIDE)
    grad_head = jnp.sum(all_heads[:, :heads] + all_heads[:, heads:], 0)
    all_slice = lax.dynamic_slice(
        everything, (0, 6 * width + 128 + place.fsdp_index * ada_rows), (everything.shape[0], ada_rows)
    )
    grad_ada = dot(all_slice, everything[:, : 6 * width], TN)
    grad_parts = gather_small(place, grad_columns[None], False)
    own_items = lax.dynamic_slice(
        grad_parts, (0, place.fsdp_index * items, 0), (grad_parts.shape[0], items, ada_rows)
    )
    grad_silu = jnp.swapaxes(own_items, 0, 1).reshape(items, width)
    gate = jax.nn.sigmoid(cond_wide)
    grad_cond = (grad_silu * gate * (1.0 + cond_wide * (1.0 - gate))).astype(LOW)

    counted = (lengths * width).astype(WIDE)
    squares = jnp.stack(
        [sum_two[0:2].sum(1), sum_one[0:2].sum(1), sum_two[2:4].sum(1)], 1
    )
    rms_rows = jnp.sqrt(squares / counted[:, None] + EPS)
    return (
        result, grad_tokens, grad_cond, grad_ada, grad_qkv, grad_proj, grad_fc1, grad_fc2,
        grad_head, rms_rows,
    )


def solution(mesh):
    both = P(("dp", "fsdp"), None)
    rows = P("fsdp", None)
    return jax.shard_map(
        functools.partial(shards, (mesh.shape["dp"], mesh.shape["fsdp"])),
        mesh=mesh,
        in_specs=(both, both, P(("dp", "fsdp")), rows, rows, rows, rows, rows, P(), both),
        out_specs=(both, both, both, rows, rows, rows, rows, rows, P(), both),
        check_vma=False,
    )
```

```python
import functools

import jax
import jax.numpy as jnp
import numpy as np
from jax import lax
from jax.experimental import pallas as pl
from jax.experimental.pallas import tpu as pltpu
from jax.sharding import PartitionSpec as P

PATCHES = (1, 2, 3, 4, 5, 6, 8, 10, 13, 16)
EPS = 1e-06
GELU_COEF = 0.7978845608028654
AXES = ("dp", "fsdp")
LOW = jnp.bfloat16
WIDE = jnp.float32
NN = (((1,), (0,)), ((), ()))
NT = (((1,), (1,)), ((), ()))
TN = (((0,), (0,)), ((), ()))
VMEM_LIMIT = 56 << 20
BLOCKED = -30000.0
LIGHT = pl.CostEstimate(flops=1024, transcendentals=0, bytes_accessed=1024)


def dot(left, right, dims=NN):
    return lax.dot_general(left, right, dims, preferred_element_type=WIDE)


def two_parts(values):
    high = values.astype(LOW)
    return high, (values - high.astype(WIDE)).astype(LOW)


def split_dot(values, table):
    high, rest = two_parts(values)
    return dot(high, table) + dot(rest, table)


class Place:
    def __init__(self, dp_count, fsdp_count):
        self.grouped = dp_count == 4 and fsdp_count == 8
        self.dp_count = dp_count
        self.fsdp_count = fsdp_count
        dp_index = lax.axis_index("dp")
        fsdp_index = lax.axis_index("fsdp")
        self.dp_index, self.fsdp_index = dp_index, fsdp_index
        self.y, self.c = dp_index // 2, dp_index % 2
        self.z, self.x = fsdp_index // 2, fsdp_index % 2
        self.table = jnp.stack([self.y, self.c, self.z, self.x]).astype(jnp.int32)


def hop(values, dy=0, dc=0, dz=0, dx=0):
    pairs = [
        (d * 8 + f, (d ^ (2 * dy + dc)) * 8 + (f ^ (2 * dz + dx)))
        for d in range(4)
        for f in range(8)
    ]
    return lax.ppermute(values, AXES, pairs)


def tie(*values):
    return lax.optimization_barrier(values)


class Gather:
    def __init__(self, own):
        self.own = own

    def over_z(self):
        self.stack = jnp.concatenate([self.own] + [hop(self.own, dz=k) for k in (1, 2, 3)], 0)

    def over_xy(self):
        self.from_x, self.from_y = hop(self.stack, dx=1), hop(self.stack, dy=1)

    def over_both(self):
        half = self.stack.shape[0] // 2
        self.from_both = [hop(self.from_x[:half], dy=1), hop(self.from_y[half:], dx=1)]

    def over_core_first(self):
        self.first = [self.stack, self.from_x, self.from_y]
        self.first_core = [hop(piece, dc=1) for piece in self.first]

    def over_core(self):
        self.last_core = [hop(piece, dc=1) for piece in self.from_both]
        return self.first + self.from_both + self.first_core + self.last_core


def own_quarter(place, shard):
    rows, columns = shard.shape
    quarter = columns // 4
    return lax.dynamic_slice(shard, (0, (place.c * 2 + place.y) * quarter), (rows, quarter))


def weight_copies(place_ref, pieces, sources, buffer, sem):
    copies = []
    if len(pieces) == 1:
        window = pieces[0].at[:, pl.ds(sources, buffer.shape[1])]
        return [pltpu.make_async_copy(window, buffer, sem.at[0])]
    for column_from, quarter, rows, column_to in sources:
        for number in range(10):
            core, kind = number // 5, number % 5
            across, side = (0, 1, 0, 1, 1)[kind], (0, 0, 1, 1, 1)[kind]
            column = column_to + ((place_ref[1] ^ core) * 2 + (place_ref[0] ^ side)) * quarter
            members = range(4) if kind < 3 else range(2 * (kind - 3), 2 * (kind - 3) + 2)
            for place_in, k in enumerate(members):
                row = ((place_ref[2] ^ k) * 2 + (place_ref[3] ^ across)) * rows
                copies.append(
                    pltpu.make_async_copy(
                        pieces[number].at[pl.ds(place_in * rows, rows), pl.ds(column_from, quarter)],
                        buffer.at[
                            pl.ds(pl.multiple_of(row, 128), rows),
                            pl.ds(pl.multiple_of(column, 128), quarter),
                        ],
                        sem.at[len(copies)],
                    )
                )
    return copies


def add(left, right):
    return left.astype(WIDE) + right.astype(WIDE)


def add_blocks(place, jobs, name):
    arrays, in_specs, out_specs, out_shapes, plan = [], [], [], [], []

    def block_spec(block, where, steps):
        return pl.BlockSpec(block, lambda n, p: where(jnp.minimum(n, steps - 1), p))

    for steps, outs in jobs:
        for blocks, block, where_out, terms in outs:
            entry = []
            for array, where, when in terms:
                entry.append((len(arrays), when))
                arrays.append(array)
                in_specs.append(block_spec(block, where, steps))
            out_specs.append(block_spec(block, where_out, steps))
            out_shapes.append(jax.ShapeDtypeStruct((blocks[0] * block[0], blocks[1] * block[1]), LOW))
            plan.append((steps, entry))

    def body(place_ref, *refs):
        step = pl.program_id(0)
        for (steps, entry), out_ref in zip(plan, refs[len(arrays) :]):

            @pl.when(step < steps)
            def _():
                total = None
                for number, when in entry:
                    value = refs[number][...].astype(WIDE)
                    if when is not None:
                        value = jnp.where(when(step, place_ref), value, 0.0)
                    total = value if total is None else total + value
                out_ref[...] = total.astype(LOW)

    results = pl.pallas_call(
        body,
        grid_spec=pltpu.PrefetchScalarGridSpec(
            num_scalar_prefetch=1,
            grid=(max(steps for steps, _ in jobs),),
            in_specs=in_specs,
            out_specs=out_specs,
        ),
        out_shape=out_shapes,
        compiler_params=pltpu.CompilerParams(vmem_limit_bytes=VMEM_LIMIT),
        cost_estimate=LIGHT,
        name=name,
    )(place.table, *arrays)
    grouped, cursor = [], 0
    for _, outs in jobs:
        grouped.append(list(results[cursor : cursor + len(outs)]))
        cursor += len(outs)
    return grouped


class RowSum:
    def __init__(self, keep, arrived, rows, order):
        self.base = [keep, arrived]
        self.rows, self.width = rows, keep.shape[1] // 2
        self.streams = (
            [{"z": 0, "count": 2, "order": "yx"}, {"z": 2, "count": 2, "order": "xy"}]
            if order == "mixed"
            else [{"z": 0, "count": 4, "order": order}]
        )

    def first(self):
        outs = []
        for stream in self.streams:
            start, count = stream["z"], stream["count"]
            if stream["order"] == "yx":
                block, blocks = (count * self.rows, self.width), (2, 1)
                where = lambda n, p: (jnp.minimum(n, 1), 1 - p[0])
                out = lambda n, p: (jnp.minimum(n, 1), 0)
            else:
                block, blocks = (self.rows, 2 * self.width), (count, 1)
                where = lambda n, p, start=start: (2 * (start + n) + 1 - p[3], 0)
                out = lambda n, p: (n, 0)
            outs.append((blocks, block, out, [(t, where, None) for t in self.base]))
        steps = 2 if self.streams[0]["order"] == "yx" else self.streams[0]["count"]
        self.axes = [{"d" + stream["order"][0]: 1} for stream in self.streams]
        return steps, outs

    def second(self, arrived):
        block = (self.rows, self.width)
        outs, steps = [], self.streams[0]["count"]
        for stream, value in zip(self.streams, arrived):
            stream["first"] = value
            start, count = stream["z"], stream["count"]
            if stream["order"] == "yx":
                where = lambda n, p, start=start: (2 * (start + n) + 1 - p[3], p[0])
                terms = [(value, lambda n, p: (2 * n + 1 - p[3], 0), None)]
            else:
                where = lambda n, p, start=start: (2 * (start + n) + p[3], 1 - p[0])
                terms = [(value, lambda n, p: (n, 1 - p[0]), None)]
            outs.append(
                ((count, 1), block, lambda n, p: (n, 0), [(t, where, None) for t in self.base] + terms)
            )
        self.axes = [{"d" + stream["order"][1]: 1} for stream in self.streams]
        return steps, outs

    def terms(self, flip):
        out = [(t, lambda n, p: (2 * (p[2] ^ flip) + p[3], p[0]), None) for t in self.base]
        for stream in self.streams:
            mask = stream["count"] - 1
            when = None
            if stream["count"] == 2:
                when = lambda n, p, start=stream["z"]: (p[2] ^ flip) // 2 == start // 2
            if stream["order"] == "yx":
                first = lambda n, p, mask=mask: (2 * ((p[2] ^ flip) & mask) + p[3], 0)
            else:
                first = lambda n, p, mask=mask: ((p[2] ^ flip) & mask, p[0])
            out.append((stream["first"], first, when))
            out.append((stream["second"], lambda n, p, mask=mask: ((p[2] ^ flip) & mask, 0), when))
        return out

    def third(self, arrived):
        for stream, value in zip(self.streams, arrived):
            stream["second"] = value
        self.axes = [{"dz": k} for k in (1, 2, 3)]
        block = (self.rows, self.width)
        return 1, [((1, 1), block, lambda n, p: (0, 0), self.terms(k)) for k in (1, 2, 3)]

    def last(self, arrived):
        terms = self.terms(0) + [(v, lambda n, p: (0, 0), None) for v in arrived]
        return 1, [((1, 1), (self.rows, self.width), lambda n, p: (0, 0), terms)]

    def moves(self, sums):
        return list(zip(sums, self.axes))


def beside(kernel, operand, moves):
    out = tie(operand, *(value for value, _ in moves))
    arrived = [hop(value, **axes) for value, (_, axes) in zip(out[1:], moves)]
    results = kernel(out[0])
    results = list(results) if isinstance(results, (list, tuple)) else [results]
    out = tie(*results, *arrived)
    results, arrived = list(out[: len(results)]), list(out[len(results) :])
    return (results[0] if len(results) == 1 else results), arrived


def lay_out_kernel(layouts, place_ref, *refs):
    quarters, outs = refs[: 4 * len(layouts)], refs[4 * len(layouts) :]
    here = place_ref[1] * 2 + place_ref[0]
    for number, ref in enumerate(quarters):
        index = here ^ (number % 4)
        for number, column, width, row, to, stride in layouts[number // 4]:
            rows = ref.shape[0]
            start = pl.multiple_of(to + index * stride, 128)
            outs[number][pl.ds(row, rows), pl.ds(start, width)] = ref[:, column : column + width].astype(WIDE)


def lay_out(place, quarters, layouts, shapes, name):
    vmem = pl.BlockSpec(memory_space=pltpu.VMEM)
    return pl.pallas_call(
        functools.partial(lay_out_kernel, layouts),
        in_specs=[pl.BlockSpec(memory_space=pltpu.SMEM)] + [vmem] * len(quarters),
        out_specs=[vmem] * len(shapes),
        out_shape=[jax.ShapeDtypeStruct(shape, WIDE) for shape in shapes],
        compiler_params=pltpu.CompilerParams(vmem_limit_bytes=VMEM_LIMIT),
        cost_estimate=LIGHT,
        name=name,
    )(place.table, *quarters)


def spread(own):
    return [own, hop(own, dy=1), hop(own, dc=1), hop(own, dy=1, dc=1)]


def reorder(stack, count, flip):
    return jnp.concatenate(
        [lax.dynamic_slice_in_dim(stack, i ^ flip, 1, axis=0) for i in range(count)], 0
    )


def small_over_z(values):
    return jnp.stack([values] + [hop(values, dz=k) for k in (1, 2, 3)])


def small_over_x(place, stack):
    count, tail = stack.shape[1], stack.shape[2:]
    stack = jnp.stack([stack, hop(stack, dx=1)], 1).reshape((8, count) + tail)
    return reorder(stack, 8, place.fsdp_index).reshape((8 * count,) + tail)


def gather_small(place, values, whole):
    if not place.grouped:
        return lax.all_gather(values, AXES if whole else "fsdp", axis=0, tiled=True)
    ordered = small_over_x(place, small_over_z(values))
    return over_dp(place, ordered) if whole else ordered


def over_dp(place, values):
    if not place.grouped:
        return lax.all_gather(values, "dp", axis=0, tiled=True)
    stack = jnp.stack([values, hop(values, dc=1), hop(values, dy=1), hop(values, dy=1, dc=1)])
    return reorder(stack, 4, place.dp_index).reshape((4 * values.shape[0],) + values.shape[1:])


def scatter_over_x(place, values):
    values = values.reshape((4, 2, values.shape[0] // 8) + values.shape[1:])
    mine = lax.dynamic_index_in_dim(values, place.x, 1, keepdims=False)
    other = lax.dynamic_index_in_dim(values, 1 - place.x, 1, keepdims=False)
    return mine + hop(other, dx=1)


def scatter_over_z(place, values):
    total = lax.dynamic_index_in_dim(values, place.z, 0, keepdims=False)
    for k in (1, 2, 3):
        total = total + hop(
            lax.dynamic_index_in_dim(values, place.z ^ k, 0, keepdims=False), dz=k
        )
    return total


def mask_tables(length):
    scale_ids = np.concatenate([np.full(side * side, i) for i, side in enumerate(PATCHES)])
    spare = np.arange(128) & 63
    slot = spare[None, :] - 2
    scale_column = scale_ids[:, None]
    later = (slot >= 0) & (slot < len(PATCHES)) & (slot > scale_column)
    query_side = np.where(later, BLOCKED, 0.0)
    key_side = np.where(slot == scale_column, 1.0, 0.0) + np.where(spare[None, :] < 2, 1.0, 0.0)
    return jnp.asarray(query_side, LOW), jnp.asarray(key_side, LOW)


FORWARD_BLOCKS = ((0, 240, 256), (240, 416, 512), (416, 680, 680))
BACKWARD_BLOCKS = ((424, 680, 680), (240, 424, 432), (0, 240, 256))


def attend_kernel(qkv_ref, qm_ref, km_ref, out_ref, extra_ref):
    query, key, value = (qkv_ref[0, :, 128 * n : 128 * n + 128] for n in range(3))
    query_mask, key_mask = qm_ref[...], km_ref[...]
    lane = lax.broadcasted_iota(jnp.int32, query.shape, 1)
    even = lane < 64
    ones = jnp.ones_like(value)
    heads = (
        (jnp.where(even, query, query_mask), jnp.where(even, key, key_mask), jnp.where(even, value, ones)),
        (jnp.where(even, query_mask, query), jnp.where(even, key_mask, key), jnp.where(even, ones, value)),
    )
    for start, stop, keys in FORWARD_BLOCKS:
        sums = []
        for query_head, key_head, value_head in heads:
            scores = dot(query_head[start:stop], key_head[:keys], NT)
            sums.append(dot(jnp.exp(scores).astype(LOW), value_head[:keys]))
        side = even[start:stop]
        chosen = jnp.where(side, sums[0], sums[1])
        totals = jnp.where(side, sums[1], sums[0])
        out_ref[0, start:stop, :] = (chosen / pltpu.roll(totals, 64, 1)).astype(LOW)
        high, rest = two_parts(-jnp.log(totals))
        spare = lane[start:stop] & 63
        extra_ref[0, start:stop, :] = jnp.where(
            spare == 0, high, jnp.where(spare == 1, rest, query_mask[start:stop])
        )


def attend(qkv, query_mask, key_mask):
    items, length, triple = qkv.shape
    pairs = triple // 384
    block = pl.BlockSpec((1, length, 128), lambda i, p: (i, 0, p))
    table = pl.BlockSpec((length, 128), lambda i, p: (0, 0))
    return pl.pallas_call(
        attend_kernel,
        grid=(items, pairs),
        in_specs=[pl.BlockSpec((1, length, 384), lambda i, p: (i, 0, p)), table, table],
        out_specs=[block, block],
        out_shape=[jax.ShapeDtypeStruct((items, length, 128 * pairs), LOW)] * 2,
        compiler_params=pltpu.CompilerParams(vmem_limit_bytes=VMEM_LIMIT),
        cost_estimate=LIGHT,
        name="attend",
    )(qkv, query_mask, key_mask)


def side_table(cross, size=128):
    first = lax.broadcasted_iota(jnp.int32, (size, size), 0) // 64
    second = lax.broadcasted_iota(jnp.int32, (size, size), 1) // 64
    return jnp.where((first != second) if cross else (first == second), 1.0, 0.0).astype(LOW)


def attend_back_kernel(
    qkv_ref, extra_ref, km_ref, out_ref, grad_ref, root_ref, gain_ref,
    grad_qkv_ref, head_ref, value_sum, key_sum, query_sum,
):
    query, key, value = (qkv_ref[0, :, 128 * n : 128 * n + 128] for n in range(3))
    key_mask, grad, extra = km_ref[...], grad_ref[0], extra_ref[0]
    lane = lax.broadcasted_iota(jnp.int32, query.shape, 1)
    even = lane < 64
    spare = lane & 63
    centre = split_dot(grad.astype(WIDE) * out_ref[0].astype(WIDE), side_table(True))
    high, rest = two_parts(-centre)
    grad_extra = jnp.where(spare == 0, high, jnp.where(spare == 1, rest, jnp.zeros_like(high)))
    ones = jnp.ones_like(value)
    key_rows = key.astype(WIDE).T.astype(LOW)
    heads = (
        (jnp.where(even, query, extra), jnp.where(even, key, key_mask),
         jnp.where(even, value, ones), jnp.where(even, grad, grad_extra)),
        (jnp.where(even, extra, query), jnp.where(even, key_mask, key),
         jnp.where(even, ones, value), jnp.where(even, grad_extra, grad)),
    )
    for head, (query_head, key_head, value_head, grad_head) in enumerate(heads):
        head_rows = key_rows[64 * head : 64 * head + 64]
        for number, (start, stop, keys) in enumerate(BACKWARD_BLOCKS):
            probs = jnp.exp(dot(key_head[:keys], query_head[start:stop], NT))
            grad_probs = dot(value_head[:keys], grad_head[start:stop], NT)
            grad_scores = (probs * grad_probs).astype(LOW)
            value_part = dot(probs.astype(LOW), grad[start:stop])
            key_part = dot(grad_scores, query[start:stop])
            if number == 0:
                value_sum[head] = value_part
                key_sum[head] = key_part
            else:
                value_sum[head, :keys] += value_part
                key_sum[head, :keys] += key_part
            query_sum[start:stop, 64 * head : 64 * head + 64] = dot(head_rows[:, :keys], grad_scores).T
    row = lax.broadcasted_iota(jnp.int32, (128, 128), 0)
    wanted = jnp.where(lax.broadcasted_iota(jnp.int32, (128, 128), 1) >= 64, 64, 0)
    roots = root_ref[0]
    root_query = dot(roots, jnp.where(row == wanted, 1.0, 0.0).astype(LOW))
    root_key = dot(roots, jnp.where(row == wanted + 32, 1.0, 0.0).astype(LOW))
    same = side_table(False)
    gain = gain_ref[...]
    grad_query = query_sum[...] * gain
    unit_query = query.astype(WIDE) / gain
    product = unit_query * grad_query
    head_ref[0] = jnp.sum(product, 0, keepdims=True)
    grad_qkv_ref[0, :, :128] = (
        root_query * (grad_query - unit_query * split_dot(product, same))
    ).astype(LOW)
    grad_key = jnp.where(even, key_sum[0], key_sum[1])
    unit_key = key.astype(WIDE)
    grad_qkv_ref[0, :, 128:256] = (
        root_key * (grad_key - unit_key * split_dot(unit_key * grad_key, same))
    ).astype(LOW)
    grad_qkv_ref[0, :, 256:] = jnp.where(even, value_sum[0], value_sum[1]).astype(LOW)


def attend_back(qkv, extra, key_mask, out, grad, roots, gain, first, pairs):
    items, length, _ = qkv.shape
    block = pl.BlockSpec((1, length, 128), lambda i, p: (i, 0, p + first))
    table = pl.BlockSpec((length, 128), lambda i, p: (0, 0))
    return pl.pallas_call(
        attend_back_kernel,
        grid=(items, pairs),
        in_specs=[pl.BlockSpec((1, length, 384), lambda i, p: (i, 0, p + first))]
        + [block, table, block, block, block, pl.BlockSpec((1, 128), lambda i, p: (0, p + first))],
        out_specs=[
            pl.BlockSpec((1, length, 384), lambda i, p: (i, 0, p)),
            pl.BlockSpec((1, 1, 128), lambda i, p: (i, 0, p)),
        ],
        out_shape=[
            jax.ShapeDtypeStruct((items, length, 384 * pairs), LOW),
            jax.ShapeDtypeStruct((items, 1, 128 * pairs), WIDE),
        ],
        scratch_shapes=[
            pltpu.VMEM((2, length, 128), WIDE),
            pltpu.VMEM((2, length, 128), WIDE),
            pltpu.VMEM((length, 128), WIDE),
        ],
        compiler_params=pltpu.CompilerParams(vmem_limit_bytes=VMEM_LIMIT),
        cost_estimate=LIGHT,
        name="attend_back",
    )(qkv, extra, key_mask, out, grad, roots, gain)


def row_facts(lengths_ref, block_rows, length):
    row = pl.program_id(0) * block_rows + lax.broadcasted_iota(jnp.int32, (block_rows, 1), 0)
    second = row >= length
    end = jnp.where(second, length + lengths_ref[1], lengths_ref[0])
    return second, row < end


def per_row(ref, second):
    return jnp.where(second, ref[1:2, :], ref[0:1, :])


def add_sums(ref, start, second, values):
    ref[start : start + 1, :] += jnp.sum(jnp.where(second, 0.0, values), 0, keepdims=True)
    ref[start + 1 : start + 2, :] += jnp.sum(jnp.where(second, values, 0.0), 0, keepdims=True)


def normalize(values):
    centred = values - jnp.mean(values, -1, keepdims=True)
    scale = lax.rsqrt(jnp.mean(centred * centred, -1, keepdims=True) + EPS)
    return centred * scale, scale


def token_call(kernel, place, rows, length, lengths, blocked, full, weights, outs, sums, name):
    block_rows = 2 * length // 5
    grid = rows // block_rows
    parts, where = [], []
    for pieces, sources, _ in weights:
        start = len(parts)
        parts.extend(pieces)
        where.append((start, len(pieces), sources))
    shapes = [weight[2] for weight in weights]
    counts = [1 if count == 1 else 32 * len(sources) for _, count, sources in where]
    blocked_count, full_count, out_count, weight_count = len(blocked), len(full), len(outs), len(weights)

    def body(place_ref, lengths_ref, *refs):
        cursor = 0

        def take(count):
            nonlocal cursor
            cursor += count
            return refs[cursor - count : cursor]

        token_refs, full_refs, part_refs = take(blocked_count), take(full_count), take(len(parts))
        out_refs, sum_refs = take(out_count), take(sums)
        buffers, sems = take(weight_count), take(weight_count)
        first = pl.program_id(0) == 0

        def copies(number):
            start, count, sources = where[number]
            return weight_copies(
                place_ref, part_refs[start : start + count], sources, buffers[number], sems[number]
            )

        @pl.when(first)
        def _():
            for number in range(weight_count):
                for copy in copies(number):
                    copy.start()
            for ref in sum_refs:
                ref[...] = jnp.zeros_like(ref)

        def ready(number):
            @pl.when(first)
            def _():
                for copy in copies(number):
                    copy.wait()

            return buffers[number]

        second, real = row_facts(lengths_ref, block_rows, length)
        kernel(second, real, token_refs, full_refs, ready, out_refs, sum_refs)

    any_space = pl.BlockSpec(memory_space=pl.ANY)
    smem = pl.BlockSpec(memory_space=pltpu.SMEM)
    return pl.pallas_call(
        body,
        grid=(grid,),
        in_specs=[smem, smem]
        + [pl.BlockSpec((block_rows, v.shape[1]), lambda i: (i, 0)) for v in blocked]
        + [pl.BlockSpec(v.shape, lambda i: (0, 0)) for v in full]
        + [any_space] * len(parts),
        out_specs=[pl.BlockSpec((block_rows, width), lambda i: (i, 0)) for width, _ in outs]
        + [pl.BlockSpec((16, 1024), lambda i: (0, 0))] * sums,
        out_shape=[jax.ShapeDtypeStruct((rows, width), kind) for width, kind in outs]
        + [jax.ShapeDtypeStruct((16, 1024), WIDE)] * sums,
        scratch_shapes=[pltpu.VMEM(shape, LOW) for shape in shapes]
        + [pltpu.SemaphoreType.DMA((count,)) for count in counts],
        compiler_params=pltpu.CompilerParams(vmem_limit_bytes=VMEM_LIMIT),
        cost_estimate=LIGHT,
        name=name,
    )(place.table, lengths, *blocked, *full, *parts)


def project_kernel(second, real, tokens, full, ready, outs, sums):
    (x_ref,) = tokens
    scale, shift, gain = full
    h_ref, qkv_ref, root_ref = outs
    unit, _ = normalize(x_ref[...].astype(WIDE))
    hidden = (unit * (1.0 + per_row(scale, second)) + per_row(shift, second)).astype(LOW)
    h_ref[...] = hidden
    same = side_table(False, 256)
    first_half = (lax.broadcasted_iota(jnp.int32, (hidden.shape[0], 128), 1) & 32) == 0
    weight = ready(0)
    for pair in range(weight.shape[1] // 384):
        start = 384 * pair
        raw = dot(hidden, weight[:, start : start + 384])
        both = raw[:, :256]
        root = lax.rsqrt(dot((both * both).astype(LOW), same) + EPS)
        root_ref[:, 128 * pair : 128 * pair + 128] = jnp.where(
            first_half, root[:, :128], root[:, 128:]
        ).astype(LOW)
        query = raw[:, :128] * (root[:, :128] * gain[:, 128 * pair : 128 * pair + 128])
        qkv_ref[:, start : start + 128] = query.astype(LOW)
        qkv_ref[:, start + 128 : start + 256] = (raw[:, 128:256] * root[:, 128:]).astype(LOW)
        qkv_ref[:, start + 256 : start + 384] = raw[:, 256:].astype(LOW)


def block_kernel(second, real, tokens, full, ready, outs, sums):
    attended_ref, x_ref, cot_ref = tokens
    gamma_one_ref, gamma_two_ref, scale_ref, shift_ref = full
    out_ref, h_ref, act_ref, mlp_grad_ref, hidden_grad_ref, middle_ref, attn_grad_ref, attended_grad_ref = outs
    (sum_ref,) = sums
    gate_one, gate_two = per_row(gamma_one_ref, second), per_row(gamma_two_ref, second)
    scale = 1.0 + per_row(scale_ref, second)
    upstream = cot_ref[...].astype(WIDE)
    mlp_grad = jnp.where(real, gate_two * upstream, 0.0).astype(LOW)
    mlp_grad_ref[...] = mlp_grad
    proj = ready(0)
    attn = dot(attended_ref[...], proj[...])
    branch_one = jnp.where(real, gate_one * attn, 0.0)
    middle = x_ref[...].astype(WIDE) + branch_one
    unit, root = normalize(middle)
    hidden = (unit * scale + per_row(shift_ref, second)).astype(LOW)
    h_ref[...] = hidden
    mlp, grad = 0.0, 0.0
    width = 1024
    fc1, fc2 = ready(1), ready(2)
    for start in range(0, fc1.shape[1], width):
        span = slice(start, start + width)
        wide = dot(hidden, fc1[:, span])
        act_grad = dot(mlp_grad, fc2[span, :], NT)
        square = wide * wide
        lift = 0.5 + 0.5 * jnp.tanh(wide * (GELU_COEF + (GELU_COEF * 0.044715) * square))
        act = (wide * lift).astype(LOW)
        act_ref[:, span] = act
        bend = wide * (2.0 * GELU_COEF + (6.0 * 0.044715 * GELU_COEF) * square)
        hidden_grad = (act_grad * (lift * (1.0 + bend * (1.0 - lift)))).astype(LOW)
        hidden_grad_ref[:, span] = hidden_grad
        mlp = mlp + dot(act, fc2[span, :])
        grad = grad + dot(hidden_grad, fc1[:, span], NT)
    branch_two = jnp.where(real, gate_two * mlp, 0.0)
    stream = middle + branch_two
    out_ref[...] = stream.astype(LOW)
    scaled = grad * scale
    middle_grad = upstream + root * (
        scaled - jnp.mean(scaled, -1, keepdims=True) - unit * jnp.mean(scaled * unit, -1, keepdims=True)
    )
    middle_ref[...] = middle_grad.astype(LOW)
    attn_grad = jnp.where(real, gate_one * middle_grad, 0.0).astype(LOW)
    attn_grad_ref[...] = attn_grad
    attended_grad_ref[...] = dot(attn_grad, proj[...], NT).astype(LOW)
    add_sums(sum_ref, 0, second, jnp.where(real, stream * stream, 0.0))
    add_sums(sum_ref, 2, second, branch_one * branch_one)
    add_sums(sum_ref, 4, second, branch_two * branch_two)
    add_sums(sum_ref, 6, second, jnp.where(real, mlp * upstream, 0.0))
    add_sums(sum_ref, 8, second, jnp.where(real, attn * middle_grad, 0.0))
    add_sums(sum_ref, 10, second, grad * unit)
    add_sums(sum_ref, 12, second, grad)


def token_back_kernel(second, real, tokens, full, ready, outs, sums):
    *grad_refs, x_ref, middle_ref = tokens
    (scale,) = full
    (out_ref,) = outs
    (sum_ref,) = sums
    weight = ready(0)
    grad, column = 0.0, 0
    for ref in grad_refs:
        grad = grad + dot(ref[...], weight[:, column : column + ref.shape[1]], NT)
        column += ref.shape[1]
    unit, root = normalize(x_ref[...].astype(WIDE))
    add_sums(sum_ref, 0, second, grad * unit)
    add_sums(sum_ref, 2, second, grad)
    scaled = grad * (1.0 + per_row(scale, second))
    total = middle_ref[...].astype(WIDE) + root * (
        scaled - jnp.mean(scaled, -1, keepdims=True) - unit * jnp.mean(scaled * unit, -1, keepdims=True)
    )
    out_ref[...] = total.astype(LOW)


def outer_kernel(half_ref, left_ref, right_ref, out_ref):
    out_ref[...] = dot(left_ref[...], right_ref[...], TN).astype(LOW)


def outer(left, right, half):
    count, height = left.shape
    width = right.shape[1] // 2
    tall = min(height, 1024)
    wide = min(width, 1024 if width % 1024 == 0 else 768 if width % 768 == 0 else 512)
    steps = width // wide
    return pl.pallas_call(
        outer_kernel,
        grid_spec=pltpu.PrefetchScalarGridSpec(
            num_scalar_prefetch=1,
            grid=(height // tall, steps),
            in_specs=[
                pl.BlockSpec((count, tall), lambda i, j, h: (0, i)),
                pl.BlockSpec((count, wide), lambda i, j, h: (0, h[0] * steps + j)),
            ],
            out_specs=pl.BlockSpec((tall, wide), lambda i, j, h: (i, j)),
        ),
        out_shape=jax.ShapeDtypeStruct((height, width), LOW),
        compiler_params=pltpu.CompilerParams(vmem_limit_bytes=VMEM_LIMIT),
        cost_estimate=LIGHT,
        name="outer",
    )(half.reshape(1).astype(jnp.int32), left, right)


def outer_pair(left, right, other_left, other_right, half):
    count, height = left.shape
    widths = (right.shape[1] // 4, other_right.shape[1] // 4)
    total = sum(widths)
    whole = lambda v: pl.BlockSpec(v.shape, lambda j, h: (0, 0))
    part = lambda width: pl.BlockSpec((count, width), lambda j, h: (0, 2 * h[0] + j))

    def body(half_ref, left_ref, right_ref, other_left_ref, other_right_ref, out_ref):
        out_ref[:, : widths[0]] = dot(left_ref[...], right_ref[...], TN).astype(LOW)
        out_ref[:, widths[0] :] = dot(other_left_ref[...], other_right_ref[...], TN).astype(LOW)

    return pl.pallas_call(
        body,
        grid_spec=pltpu.PrefetchScalarGridSpec(
            num_scalar_prefetch=1,
            grid=(2,),
            in_specs=[whole(left), part(widths[0]), whole(other_left), part(widths[1])],
            out_specs=pl.BlockSpec((height, total), lambda j, h: (0, j)),
        ),
        out_shape=jax.ShapeDtypeStruct((height, 2 * total), LOW),
        compiler_params=pltpu.CompilerParams(vmem_limit_bytes=VMEM_LIMIT),
        cost_estimate=LIGHT,
        name="outer_pair",
    )(half.reshape(1).astype(jnp.int32), left, right, other_left, other_right)


def plain_sum(place, keep, send):
    flip = place.c == 1
    full = jnp.concatenate([jnp.where(flip, send, keep), jnp.where(flip, keep, send)], 1)
    part = lax.psum_scatter(full, "fsdp", scatter_dimension=0, tiled=True)
    return lax.psum(part, "dp").astype(WIDE)


def shards(place_counts, tokens, cond, stop_scale, w_ada, w_qkv, w_proj, w_fc1, w_fc2, head_log_scale, cotangent):
    place = Place(*place_counts)
    items, width = cond.shape
    rows = tokens.shape[0]
    length = rows // items
    heads = head_log_scale.shape[0]
    pairs = heads // 2
    hidden_width = w_fc1.shape[1]
    ends = jnp.asarray(np.cumsum([side * side for side in PATCHES]).astype(np.int32))
    lengths = jnp.sum(jnp.where(jnp.arange(len(PATCHES))[None, :] == stop_scale[:, None], ends[None, :], 0), 1)

    def by_pair(matrix):
        return jnp.swapaxes(matrix.reshape(matrix.shape[0], 3, pairs, 128), 1, 2).reshape(matrix.shape)

    def from_pair(matrix):
        return jnp.swapaxes(matrix.reshape(matrix.shape[0], pairs, 3, 128), 1, 2).reshape(matrix.shape)

    paired = by_pair(w_qkv)
    half = paired.shape[1] // 2
    cond_wide = cond.astype(WIDE)
    silu_cond = (cond_wide * jax.nn.sigmoid(cond_wide)).astype(LOW)
    ada_rows = w_ada.shape[0]
    group_count = items * place.fsdp_count
    ada_columns = (0, place.fsdp_index * ada_rows)

    def part_modulation(group_cond):
        return dot(lax.dynamic_slice(group_cond, ada_columns, (group_count, ada_rows)), w_ada)

    if place.grouped:
        unit_rows = w_qkv.shape[0]
        cond_stack = small_over_z(silu_cond)
        own_qkv, cond_stack = tie(own_quarter(place, paired), cond_stack)
        qkv = Gather(own_qkv)
        qkv.over_z()
        mixed = scatter_over_x(place, part_modulation(small_over_x(place, cond_stack)))
        qkv.stack, mixed = tie(qkv.stack, mixed)
        qkv.over_xy()
        modulation = scatter_over_z(place, mixed)
        own_rest = jnp.concatenate([own_quarter(place, w_proj), own_quarter(place, w_fc1)], 1)
        own_rest, modulation = tie(own_rest, modulation)
        rest = Gather(own_rest)
        rest.over_z()
        qkv.over_both()
        qkv.over_core_first()
        rest.stack, *qkv.from_both = tie(rest.stack, *qkv.from_both)
        rest.over_xy()
        qkv_parts = qkv.over_core()
        piece = w_fc2.shape[0] // place.dp_count
        fc2_piece = lax.dynamic_slice(w_fc2, (place.dp_index * piece, 0), (piece, width))
        fc2_piece, qkv_parts[-1] = tie(fc2_piece, qkv_parts[-1])
        fc2_full = lax.all_gather(fc2_piece, ("fsdp", "dp"), axis=0, tiled=True)
        quarter = half // 2
        qkv_weight = (qkv_parts, [(0, quarter, unit_rows, 0)], (width, 2 * half))
        fc2_weight = ([fc2_full], 0, (hidden_width, width))
    else:
        qkv_weight, proj_weight, fc1_weight, fc2_weight = (
            ([lax.all_gather(w, "fsdp", axis=0, tiled=True)], 0, (w.shape[0] * place.fsdp_count, w.shape[1]))
            for w in (paired, w_proj, w_fc1, w_fc2)
        )
        modulation = lax.psum_scatter(
            part_modulation(gather_small(place, silu_cond, False)), "fsdp", scatter_dimension=0, tiled=True
        )
    gamma_one, gamma_two, scale_one, scale_two, shift_one, shift_two = [
        modulation[:, n * width : (n + 1) * width] for n in range(6)
    ]

    gain = jnp.repeat(jnp.exp(head_log_scale), width // heads)[None, :]
    normed_one, projected, roots = token_call(
        project_kernel, place, rows, length, lengths, [tokens], [scale_one, shift_one, gain],
        [qkv_weight], [(width, LOW), (3 * width, LOW), (width, LOW)], 0, "project",
    )
    if place.grouped:
        rest.from_x, rest.from_y, projected = tie(rest.from_x, rest.from_y, projected)
        rest.over_both()
        rest.over_core_first()
    cube = (items, length, width)
    projected, roots = projected.reshape(items, length, 3 * width), roots.reshape(cube)
    query_mask, key_mask = mask_tables(length)
    attended, extra = attend(projected, query_mask, key_mask)
    if place.grouped:
        attended, *rest.from_both = tie(attended, *rest.from_both)
        rest_parts = rest.over_core()
        proj_weight = (rest_parts, [(0, width // 4, unit_rows, 0)], (width, width))
        fc1_weight = (
            rest_parts, [(width // 4, hidden_width // 4, unit_rows, 0)], (width, hidden_width)
        )
    flat_attended = attended.reshape(rows, width)
    (
        result, normed_two, act, grad_mlp, grad_hidden, grad_middle, grad_attn, grad_attended, sum_one,
    ) = token_call(
        block_kernel, place, rows, length, lengths, [flat_attended, tokens, cotangent],
        [gamma_one, gamma_two, scale_two, shift_two], [proj_weight, fc1_weight, fc2_weight],
        [(width, LOW), (width, LOW), (hidden_width, LOW), (width, LOW), (hidden_width, LOW)]
        + [(width, LOW)] * 3, 1, "block",
    )

    def send_part(left, right):
        return outer(left, right, 1 - place.c)

    def keep_part(left, right):
        return outer(left, right, place.c)

    def heads_back(grad, first):
        out, sums = attend_back(
            projected, extra, key_mask, attended, grad.reshape(cube), roots, gain, first, pairs // 2
        )
        return out.reshape(rows, half), sums

    def token_back(first, second):
        return token_call(
            token_back_kernel, place, rows, length, lengths, [first, second, tokens, grad_middle],
            [scale_one], [qkv_weight], [(width, LOW)], 1, "token_back",
        )

    if place.grouped:
        quarter = width // 4
        fc2_send = send_part(act, grad_mlp)
        fc2_keep, arrived = beside(lambda g: keep_part(act, g), grad_mlp, [(fc2_send, {"dc": 1})])
        fc2 = RowSum(fc2_keep, arrived[0], w_fc2.shape[0], "mixed")
        (sums,) = add_blocks(place, [fc2.first()], "sums_a")

        (grad_first, heads_first), arrived = beside(
            lambda g: heads_back(g, 0), grad_attended, fc2.moves(sums)
        )
        (sums,) = add_blocks(place, [fc2.second(arrived)], "sums_b")

        first_pair = functools.partial(outer_pair, normed_one, grad_first, flat_attended)
        first_send, fc2_arrived = beside(
            lambda g: first_pair(g, 1 - place.c), tie(grad_attn, grad_first)[0], fc2.moves(sums)
        )
        first_keep, arrived = beside(lambda g: first_pair(g, place.c), grad_attn, [(first_send, {"dc": 1})])
        first = RowSum(first_keep, arrived[0], unit_rows, "mixed")
        first_sums, fc2_sums = add_blocks(place, [first.first(), fc2.third(fc2_arrived)], "sums_c")
        fc2_moves = fc2.moves(fc2_sums)

        fc1_send, arrived = beside(lambda g: send_part(normed_two, g), grad_hidden, first.moves(first_sums))
        (first_sums,) = add_blocks(place, [first.second(arrived)], "sums_d")
        fc1_keep, arrived = beside(
            lambda g: keep_part(normed_two, g), grad_hidden, [(fc1_send, {"dc": 1})] + first.moves(first_sums)
        )
        fc1 = RowSum(fc1_keep, arrived[0], unit_rows, "mixed")
        fc1_sums, first_sums = add_blocks(place, [fc1.first(), first.third(arrived[1:])], "sums_e")
        first_moves = first.moves(first_sums)

        (grad_second, heads_second), arrived = beside(
            lambda g: heads_back(g, pairs // 2), grad_attended, fc1.moves(fc1_sums) + fc2_moves
        )
        fc1_sums, (fc2_own,) = add_blocks(
            place, [fc1.second(arrived[:2]), fc2.last(arrived[2:])], "sums_f"
        )
        second_send, fc1_arrived = beside(
            lambda g: send_part(normed_one, g), grad_second, fc1.moves(fc1_sums)
        )
        second_keep, arrived = beside(
            lambda g: keep_part(normed_one, g), grad_second,
            [(second_send, {"dc": 1}), (fc2_own, {"dy": 1})] + first_moves,
        )
        fc2_y = arrived[1]
        second = RowSum(second_keep, arrived[0], unit_rows, "mixed")
        second_sums, fc1_sums, (first_own,) = add_blocks(
            place, [second.first(), fc1.third(fc1_arrived), first.last(arrived[2:])], "sums_g"
        )
        (grad_tokens, sum_four), arrived = beside(
            lambda g: token_back(grad_first, g), grad_second, second.moves(second_sums) + fc1.moves(fc1_sums)
        )
        second_sums, (fc1_own,) = add_blocks(
            place, [second.second(arrived[:2]), fc1.last(arrived[2:])], "sums_h"
        )
        second_moves = second.moves(second_sums)
        sum_four = tie(sum_four, *second_sums)[0]
        second_arrived = [hop(v, **axes) for v, axes in second_moves]
        (second_sums,) = add_blocks(place, [second.third(second_arrived)], "sums_i")
        fc2_core = [hop(fc2_own, dc=1), hop(fc2_y, dc=1)]
        others = jnp.concatenate([fc1_own, first_own], 1)
        others_y = hop(others, dy=1)
        others_core = [hop(others, dc=1), hop(others_y, dc=1)]
        ((second_own,),) = add_blocks(
            place, [second.last([hop(v, **axes) for v, axes in second.moves(second_sums)])], "sums_j"
        )
        second_all = spread(second_own)
        (grad_fc2,) = lay_out(
            place, [fc2_own, fc2_y] + fc2_core, [[(0, 0, quarter, 0, 0, quarter)]], [w_fc2.shape], "lay_out_fc2"
        )
        wide = hidden_width // 4
        layout = [(0, 0, wide, 0, 0, wide), (1, wide + 384, quarter, 0, 0, quarter)]
        layout += [(2, wide + 128 * n, 128, 0, n * width, 128) for n in range(3)]
        layout_two = [(2, 128 * n, 128, 0, n * width + 512, 128) for n in range(3)]
        grad_fc1, grad_proj, grad_qkv = lay_out(
            place, [others, others_y] + others_core + second_all, [layout, layout_two],
            [w_fc1.shape, w_proj.shape, w_qkv.shape], "lay_out_others",
        )
    else:
        def whole_sum(left, right):
            return plain_sum(place, keep_part(left, right), send_part(left, right))

        grad_fc2 = whole_sum(act, grad_mlp)
        grad_fc1 = whole_sum(normed_two, grad_hidden)
        grad_proj = whole_sum(flat_attended, grad_attn)
        grad_first, heads_first = heads_back(grad_attended, 0)
        grad_second, heads_second = heads_back(grad_attended, pairs // 2)
        grad_qkv = from_pair(
            jnp.concatenate([whole_sum(normed_one, grad_first), whole_sum(normed_one, grad_second)], 1)
        )
        grad_tokens, sum_four = token_back(grad_first, grad_second)

    head_terms = jnp.concatenate([heads_first, heads_second], 2).reshape(items, heads, width // heads).sum(2)
    head_parts = jnp.concatenate([*two_parts(head_terms), jnp.zeros((items, 128 - 2 * heads), LOW)], 1)
    grad_modulation = jnp.concatenate(
        [sum_one[8:10], sum_one[6:8], sum_four[0:2], sum_one[10:12], sum_four[2:4], sum_one[12:14]], 1
    ).astype(LOW)
    group = gather_small(place, jnp.concatenate([grad_modulation, head_parts, silu_cond], 1), False)
    grad_columns = dot(group[:, : 6 * width], w_ada, NT)
    everything = over_dp(place, group)
    all_heads = everything[:, 6 * width : 6 * width + 2 * heads].astype(WIDE)
    grad_head = jnp.sum(all_heads[:, :heads] + all_heads[:, heads:], 0)
    all_slice = lax.dynamic_slice(
        everything, (0, 6 * width + 128 + place.fsdp_index * ada_rows), (everything.shape[0], ada_rows)
    )
    grad_ada = dot(all_slice, everything[:, : 6 * width], TN)
    grad_parts = gather_small(place, grad_columns[None], False)
    own_items = lax.dynamic_slice(
        grad_parts, (0, place.fsdp_index * items, 0), (grad_parts.shape[0], items, ada_rows)
    )
    grad_silu = jnp.swapaxes(own_items, 0, 1).reshape(items, width)
    gate = jax.nn.sigmoid(cond_wide)
    grad_cond = (grad_silu * gate * (1.0 + cond_wide * (1.0 - gate))).astype(LOW)

    counted = (lengths * width).astype(WIDE)
    squares = jnp.stack(
        [sum_one[0:2].sum(1), sum_one[2:4].sum(1), sum_one[4:6].sum(1)], 1
    )
    rms_rows = jnp.sqrt(squares / counted[:, None] + EPS)
    return (
        result, grad_tokens, grad_cond, grad_ada, grad_qkv, grad_proj, grad_fc1, grad_fc2,
        grad_head, rms_rows,
    )


def solution(mesh):
    both = P(("dp", "fsdp"), None)
    rows = P("fsdp", None)
    return jax.shard_map(
        functools.partial(shards, (mesh.shape["dp"], mesh.shape["fsdp"])),
        mesh=mesh,
        in_specs=(both, both, P(("dp", "fsdp")), rows, rows, rows, rows, rows, P(), both),
        out_specs=(both, both, both, rows, rows, rows, rows, rows, P(), both),
        check_vma=False,
    )
```

```python
import functools

import jax
import jax.numpy as jnp
import numpy as np
from jax import lax
from jax.experimental import pallas as pl
from jax.experimental.pallas import tpu as pltpu
from jax.sharding import PartitionSpec as P

PATCHES = (1, 2, 3, 4, 5, 6, 8, 10, 13, 16)
EPS = 1e-06
GELU_COEF = 0.7978845608028654
AXES = ("dp", "fsdp")
LOW = jnp.bfloat16
WIDE = jnp.float32
NN = (((1,), (0,)), ((), ()))
NT = (((1,), (1,)), ((), ()))
TN = (((0,), (0,)), ((), ()))
VMEM_LIMIT = 56 << 20
BLOCKED = -30000.0
LIGHT = pl.CostEstimate(flops=1024, transcendentals=0, bytes_accessed=1024)


def dot(left, right, dims=NN):
    return lax.dot_general(left, right, dims, preferred_element_type=WIDE)


def far(values):
    return pltpu.with_memory_space_constraint(values, pltpu.HBM)


def two_parts(values):
    high = values.astype(LOW)
    return high, (values - high.astype(WIDE)).astype(LOW)


def split_dot(values, table):
    high, rest = two_parts(values)
    return dot(high, table) + dot(rest, table)


class Place:
    def __init__(self, dp_count, fsdp_count):
        self.grouped = dp_count == 4 and fsdp_count == 8
        self.dp_count = dp_count
        self.fsdp_count = fsdp_count
        dp_index = lax.axis_index("dp")
        fsdp_index = lax.axis_index("fsdp")
        self.dp_index, self.fsdp_index = dp_index, fsdp_index
        self.y, self.c = dp_index // 2, dp_index % 2
        self.z, self.x = fsdp_index // 2, fsdp_index % 2
        self.table = jnp.stack([self.y, self.c, self.z, self.x]).astype(jnp.int32)


def hop(values, dy=0, dc=0, dz=0, dx=0):
    pairs = [
        (d * 8 + f, (d ^ (2 * dy + dc)) * 8 + (f ^ (2 * dz + dx)))
        for d in range(4)
        for f in range(8)
    ]
    return lax.ppermute(values, AXES, pairs)


def tie(*values):
    return lax.optimization_barrier(values)


class Gather:
    def __init__(self, own):
        self.own = own

    def over_z(self):
        self.stack = jnp.concatenate([self.own] + [hop(self.own, dz=k) for k in (1, 2, 3)], 0)

    def over_xy(self):
        self.from_x, self.from_y = hop(self.stack, dx=1), hop(self.stack, dy=1)

    def over_both(self):
        half = self.stack.shape[0] // 2
        self.from_both = [hop(self.from_x[:half], dy=1), hop(self.from_y[half:], dx=1)]

    def over_core_first(self):
        self.first = [self.stack, self.from_x, self.from_y]
        self.first_core = [hop(piece, dc=1) for piece in self.first]

    def over_core(self):
        self.last_core = [hop(piece, dc=1) for piece in self.from_both]
        return self.first + self.from_both + self.first_core + self.last_core


def own_quarter(place, shard):
    rows, columns = shard.shape
    quarter = columns // 4
    return lax.dynamic_slice(shard, (0, (place.c * 2 + place.y) * quarter), (rows, quarter))


def weight_copies(place_ref, pieces, sources, buffer, sem):
    copies = []
    if len(pieces) == 1:
        window = pieces[0].at[:, pl.ds(sources, buffer.shape[1])]
        return [pltpu.make_async_copy(window, buffer, sem.at[0])]
    for column_from, quarter, rows, column_to in sources:
        for number in range(10):
            core, kind = number // 5, number % 5
            across, side = (0, 1, 0, 1, 1)[kind], (0, 0, 1, 1, 1)[kind]
            column = column_to + ((place_ref[1] ^ core) * 2 + (place_ref[0] ^ side)) * quarter
            members = range(4) if kind < 3 else range(2 * (kind - 3), 2 * (kind - 3) + 2)
            for place_in, k in enumerate(members):
                row = ((place_ref[2] ^ k) * 2 + (place_ref[3] ^ across)) * rows
                copies.append(
                    pltpu.make_async_copy(
                        pieces[number].at[pl.ds(place_in * rows, rows), pl.ds(column_from, quarter)],
                        buffer.at[
                            pl.ds(pl.multiple_of(row, 128), rows),
                            pl.ds(pl.multiple_of(column, 128), quarter),
                        ],
                        sem.at[len(copies)],
                    )
                )
    return copies


def add(left, right):
    return left.astype(WIDE) + right.astype(WIDE)


def add_blocks(place, jobs, name):
    arrays, in_specs, out_specs, out_shapes, plan = [], [], [], [], []

    def block_spec(block, where, steps):
        return pl.BlockSpec(block, lambda n, p: where(jnp.minimum(n, steps - 1), p))

    for steps, outs in jobs:
        for blocks, block, where_out, terms in outs:
            entry = []
            for array, where, when in terms:
                entry.append((len(arrays), when))
                arrays.append(array)
                in_specs.append(block_spec(block, where, steps))
            out_specs.append(block_spec(block, where_out, steps))
            out_shapes.append(jax.ShapeDtypeStruct((blocks[0] * block[0], blocks[1] * block[1]), LOW))
            plan.append((steps, entry))

    def body(place_ref, *refs):
        step = pl.program_id(0)
        for (steps, entry), out_ref in zip(plan, refs[len(arrays) :]):

            @pl.when(step < steps)
            def _():
                total = None
                for number, when in entry:
                    value = refs[number][...].astype(WIDE)
                    if when is not None:
                        value = jnp.where(when(step, place_ref), value, 0.0)
                    total = value if total is None else total + value
                out_ref[...] = total.astype(LOW)

    results = pl.pallas_call(
        body,
        grid_spec=pltpu.PrefetchScalarGridSpec(
            num_scalar_prefetch=1,
            grid=(max(steps for steps, _ in jobs),),
            in_specs=in_specs,
            out_specs=out_specs,
        ),
        out_shape=out_shapes,
        compiler_params=pltpu.CompilerParams(vmem_limit_bytes=20 << 20),
        cost_estimate=LIGHT,
        name=name,
    )(place.table, *arrays)
    grouped, cursor = [], 0
    for _, outs in jobs:
        grouped.append(list(results[cursor : cursor + len(outs)]))
        cursor += len(outs)
    return grouped


class RowSum:
    def __init__(self, keep, arrived, rows, order):
        self.base = [keep, arrived]
        self.rest = [far(keep), far(arrived)]
        self.rows, self.width = rows, keep.shape[1] // 2
        self.streams = (
            [{"z": 0, "count": 2, "order": "yx"}, {"z": 2, "count": 2, "order": "xy"}]
            if order == "mixed"
            else [{"z": 0, "count": 4, "order": order}]
        )

    def first(self):
        outs = []
        for stream in self.streams:
            start, count = stream["z"], stream["count"]
            if stream["order"] == "yx":
                block, blocks = (count * self.rows, self.width), (2, 1)
                where = lambda n, p: (jnp.minimum(n, 1), 1 - p[0])
                out = lambda n, p: (jnp.minimum(n, 1), 0)
            else:
                block, blocks = (self.rows, 2 * self.width), (count, 1)
                where = lambda n, p, start=start: (2 * (start + n) + 1 - p[3], 0)
                out = lambda n, p: (n, 0)
            outs.append((blocks, block, out, [(t, where, None) for t in self.base]))
        steps = 2 if self.streams[0]["order"] == "yx" else self.streams[0]["count"]
        self.axes = [{"d" + stream["order"][0]: 1} for stream in self.streams]
        return steps, outs

    def second(self, arrived):
        block = (self.rows, self.width)
        outs, steps = [], self.streams[0]["count"]
        for stream, value in zip(self.streams, arrived):
            stream["first"] = value
            start, count = stream["z"], stream["count"]
            if stream["order"] == "yx":
                where = lambda n, p, start=start: (2 * (start + n) + 1 - p[3], p[0])
                terms = [(value, lambda n, p: (2 * n + 1 - p[3], 0), None)]
            else:
                where = lambda n, p, start=start: (2 * (start + n) + p[3], 1 - p[0])
                terms = [(value, lambda n, p: (n, 1 - p[0]), None)]
            outs.append(
                ((count, 1), block, lambda n, p: (n, 0), [(t, where, None) for t in self.rest] + terms)
            )
        self.axes = [{"d" + stream["order"][1]: 1} for stream in self.streams]
        return steps, outs

    def terms(self, flip):
        out = [(t, lambda n, p: (2 * (p[2] ^ flip) + p[3], p[0]), None) for t in self.rest]
        for stream in self.streams:
            mask = stream["count"] - 1
            when = None
            if stream["count"] == 2:
                when = lambda n, p, start=stream["z"]: (p[2] ^ flip) // 2 == start // 2
            if stream["order"] == "yx":
                first = lambda n, p, mask=mask: (2 * ((p[2] ^ flip) & mask) + p[3], 0)
            else:
                first = lambda n, p, mask=mask: ((p[2] ^ flip) & mask, p[0])
            out.append((stream["first"], first, when))
            out.append((stream["second"], lambda n, p, mask=mask: ((p[2] ^ flip) & mask, 0), when))
        return out

    def third(self, arrived):
        for stream, value in zip(self.streams, arrived):
            stream["second"] = value
        self.axes = [{"dz": k} for k in (1, 2, 3)]
        block = (self.rows, self.width)
        return 1, [((1, 1), block, lambda n, p: (0, 0), self.terms(k)) for k in (1, 2, 3)]

    def last(self, arrived):
        terms = self.terms(0) + [(v, lambda n, p: (0, 0), None) for v in arrived]
        return 1, [((1, 1), (self.rows, self.width), lambda n, p: (0, 0), terms)]

    def moves(self, sums):
        return list(zip(sums, self.axes))


def beside(kernel, operand, moves):
    out = tie(operand, *(value for value, _ in moves))
    arrived = [hop(value, **axes) for value, (_, axes) in zip(out[1:], moves)]
    results = kernel(out[0])
    results = list(results) if isinstance(results, (list, tuple)) else [results]
    out = tie(*results, *arrived)
    results, arrived = list(out[: len(results)]), list(out[len(results) :])
    return (results[0] if len(results) == 1 else results), arrived


def lay_out_kernel(layouts, place_ref, *refs):
    quarters, outs = refs[: 4 * len(layouts)], refs[4 * len(layouts) :]
    here = place_ref[1] * 2 + place_ref[0]
    for number, ref in enumerate(quarters):
        index = here ^ (number % 4)
        for number, column, width, row, to, stride in layouts[number // 4]:
            rows = ref.shape[0]
            start = pl.multiple_of(to + index * stride, 128)
            outs[number][pl.ds(row, rows), pl.ds(start, width)] = ref[:, column : column + width].astype(WIDE)


def lay_out(place, quarters, layouts, shapes, name):
    vmem = pl.BlockSpec(memory_space=pltpu.VMEM)
    return pl.pallas_call(
        functools.partial(lay_out_kernel, layouts),
        in_specs=[pl.BlockSpec(memory_space=pltpu.SMEM)] + [vmem] * len(quarters),
        out_specs=[vmem] * len(shapes),
        out_shape=[jax.ShapeDtypeStruct(shape, WIDE) for shape in shapes],
        compiler_params=pltpu.CompilerParams(vmem_limit_bytes=20 << 20),
        cost_estimate=LIGHT,
        name=name,
    )(place.table, *quarters)


def spread(own):
    return [own, hop(own, dy=1), hop(own, dc=1), hop(own, dy=1, dc=1)]


def reorder(stack, count, flip):
    return jnp.concatenate(
        [lax.dynamic_slice_in_dim(stack, i ^ flip, 1, axis=0) for i in range(count)], 0
    )


def small_over_z(values):
    return jnp.stack([values] + [hop(values, dz=k) for k in (1, 2, 3)])


def small_over_x(place, stack):
    count, tail = stack.shape[1], stack.shape[2:]
    stack = jnp.stack([stack, hop(stack, dx=1)], 1).reshape((8, count) + tail)
    return reorder(stack, 8, place.fsdp_index).reshape((8 * count,) + tail)


def gather_small(place, values, whole):
    if not place.grouped:
        return lax.all_gather(values, AXES if whole else "fsdp", axis=0, tiled=True)
    ordered = small_over_x(place, small_over_z(values))
    return over_dp(place, ordered) if whole else ordered


def over_dp(place, values):
    if not place.grouped:
        return lax.all_gather(values, "dp", axis=0, tiled=True)
    stack = jnp.stack([values, hop(values, dc=1), hop(values, dy=1), hop(values, dy=1, dc=1)])
    return reorder(stack, 4, place.dp_index).reshape((4 * values.shape[0],) + values.shape[1:])


def scatter_over_x(place, values):
    values = values.reshape((4, 2, values.shape[0] // 8) + values.shape[1:])
    mine = lax.dynamic_index_in_dim(values, place.x, 1, keepdims=False)
    other = lax.dynamic_index_in_dim(values, 1 - place.x, 1, keepdims=False)
    return mine + hop(other, dx=1)


def scatter_over_z(place, values):
    total = lax.dynamic_index_in_dim(values, place.z, 0, keepdims=False)
    for k in (1, 2, 3):
        total = total + hop(
            lax.dynamic_index_in_dim(values, place.z ^ k, 0, keepdims=False), dz=k
        )
    return total


def mask_tables(length):
    scale_ids = np.concatenate([np.full(side * side, i) for i, side in enumerate(PATCHES)])
    spare = np.arange(128) & 63
    slot = spare[None, :] - 2
    scale_column = scale_ids[:, None]
    later = (slot >= 0) & (slot < len(PATCHES)) & (slot > scale_column)
    query_side = np.where(later, BLOCKED, 0.0)
    key_side = np.where(slot == scale_column, 1.0, 0.0) + np.where(spare[None, :] < 2, 1.0, 0.0)
    return jnp.asarray(query_side, LOW), jnp.asarray(key_side, LOW)


FORWARD_BLOCKS = ((0, 240, 256), (240, 416, 512), (416, 680, 680))
BACKWARD_BLOCKS = ((424, 680, 680), (240, 424, 432), (0, 240, 256))


def attend_kernel(qkv_ref, qm_ref, km_ref, out_ref, extra_ref):
    query, key, value = (qkv_ref[0, :, 128 * n : 128 * n + 128] for n in range(3))
    query_mask, key_mask = qm_ref[...], km_ref[...]
    lane = lax.broadcasted_iota(jnp.int32, query.shape, 1)
    even = lane < 64
    ones = jnp.ones_like(value)
    heads = (
        (jnp.where(even, query, query_mask), jnp.where(even, key, key_mask), jnp.where(even, value, ones)),
        (jnp.where(even, query_mask, query), jnp.where(even, key_mask, key), jnp.where(even, ones, value)),
    )
    for start, stop, keys in FORWARD_BLOCKS:
        sums = []
        for query_head, key_head, value_head in heads:
            scores = dot(query_head[start:stop], key_head[:keys], NT)
            sums.append(dot(jnp.exp(scores).astype(LOW), value_head[:keys]))
        side = even[start:stop]
        chosen = jnp.where(side, sums[0], sums[1])
        totals = jnp.where(side, sums[1], sums[0])
        out_ref[0, start:stop, :] = (chosen / pltpu.roll(totals, 64, 1)).astype(LOW)
        high, rest = two_parts(-jnp.log(totals))
        spare = lane[start:stop] & 63
        extra_ref[0, start:stop, :] = jnp.where(
            spare == 0, high, jnp.where(spare == 1, rest, query_mask[start:stop])
        )


def attend(qkv, query_mask, key_mask):
    items, length, triple = qkv.shape
    pairs = triple // 384
    block = pl.BlockSpec((1, length, 128), lambda i, p: (i, 0, p))
    table = pl.BlockSpec((length, 128), lambda i, p: (0, 0))
    return pl.pallas_call(
        attend_kernel,
        grid=(items, pairs),
        in_specs=[pl.BlockSpec((1, length, 384), lambda i, p: (i, 0, p)), table, table],
        out_specs=[block, block],
        out_shape=[jax.ShapeDtypeStruct((items, length, 128 * pairs), LOW)] * 2,
        compiler_params=pltpu.CompilerParams(vmem_limit_bytes=24 << 20),
        cost_estimate=LIGHT,
        name="attend",
    )(far(qkv), query_mask, key_mask)


def side_table(cross, size=128):
    first = lax.broadcasted_iota(jnp.int32, (size, size), 0) // 64
    second = lax.broadcasted_iota(jnp.int32, (size, size), 1) // 64
    return jnp.where((first != second) if cross else (first == second), 1.0, 0.0).astype(LOW)


def attend_back_kernel(
    qkv_ref, extra_ref, km_ref, out_ref, grad_ref, root_ref, gain_ref,
    grad_qkv_ref, head_ref, value_sum, key_sum, query_sum,
):
    query, key, value = (qkv_ref[0, :, 128 * n : 128 * n + 128] for n in range(3))
    key_mask, grad, extra = km_ref[...], grad_ref[0], extra_ref[0]
    lane = lax.broadcasted_iota(jnp.int32, query.shape, 1)
    even = lane < 64
    spare = lane & 63
    centre = split_dot(grad.astype(WIDE) * out_ref[0].astype(WIDE), side_table(True))
    high, rest = two_parts(-centre)
    grad_extra = jnp.where(spare == 0, high, jnp.where(spare == 1, rest, jnp.zeros_like(high)))
    ones = jnp.ones_like(value)
    key_rows = key.astype(WIDE).T.astype(LOW)
    heads = (
        (jnp.where(even, query, extra), jnp.where(even, key, key_mask),
         jnp.where(even, value, ones), jnp.where(even, grad, grad_extra)),
        (jnp.where(even, extra, query), jnp.where(even, key_mask, key),
         jnp.where(even, ones, value), jnp.where(even, grad_extra, grad)),
    )
    for head, (query_head, key_head, value_head, grad_head) in enumerate(heads):
        head_rows = key_rows[64 * head : 64 * head + 64]
        for number, (start, stop, keys) in enumerate(BACKWARD_BLOCKS):
            probs = jnp.exp(dot(key_head[:keys], query_head[start:stop], NT))
            grad_probs = dot(value_head[:keys], grad_head[start:stop], NT)
            grad_scores = (probs * grad_probs).astype(LOW)
            value_part = dot(probs.astype(LOW), grad[start:stop])
            key_part = dot(grad_scores, query[start:stop])
            if number == 0:
                value_sum[head] = value_part
                key_sum[head] = key_part
            else:
                value_sum[head, :keys] += value_part
                key_sum[head, :keys] += key_part
            query_sum[start:stop, 64 * head : 64 * head + 64] = dot(head_rows[:, :keys], grad_scores).T
    row = lax.broadcasted_iota(jnp.int32, (128, 128), 0)
    wanted = jnp.where(lax.broadcasted_iota(jnp.int32, (128, 128), 1) >= 64, 64, 0)
    roots = root_ref[0]
    root_query = dot(roots, jnp.where(row == wanted, 1.0, 0.0).astype(LOW))
    root_key = dot(roots, jnp.where(row == wanted + 32, 1.0, 0.0).astype(LOW))
    same = side_table(False)
    gain = gain_ref[...]
    grad_query = query_sum[...] * gain
    unit_query = query.astype(WIDE) / gain
    product = unit_query * grad_query
    head_ref[0] = jnp.sum(product, 0, keepdims=True)
    grad_qkv_ref[0, :, :128] = (
        root_query * (grad_query - unit_query * split_dot(product, same))
    ).astype(LOW)
    grad_key = jnp.where(even, key_sum[0], key_sum[1])
    unit_key = key.astype(WIDE)
    grad_qkv_ref[0, :, 128:256] = (
        root_key * (grad_key - unit_key * split_dot(unit_key * grad_key, same))
    ).astype(LOW)
    grad_qkv_ref[0, :, 256:] = jnp.where(even, value_sum[0], value_sum[1]).astype(LOW)


def attend_back(qkv, extra, key_mask, out, grad, roots, gain, first, pairs):
    items, length, _ = qkv.shape
    block = pl.BlockSpec((1, length, 128), lambda i, p: (i, 0, p + first))
    table = pl.BlockSpec((length, 128), lambda i, p: (0, 0))
    return pl.pallas_call(
        attend_back_kernel,
        grid=(items, pairs),
        in_specs=[pl.BlockSpec((1, length, 384), lambda i, p: (i, 0, p + first))]
        + [block, table, block, block, block, pl.BlockSpec((1, 128), lambda i, p: (0, p + first))],
        out_specs=[
            pl.BlockSpec((1, length, 384), lambda i, p: (i, 0, p)),
            pl.BlockSpec((1, 1, 128), lambda i, p: (i, 0, p)),
        ],
        out_shape=[
            jax.ShapeDtypeStruct((items, length, 384 * pairs), LOW),
            jax.ShapeDtypeStruct((items, 1, 128 * pairs), WIDE),
        ],
        scratch_shapes=[
            pltpu.VMEM((2, length, 128), WIDE),
            pltpu.VMEM((2, length, 128), WIDE),
            pltpu.VMEM((length, 128), WIDE),
        ],
        compiler_params=pltpu.CompilerParams(vmem_limit_bytes=24 << 20),
        cost_estimate=LIGHT,
        name="attend_back",
    )(far(qkv), far(extra), key_mask, far(out), far(grad), far(roots), gain)


def row_facts(lengths_ref, block_rows, length):
    row = pl.program_id(0) * block_rows + lax.broadcasted_iota(jnp.int32, (block_rows, 1), 0)
    second = row >= length
    end = jnp.where(second, length + lengths_ref[1], lengths_ref[0])
    return second, row < end


def per_row(ref, second):
    return jnp.where(second, ref[1:2, :], ref[0:1, :])


def add_sums(ref, second, values):
    count = values[0].shape[0]
    flags = pl.program_id(0) * count
    half = count * pl.num_programs(0) // 2
    split = (flags < half) & (flags + count > half)

    @pl.when(jnp.logical_not(split))
    def _():
        for number, value in enumerate(values):
            row = 2 * number + jnp.where(flags >= half, 1, 0)
            ref[pl.ds(row, 1), :] += jnp.sum(value, 0, keepdims=True)

    @pl.when(split)
    def _():
        for number, value in enumerate(values):
            later = jnp.sum(jnp.where(second, value, 0.0), 0, keepdims=True)
            ref[2 * number : 2 * number + 1, :] += jnp.sum(value, 0, keepdims=True) - later
            ref[2 * number + 1 : 2 * number + 2, :] += later


def normalize(values):
    centred = values - jnp.mean(values, -1, keepdims=True)
    scale = lax.rsqrt(jnp.mean(centred * centred, -1, keepdims=True) + EPS)
    return centred * scale, scale


def token_call(kernel, place, rows, length, lengths, blocked, full, weights, outs, sums, name):
    block_rows = 2 * length // 5
    grid = rows // block_rows
    parts, where = [], []
    for pieces, sources, _ in weights:
        start = len(parts)
        parts.extend(pieces)
        where.append((start, len(pieces), sources))
    shapes = [weight[2] for weight in weights]
    counts = [1 if count == 1 else 32 * len(sources) for _, count, sources in where]
    blocked_count, full_count, out_count, weight_count = len(blocked), len(full), len(outs), len(weights)

    def body(place_ref, lengths_ref, *refs):
        cursor = 0

        def take(count):
            nonlocal cursor
            cursor += count
            return refs[cursor - count : cursor]

        token_refs, full_refs, part_refs = take(blocked_count), take(full_count), take(len(parts))
        out_refs, sum_refs = take(out_count), take(sums)
        buffers, sems = take(weight_count), take(weight_count)
        first = pl.program_id(0) == 0

        def copies(number):
            start, count, sources = where[number]
            return weight_copies(
                place_ref, part_refs[start : start + count], sources, buffers[number], sems[number]
            )

        @pl.when(first)
        def _():
            for number in range(weight_count):
                for copy in copies(number):
                    copy.start()
            for ref in sum_refs:
                ref[...] = jnp.zeros_like(ref)

        def ready(number):
            @pl.when(first)
            def _():
                for copy in copies(number):
                    copy.wait()

            return buffers[number]

        second, real = row_facts(lengths_ref, block_rows, length)
        kernel(second, real, token_refs, full_refs, ready, out_refs, sum_refs)

    any_space = pl.BlockSpec(memory_space=pl.ANY)
    smem = pl.BlockSpec(memory_space=pltpu.SMEM)
    return pl.pallas_call(
        body,
        grid=(grid,),
        in_specs=[smem, smem]
        + [pl.BlockSpec((block_rows, v.shape[1]), lambda i: (i, 0)) for v in blocked]
        + [pl.BlockSpec(v.shape, lambda i: (0, 0)) for v in full]
        + [any_space] * len(parts),
        out_specs=[pl.BlockSpec((block_rows, width), lambda i: (i, 0)) for width, _ in outs]
        + [pl.BlockSpec((16, 1024), lambda i: (0, 0))] * sums,
        out_shape=[jax.ShapeDtypeStruct((rows, width), kind) for width, kind in outs]
        + [jax.ShapeDtypeStruct((16, 1024), WIDE)] * sums,
        scratch_shapes=[pltpu.VMEM(shape, LOW) for shape in shapes]
        + [pltpu.SemaphoreType.DMA((count,)) for count in counts],
        compiler_params=pltpu.CompilerParams(vmem_limit_bytes=VMEM_LIMIT),
        cost_estimate=LIGHT,
        name=name,
    )(place.table, lengths, *map(far, blocked), *full, *parts)


def project_kernel(second, real, tokens, full, ready, outs, sums):
    (x_ref,) = tokens
    scale, shift, gain = full
    h_ref, qkv_ref, root_ref = outs
    unit, _ = normalize(x_ref[...].astype(WIDE))
    hidden = (unit * (1.0 + per_row(scale, second)) + per_row(shift, second)).astype(LOW)
    h_ref[...] = hidden
    same = side_table(False, 256)
    first_half = (lax.broadcasted_iota(jnp.int32, (hidden.shape[0], 128), 1) & 32) == 0
    weight = ready(0)
    for pair in range(weight.shape[1] // 384):
        start = 384 * pair
        raw = dot(hidden, weight[:, start : start + 384])
        both = raw[:, :256]
        root = lax.rsqrt(dot((both * both).astype(LOW), same) + EPS)
        root_ref[:, 128 * pair : 128 * pair + 128] = jnp.where(
            first_half, root[:, :128], root[:, 128:]
        ).astype(LOW)
        query = raw[:, :128] * (root[:, :128] * gain[:, 128 * pair : 128 * pair + 128])
        qkv_ref[:, start : start + 128] = query.astype(LOW)
        qkv_ref[:, start + 128 : start + 256] = (raw[:, 128:256] * root[:, 128:]).astype(LOW)
        qkv_ref[:, start + 256 : start + 384] = raw[:, 256:].astype(LOW)


def block_kernel(second, real, tokens, full, ready, outs, sums):
    attended_ref, x_ref, cot_ref = tokens
    gamma_one_ref, gamma_two_ref, scale_ref, shift_ref = full
    out_ref, h_ref, act_ref, mlp_grad_ref, hidden_grad_ref, middle_ref, attn_grad_ref, attended_grad_ref = outs
    (sum_ref,) = sums
    gate_one, gate_two = per_row(gamma_one_ref, second), per_row(gamma_two_ref, second)
    scale = 1.0 + per_row(scale_ref, second)
    upstream = cot_ref[...].astype(WIDE)
    mlp_grad = jnp.where(real, gate_two * upstream, 0.0).astype(LOW)
    mlp_grad_ref[...] = mlp_grad
    proj = ready(0)
    attn = dot(attended_ref[...], proj[...])
    branch_one = jnp.where(real, gate_one * attn, 0.0)
    middle = x_ref[...].astype(WIDE) + branch_one
    unit, root = normalize(middle)
    hidden = (unit * scale + per_row(shift_ref, second)).astype(LOW)
    h_ref[...] = hidden
    mlp, grad = 0.0, 0.0
    width = 1024
    fc1, fc2 = ready(1), ready(2)
    for start in range(0, fc1.shape[1], width):
        span = slice(start, start + width)
        wide = dot(hidden, fc1[:, span])
        act_grad = dot(mlp_grad, fc2[span, :], NT)
        square = wide * wide
        lift = 0.5 + 0.5 * jnp.tanh(wide * (GELU_COEF + (GELU_COEF * 0.044715) * square))
        act = (wide * lift).astype(LOW)
        act_ref[:, span] = act
        bend = wide * (2.0 * GELU_COEF + (6.0 * 0.044715 * GELU_COEF) * square)
        hidden_grad = (act_grad * (lift * (1.0 + bend * (1.0 - lift)))).astype(LOW)
        hidden_grad_ref[:, span] = hidden_grad
        mlp = mlp + dot(act, fc2[span, :])
        grad = grad + dot(hidden_grad, fc1[:, span], NT)
    branch_two = jnp.where(real, gate_two * mlp, 0.0)
    stream = middle + branch_two
    out_ref[...] = stream.astype(LOW)
    scaled = grad * scale
    middle_grad = upstream + root * (
        scaled - jnp.mean(scaled, -1, keepdims=True) - unit * jnp.mean(scaled * unit, -1, keepdims=True)
    )
    middle_ref[...] = middle_grad.astype(LOW)
    attn_grad = jnp.where(real, gate_one * middle_grad, 0.0).astype(LOW)
    attn_grad_ref[...] = attn_grad
    attended_grad_ref[...] = dot(attn_grad, proj[...], NT).astype(LOW)
    add_sums(
        sum_ref,
        second,
        [
            jnp.where(real, stream * stream, 0.0),
            branch_one * branch_one,
            branch_two * branch_two,
            jnp.where(real, mlp * upstream, 0.0),
            jnp.where(real, attn * middle_grad, 0.0),
            grad * unit,
            grad,
        ],
    )


def token_back_kernel(second, real, tokens, full, ready, outs, sums):
    *grad_refs, x_ref, middle_ref = tokens
    (scale,) = full
    (out_ref,) = outs
    (sum_ref,) = sums
    weight = ready(0)
    grad, column = 0.0, 0
    for ref in grad_refs:
        grad = grad + dot(ref[...], weight[:, column : column + ref.shape[1]], NT)
        column += ref.shape[1]
    unit, root = normalize(x_ref[...].astype(WIDE))
    add_sums(sum_ref, second, [grad * unit, grad])
    scaled = grad * (1.0 + per_row(scale, second))
    total = middle_ref[...].astype(WIDE) + root * (
        scaled - jnp.mean(scaled, -1, keepdims=True) - unit * jnp.mean(scaled * unit, -1, keepdims=True)
    )
    out_ref[...] = total.astype(LOW)


def outer_kernel(half_ref, left_ref, right_ref, out_ref):
    out_ref[...] = dot(left_ref[...], right_ref[...], TN).astype(LOW)


def outer(left, right, half):
    count, height = left.shape
    width = right.shape[1] // 2
    tall = min(height, 1024)
    wide = min(width, 1024 if width % 1024 == 0 else 768 if width % 768 == 0 else 512)
    steps = width // wide
    return pl.pallas_call(
        outer_kernel,
        grid_spec=pltpu.PrefetchScalarGridSpec(
            num_scalar_prefetch=1,
            grid=(height // tall, steps),
            in_specs=[
                pl.BlockSpec((count, tall), lambda i, j, h: (0, i)),
                pl.BlockSpec((count, wide), lambda i, j, h: (0, h[0] * steps + j)),
            ],
            out_specs=pl.BlockSpec((tall, wide), lambda i, j, h: (i, j)),
        ),
        out_shape=jax.ShapeDtypeStruct((height, width), LOW),
        compiler_params=pltpu.CompilerParams(vmem_limit_bytes=28 << 20),
        cost_estimate=LIGHT,
        name="outer",
    )(half.reshape(1).astype(jnp.int32), far(left), far(right))


def outer_joint(left, rights, other_left, other_right, half):
    count, height = left.shape
    rights = [*rights, other_right]
    widths = [right.shape[1] // 4 for right in rights]
    total = sum(widths)
    whole = lambda v: pl.BlockSpec(v.shape, lambda j, h: (0, 0))
    part = lambda width: pl.BlockSpec((count, width), lambda j, h: (0, 2 * h[0] + j))

    def body(half_ref, left_ref, other_ref, *refs):
        *right_refs, out_ref = refs
        column = 0
        for number, (ref, width) in enumerate(zip(right_refs, widths)):
            source = other_ref if number == len(widths) - 1 else left_ref
            out_ref[:, column : column + width] = dot(source[...], ref[...], TN).astype(LOW)
            column += width

    return pl.pallas_call(
        body,
        grid_spec=pltpu.PrefetchScalarGridSpec(
            num_scalar_prefetch=1,
            grid=(2,),
            in_specs=[whole(left), whole(other_left)] + [part(width) for width in widths],
            out_specs=pl.BlockSpec((height, total), lambda j, h: (0, j)),
        ),
        out_shape=jax.ShapeDtypeStruct((height, 2 * total), LOW),
        compiler_params=pltpu.CompilerParams(vmem_limit_bytes=40 << 20),
        cost_estimate=LIGHT,
        name="outer_joint",
    )(half.reshape(1).astype(jnp.int32), far(left), far(other_left), *map(far, rights))


def plain_sum(place, keep, send):
    flip = place.c == 1
    full = jnp.concatenate([jnp.where(flip, send, keep), jnp.where(flip, keep, send)], 1)
    part = lax.psum_scatter(full, "fsdp", scatter_dimension=0, tiled=True)
    return lax.psum(part, "dp").astype(WIDE)


def shards(place_counts, tokens, cond, stop_scale, w_ada, w_qkv, w_proj, w_fc1, w_fc2, head_log_scale, cotangent):
    place = Place(*place_counts)
    items, width = cond.shape
    rows = tokens.shape[0]
    length = rows // items
    heads = head_log_scale.shape[0]
    pairs = heads // 2
    hidden_width = w_fc1.shape[1]
    ends = jnp.asarray(np.cumsum([side * side for side in PATCHES]).astype(np.int32))
    lengths = jnp.sum(jnp.where(jnp.arange(len(PATCHES))[None, :] == stop_scale[:, None], ends[None, :], 0), 1)

    def by_pair(matrix):
        return jnp.swapaxes(matrix.reshape(matrix.shape[0], 3, pairs, 128), 1, 2).reshape(matrix.shape)

    def from_pair(matrix):
        return jnp.swapaxes(matrix.reshape(matrix.shape[0], pairs, 3, 128), 1, 2).reshape(matrix.shape)

    paired = by_pair(w_qkv)
    half = paired.shape[1] // 2
    cond_wide = cond.astype(WIDE)
    silu_cond = (cond_wide * jax.nn.sigmoid(cond_wide)).astype(LOW)
    ada_rows = w_ada.shape[0]
    group_count = items * place.fsdp_count
    ada_columns = (0, place.fsdp_index * ada_rows)

    def part_modulation(group_cond):
        return dot(lax.dynamic_slice(group_cond, ada_columns, (group_count, ada_rows)), w_ada)

    if place.grouped:
        unit_rows = w_qkv.shape[0]
        cond_stack = small_over_z(silu_cond)
        own_qkv, cond_stack = tie(own_quarter(place, paired), cond_stack)
        qkv = Gather(own_qkv)
        qkv.over_z()
        mixed = scatter_over_x(place, part_modulation(small_over_x(place, cond_stack)))
        qkv.stack, mixed = tie(qkv.stack, mixed)
        qkv.over_xy()
        modulation = scatter_over_z(place, mixed)
        own_rest = jnp.concatenate([own_quarter(place, w_proj), own_quarter(place, w_fc1)], 1)
        own_rest, modulation = tie(own_rest, modulation)
        rest = Gather(own_rest)
        rest.over_z()
        qkv.over_both()
        qkv.over_core_first()
        rest.stack, *qkv.from_both = tie(rest.stack, *qkv.from_both)
        rest.over_xy()
        qkv_parts = qkv.over_core()
        piece = w_fc2.shape[0] // place.dp_count
        fc2_piece = lax.dynamic_slice(w_fc2, (place.dp_index * piece, 0), (piece, width))
        fc2_piece, qkv_parts[-1] = tie(fc2_piece, qkv_parts[-1])
        fc2_full = lax.all_gather(fc2_piece, ("fsdp", "dp"), axis=0, tiled=True)
        quarter = half // 2
        qkv_weight = (qkv_parts, [(0, quarter, unit_rows, 0)], (width, 2 * half))
        fc2_weight = ([fc2_full], 0, (hidden_width, width))
    else:
        qkv_weight, proj_weight, fc1_weight, fc2_weight = (
            ([lax.all_gather(w, "fsdp", axis=0, tiled=True)], 0, (w.shape[0] * place.fsdp_count, w.shape[1]))
            for w in (paired, w_proj, w_fc1, w_fc2)
        )
        modulation = lax.psum_scatter(
            part_modulation(gather_small(place, silu_cond, False)), "fsdp", scatter_dimension=0, tiled=True
        )
    gamma_one, gamma_two, scale_one, scale_two, shift_one, shift_two = [
        modulation[:, n * width : (n + 1) * width] for n in range(6)
    ]

    gain = jnp.repeat(jnp.exp(head_log_scale), width // heads)[None, :]
    normed_one, projected, roots = token_call(
        project_kernel, place, rows, length, lengths, [tokens], [scale_one, shift_one, gain],
        [qkv_weight], [(width, LOW), (3 * width, LOW), (width, LOW)], 0, "project",
    )
    if place.grouped:
        rest.from_x, rest.from_y, projected = tie(rest.from_x, rest.from_y, projected)
        rest.over_both()
        rest.over_core_first()
    cube = (items, length, width)
    projected, roots = projected.reshape(items, length, 3 * width), roots.reshape(cube)
    query_mask, key_mask = mask_tables(length)
    attended, extra = attend(projected, query_mask, key_mask)
    if place.grouped:
        attended, *rest.from_both = tie(attended, *rest.from_both)
        rest_parts = rest.over_core()
        proj_weight = (rest_parts, [(0, width // 4, unit_rows, 0)], (width, width))
        fc1_weight = (
            rest_parts, [(width // 4, hidden_width // 4, unit_rows, 0)], (width, hidden_width)
        )
    flat_attended = attended.reshape(rows, width)
    (
        result, normed_two, act, grad_mlp, grad_hidden, grad_middle, grad_attn, grad_attended, sum_one,
    ) = token_call(
        block_kernel, place, rows, length, lengths, [flat_attended, tokens, cotangent],
        [gamma_one, gamma_two, scale_two, shift_two], [proj_weight, fc1_weight, fc2_weight],
        [(width, LOW), (width, LOW), (hidden_width, LOW), (width, LOW), (hidden_width, LOW)]
        + [(width, LOW)] * 3, 1, "block",
    )

    def small_group(sum_four):
        head_terms = jnp.concatenate([heads_first, heads_second], 2).reshape(items, heads, width // heads).sum(2)
        head_parts = jnp.concatenate([*two_parts(head_terms), jnp.zeros((items, 128 - 2 * heads), LOW)], 1)
        grad_modulation = jnp.concatenate(
            [sum_one[8:10], sum_one[6:8], sum_four[0:2], sum_one[10:12], sum_four[2:4], sum_one[12:14]], 1
        ).astype(LOW)
        return jnp.concatenate([grad_modulation, head_parts, silu_cond], 1)

    def send_part(left, right):
        return outer(left, right, 1 - place.c)

    def keep_part(left, right):
        return outer(left, right, place.c)

    def heads_back(grad, first):
        out, sums = attend_back(
            projected, extra, key_mask, attended, grad.reshape(cube), roots, gain, first, pairs // 2
        )
        return out.reshape(rows, half), sums

    def token_back(first, second):
        return token_call(
            token_back_kernel, place, rows, length, lengths, [first, second, tokens, grad_middle],
            [scale_one], [qkv_weight], [(width, LOW)], 1, "token_back",
        )

    if place.grouped:
        quarter = width // 4
        fc2_send = send_part(act, grad_mlp)
        fc2_keep, arrived = beside(lambda g: keep_part(act, g), grad_mlp, [(fc2_send, {"dc": 1})])
        fc2 = RowSum(fc2_keep, arrived[0], w_fc2.shape[0], "mixed")
        (sums,) = add_blocks(place, [fc2.first()], "sums_a")

        (grad_first, heads_first), arrived = beside(
            lambda g: heads_back(g, 0), grad_attended, fc2.moves(sums)
        )
        (sums,) = add_blocks(place, [fc2.second(arrived)], "sums_b")

        fc1_send, fc2_arrived = beside(
            lambda g: send_part(normed_two, g), tie(grad_hidden, grad_first)[0], fc2.moves(sums)
        )
        fc1_keep, arrived = beside(lambda g: keep_part(normed_two, g), grad_hidden, [(fc1_send, {"dc": 1})])
        fc1 = RowSum(fc1_keep, arrived[0], unit_rows, "mixed")
        fc1_sums, fc2_sums = add_blocks(place, [fc1.first(), fc2.third(fc2_arrived)], "sums_c")

        (grad_second, heads_second), arrived = beside(
            lambda g: heads_back(g, pairs // 2), grad_attended, fc1.moves(fc1_sums) + fc2.moves(fc2_sums)
        )
        fc1_sums, (fc2_own,) = add_blocks(
            place, [fc1.second(arrived[:2]), fc2.last(arrived[2:])], "sums_d"
        )
        joint = functools.partial(outer_joint, normed_one, [grad_first, grad_second], flat_attended)
        last_send, (*fc1_arrived, fc2_y, fc2_c) = beside(
            lambda g: joint(g, 1 - place.c),
            tie(grad_attn, grad_second)[0],
            fc1.moves(fc1_sums) + [(fc2_own, {"dy": 1}), (fc2_own, {"dc": 1})],
        )
        last_keep, (arrived, fc2_both) = beside(
            lambda g: joint(g, place.c), grad_attn, [(last_send, {"dc": 1}), (fc2_y, {"dc": 1})]
        )
        last = RowSum(last_keep, arrived, unit_rows, "mixed")
        fc1_sums, last_sums = add_blocks(place, [fc1.third(fc1_arrived), last.first()], "sums_e")

        (grad_tokens, sum_four), arrived = beside(
            lambda g: token_back(grad_first, g), grad_second, last.moves(last_sums) + fc1.moves(fc1_sums)
        )
        last_sums, (fc1_own,) = add_blocks(place, [last.second(arrived[:2]), fc1.last(arrived[2:])], "sums_f")
        group = small_group(sum_four)
        moves = last.moves(last_sums)
        sent, group = tie(tuple(v for v, _ in moves), group)
        arrived = [hop(v, **axes) for v, (_, axes) in zip(sent, moves)]
        group_stack = small_over_z(group)
        arrived, group_stack = tie(arrived, group_stack)
        (last_sums,) = add_blocks(place, [last.third(arrived)], "sums_g")
        sent, group_stack = tie(tuple(last_sums), group_stack)
        arrived = [hop(v, **axes) for v, axes in last.moves(sent)]
        group = small_over_x(place, group_stack)
        fc1_y = hop(fc1_own, dy=1)
        ((last_own,),) = add_blocks(place, [last.last(arrived)], "sums_h")
        last_all = spread(last_own)
        fc1_core = [hop(fc1_own, dc=1), hop(fc1_y, dc=1)]
        (grad_fc2,) = lay_out(
            place, [fc2_own, fc2_y, fc2_c, fc2_both], [[(0, 0, quarter, 0, 0, quarter)]], [w_fc2.shape],
            "lay_out_fc2",
        )
        wide = hidden_width // 4
        (grad_fc1,) = lay_out(
            place, [fc1_own, fc1_y] + fc1_core, [[(0, 0, wide, 0, 0, wide)]], [w_fc1.shape], "lay_out_fc1"
        )
        layout = [
            (0, 384 * side + 128 * n, 128, 0, n * width + 512 * side, 128) for side in range(2) for n in range(3)
        ]
        layout.append((1, 768, quarter, 0, 0, quarter))
        grad_qkv, grad_proj = lay_out(
            place, last_all, [layout], [w_qkv.shape, w_proj.shape], "lay_out_last"
        )
    else:
        def whole_sum(left, right):
            return plain_sum(place, keep_part(left, right), send_part(left, right))

        grad_fc2 = whole_sum(act, grad_mlp)
        grad_fc1 = whole_sum(normed_two, grad_hidden)
        grad_proj = whole_sum(flat_attended, grad_attn)
        grad_first, heads_first = heads_back(grad_attended, 0)
        grad_second, heads_second = heads_back(grad_attended, pairs // 2)
        grad_qkv = from_pair(
            jnp.concatenate([whole_sum(normed_one, grad_first), whole_sum(normed_one, grad_second)], 1)
        )
        grad_tokens, sum_four = token_back(grad_first, grad_second)
        group = gather_small(place, small_group(sum_four), False)

    grad_columns = dot(group[:, : 6 * width], w_ada, NT)
    everything = over_dp(place, group)
    all_heads = everything[:, 6 * width : 6 * width + 2 * heads].astype(WIDE)
    grad_head = jnp.sum(all_heads[:, :heads] + all_heads[:, heads:], 0)
    all_slice = lax.dynamic_slice(
        everything, (0, 6 * width + 128 + place.fsdp_index * ada_rows), (everything.shape[0], ada_rows)
    )
    grad_ada = dot(all_slice, everything[:, : 6 * width], TN)
    grad_parts = gather_small(place, grad_columns[None], False)
    own_items = lax.dynamic_slice(
        grad_parts, (0, place.fsdp_index * items, 0), (grad_parts.shape[0], items, ada_rows)
    )
    grad_silu = jnp.swapaxes(own_items, 0, 1).reshape(items, width)
    gate = jax.nn.sigmoid(cond_wide)
    grad_cond = (grad_silu * gate * (1.0 + cond_wide * (1.0 - gate))).astype(LOW)

    counted = (lengths * width).astype(WIDE)
    squares = jnp.stack(
        [sum_one[0:2].sum(1), sum_one[2:4].sum(1), sum_one[4:6].sum(1)], 1
    )
    rms_rows = jnp.sqrt(squares / counted[:, None] + EPS)
    return (
        result, grad_tokens, grad_cond, grad_ada, grad_qkv, grad_proj, grad_fc1, grad_fc2,
        grad_head, rms_rows,
    )


def solution(mesh):
    both = P(("dp", "fsdp"), None)
    rows = P("fsdp", None)
    return jax.shard_map(
        functools.partial(shards, (mesh.shape["dp"], mesh.shape["fsdp"])),
        mesh=mesh,
        in_specs=(both, both, P(("dp", "fsdp")), rows, rows, rows, rows, rows, P(), both),
        out_specs=(both, both, both, rows, rows, rows, rows, rows, P(), both),
        check_vma=False,
    )
```

```python
import functools

import jax
import jax.numpy as jnp
import numpy as np
from jax import lax
from jax.experimental import pallas as pl
from jax.experimental.pallas import tpu as pltpu
from jax.sharding import PartitionSpec as P

PATCHES = (1, 2, 3, 4, 5, 6, 8, 10, 13, 16)
EPS = 1e-06
GELU_COEF = 0.7978845608028654
AXES = ("dp", "fsdp")
LOW = jnp.bfloat16
WIDE = jnp.float32
NN = (((1,), (0,)), ((), ()))
NT = (((1,), (1,)), ((), ()))
TN = (((0,), (0,)), ((), ()))
VMEM_LIMIT = 56 << 20
BLOCKED = -30000.0
LIGHT = pl.CostEstimate(flops=1024, transcendentals=0, bytes_accessed=1024)


def dot(left, right, dims=NN):
    return lax.dot_general(left, right, dims, preferred_element_type=WIDE)


def far(values):
    return pltpu.with_memory_space_constraint(values, pltpu.HBM)


def two_parts(values):
    high = values.astype(LOW)
    return high, (values - high.astype(WIDE)).astype(LOW)


class Place:
    def __init__(self, dp_count, fsdp_count):
        self.grouped = dp_count == 4 and fsdp_count == 8
        self.dp_count = dp_count
        self.fsdp_count = fsdp_count
        dp_index = lax.axis_index("dp")
        fsdp_index = lax.axis_index("fsdp")
        self.dp_index, self.fsdp_index = dp_index, fsdp_index
        self.y, self.c = dp_index // 2, dp_index % 2
        self.z, self.x = fsdp_index // 2, fsdp_index % 2
        self.table = jnp.stack([self.y, self.c, self.z, self.x]).astype(jnp.int32)


def hop(values, dy=0, dc=0, dz=0, dx=0):
    pairs = [
        (d * 8 + f, (d ^ (2 * dy + dc)) * 8 + (f ^ (2 * dz + dx)))
        for d in range(4)
        for f in range(8)
    ]
    return lax.ppermute(values, AXES, pairs)


def tie(*values):
    return lax.optimization_barrier(values)


class Gather:
    def __init__(self, own):
        self.own = own

    def over_z(self):
        self.stack = jnp.concatenate([self.own] + [hop(self.own, dz=k) for k in (1, 2, 3)], 0)

    def over_xy(self):
        self.from_x, self.from_y = hop(self.stack, dx=1), hop(self.stack, dy=1)

    def over_both(self):
        half = self.stack.shape[0] // 2
        self.from_both = [hop(self.from_x[:half], dy=1), hop(self.from_y[half:], dx=1)]

    def over_core_first(self):
        self.first = [self.stack, self.from_x, self.from_y]
        self.first_core = [hop(piece, dc=1) for piece in self.first]

    def over_core(self):
        self.last_core = [hop(piece, dc=1) for piece in self.from_both]
        return self.first + self.from_both + self.first_core + self.last_core


def own_quarter(place, shard):
    rows, columns = shard.shape
    quarter = columns // 4
    return lax.dynamic_slice(shard, (0, (place.c * 2 + place.y) * quarter), (rows, quarter))


def weight_copies(place_ref, pieces, sources, buffer, sem):
    copies = []
    if len(pieces) == 1:
        window = pieces[0].at[:, pl.ds(sources, buffer.shape[1])]
        return [pltpu.make_async_copy(window, buffer, sem.at[0])]
    for column_from, quarter, rows, column_to in sources:
        for number in range(10):
            core, kind = number // 5, number % 5
            across, side = (0, 1, 0, 1, 1)[kind], (0, 0, 1, 1, 1)[kind]
            column = column_to + ((place_ref[1] ^ core) * 2 + (place_ref[0] ^ side)) * quarter
            members = range(4) if kind < 3 else range(2 * (kind - 3), 2 * (kind - 3) + 2)
            for place_in, k in enumerate(members):
                row = ((place_ref[2] ^ k) * 2 + (place_ref[3] ^ across)) * rows
                copies.append(
                    pltpu.make_async_copy(
                        pieces[number].at[pl.ds(place_in * rows, rows), pl.ds(column_from, quarter)],
                        buffer.at[
                            pl.ds(pl.multiple_of(row, 128), rows),
                            pl.ds(pl.multiple_of(column, 128), quarter),
                        ],
                        sem.at[len(copies)],
                    )
                )
    return copies


def add(left, right):
    return left.astype(WIDE) + right.astype(WIDE)


def add_blocks(place, jobs, name):
    arrays, in_specs, out_specs, out_shapes, plan = [], [], [], [], []

    def block_spec(block, where, steps):
        return pl.BlockSpec(block, lambda n, p: where(jnp.minimum(n, steps - 1), p))

    for steps, outs in jobs:
        for blocks, block, where_out, terms in outs:
            entry = []
            for array, where, when in terms:
                entry.append((len(arrays), when))
                arrays.append(array)
                in_specs.append(block_spec(block, where, steps))
            out_specs.append(block_spec(block, where_out, steps))
            out_shapes.append(jax.ShapeDtypeStruct((blocks[0] * block[0], blocks[1] * block[1]), LOW))
            plan.append((steps, entry))

    def body(place_ref, *refs):
        step = pl.program_id(0)
        for (steps, entry), out_ref in zip(plan, refs[len(arrays) :]):

            @pl.when(step < steps)
            def _():
                total = None
                for number, when in entry:
                    value = refs[number][...].astype(WIDE)
                    if when is not None:
                        value = jnp.where(when(step, place_ref), value, 0.0)
                    total = value if total is None else total + value
                out_ref[...] = total.astype(LOW)

    results = pl.pallas_call(
        body,
        grid_spec=pltpu.PrefetchScalarGridSpec(
            num_scalar_prefetch=1,
            grid=(max(steps for steps, _ in jobs),),
            in_specs=in_specs,
            out_specs=out_specs,
        ),
        out_shape=out_shapes,
        compiler_params=pltpu.CompilerParams(vmem_limit_bytes=20 << 20),
        cost_estimate=LIGHT,
        name=name,
    )(place.table, *arrays)
    grouped, cursor = [], 0
    for _, outs in jobs:
        grouped.append(list(results[cursor : cursor + len(outs)]))
        cursor += len(outs)
    return grouped


class RowSum:
    def __init__(self, keep, arrived, rows, order):
        self.base = [keep, arrived]
        self.rest = [far(keep), far(arrived)]
        self.rows, self.width = rows, keep.shape[1] // 2
        self.streams = (
            [{"z": 0, "count": 2, "order": "yx"}, {"z": 2, "count": 2, "order": "xy"}]
            if order == "mixed"
            else [{"z": 0, "count": 4, "order": order}]
        )

    def first(self):
        outs = []
        for stream in self.streams:
            start, count = stream["z"], stream["count"]
            if stream["order"] == "yx":
                block, blocks = (count * self.rows, self.width), (2, 1)
                where = lambda n, p: (jnp.minimum(n, 1), 1 - p[0])
                out = lambda n, p: (jnp.minimum(n, 1), 0)
            else:
                block, blocks = (self.rows, 2 * self.width), (count, 1)
                where = lambda n, p, start=start: (2 * (start + n) + 1 - p[3], 0)
                out = lambda n, p: (n, 0)
            outs.append((blocks, block, out, [(t, where, None) for t in self.base]))
        steps = 2 if self.streams[0]["order"] == "yx" else self.streams[0]["count"]
        self.axes = [{"d" + stream["order"][0]: 1} for stream in self.streams]
        return steps, outs

    def second(self, arrived):
        block = (self.rows, self.width)
        outs, steps = [], self.streams[0]["count"]
        for stream, value in zip(self.streams, arrived):
            stream["first"] = value
            start, count = stream["z"], stream["count"]
            if stream["order"] == "yx":
                where = lambda n, p, start=start: (2 * (start + n) + 1 - p[3], p[0])
                terms = [(value, lambda n, p: (2 * n + 1 - p[3], 0), None)]
            else:
                where = lambda n, p, start=start: (2 * (start + n) + p[3], 1 - p[0])
                terms = [(value, lambda n, p: (n, 1 - p[0]), None)]
            outs.append(
                ((count, 1), block, lambda n, p: (n, 0), [(t, where, None) for t in self.rest] + terms)
            )
        self.axes = [{"d" + stream["order"][1]: 1} for stream in self.streams]
        return steps, outs

    def terms(self, flip):
        out = [(t, lambda n, p: (2 * (p[2] ^ flip) + p[3], p[0]), None) for t in self.rest]
        for stream in self.streams:
            mask = stream["count"] - 1
            when = None
            if stream["count"] == 2:
                when = lambda n, p, start=stream["z"]: (p[2] ^ flip) // 2 == start // 2
            if stream["order"] == "yx":
                first = lambda n, p, mask=mask: (2 * ((p[2] ^ flip) & mask) + p[3], 0)
            else:
                first = lambda n, p, mask=mask: ((p[2] ^ flip) & mask, p[0])
            out.append((stream["first"], first, when))
            out.append((stream["second"], lambda n, p, mask=mask: ((p[2] ^ flip) & mask, 0), when))
        return out

    def third(self, arrived):
        for stream, value in zip(self.streams, arrived):
            stream["second"] = value
        self.axes = [{"dz": k} for k in (1, 2, 3)]
        block = (self.rows, self.width)
        return 1, [((1, 1), block, lambda n, p: (0, 0), self.terms(k)) for k in (1, 2, 3)]

    def last(self, arrived):
        terms = self.terms(0) + [(v, lambda n, p: (0, 0), None) for v in arrived]
        return 1, [((1, 1), (self.rows, self.width), lambda n, p: (0, 0), terms)]

    def moves(self, sums):
        return list(zip(sums, self.axes))


def beside(kernel, operand, moves):
    out = tie(operand, *(value for value, _ in moves))
    arrived = [hop(value, **axes) for value, (_, axes) in zip(out[1:], moves)]
    results = kernel(out[0])
    results = list(results) if isinstance(results, (list, tuple)) else [results]
    out = tie(*results, *arrived)
    results, arrived = list(out[: len(results)]), list(out[len(results) :])
    return (results[0] if len(results) == 1 else results), arrived


def lay_out_kernel(layouts, place_ref, *refs):
    quarters, outs = refs[: 4 * len(layouts)], refs[4 * len(layouts) :]
    here = place_ref[1] * 2 + place_ref[0]
    for number, ref in enumerate(quarters):
        index = here ^ (number % 4)
        for number, column, width, row, to, stride in layouts[number // 4]:
            rows = ref.shape[0]
            start = pl.multiple_of(to + index * stride, 128)
            outs[number][pl.ds(row, rows), pl.ds(start, width)] = ref[:, column : column + width].astype(WIDE)


def lay_out(place, quarters, layouts, shapes, name):
    vmem = pl.BlockSpec(memory_space=pltpu.VMEM)
    return pl.pallas_call(
        functools.partial(lay_out_kernel, layouts),
        in_specs=[pl.BlockSpec(memory_space=pltpu.SMEM)] + [vmem] * len(quarters),
        out_specs=[vmem] * len(shapes),
        out_shape=[jax.ShapeDtypeStruct(shape, WIDE) for shape in shapes],
        compiler_params=pltpu.CompilerParams(vmem_limit_bytes=20 << 20),
        cost_estimate=LIGHT,
        name=name,
    )(place.table, *quarters)


def spread(own):
    return [own, hop(own, dy=1), hop(own, dc=1), hop(own, dy=1, dc=1)]


def reorder(stack, count, flip):
    return jnp.concatenate(
        [lax.dynamic_slice_in_dim(stack, i ^ flip, 1, axis=0) for i in range(count)], 0
    )


def small_over_z(values):
    return jnp.stack([values] + [hop(values, dz=k) for k in (1, 2, 3)])


def small_over_x(place, stack):
    count, tail = stack.shape[1], stack.shape[2:]
    stack = jnp.stack([stack, hop(stack, dx=1)], 1).reshape((8, count) + tail)
    return reorder(stack, 8, place.fsdp_index).reshape((8 * count,) + tail)


def gather_small(place, values, whole):
    if not place.grouped:
        return lax.all_gather(values, AXES if whole else "fsdp", axis=0, tiled=True)
    ordered = small_over_x(place, small_over_z(values))
    return over_dp(place, ordered) if whole else ordered


def over_dp(place, values):
    if not place.grouped:
        return lax.all_gather(values, "dp", axis=0, tiled=True)
    stack = jnp.stack([values, hop(values, dc=1), hop(values, dy=1), hop(values, dy=1, dc=1)])
    return reorder(stack, 4, place.dp_index).reshape((4 * values.shape[0],) + values.shape[1:])


def scatter_over_x(place, values):
    values = values.reshape((4, 2, values.shape[0] // 8) + values.shape[1:])
    mine = lax.dynamic_index_in_dim(values, place.x, 1, keepdims=False)
    other = lax.dynamic_index_in_dim(values, 1 - place.x, 1, keepdims=False)
    return mine + hop(other, dx=1)


def scatter_over_z(place, values):
    total = lax.dynamic_index_in_dim(values, place.z, 0, keepdims=False)
    for k in (1, 2, 3):
        total = total + hop(
            lax.dynamic_index_in_dim(values, place.z ^ k, 0, keepdims=False), dz=k
        )
    return total


def mask_tables(length):
    scale_ids = np.concatenate([np.full(side * side, i) for i, side in enumerate(PATCHES)])
    spare = np.arange(128) & 63
    slot = spare[None, :] - 2
    scale_column = scale_ids[:, None]
    later = (slot >= 0) & (slot < len(PATCHES)) & (slot > scale_column)
    query_side = np.where(later, BLOCKED, 0.0)
    key_side = np.where(slot == scale_column, 1.0, 0.0) + np.where(spare[None, :] < 2, 1.0, 0.0)
    return jnp.asarray(query_side, LOW), jnp.asarray(key_side, LOW)


FORWARD_BLOCKS = ((416, 680, 680), (0, 416, 512))
BACKWARD_BLOCKS = ((424, 680, 680), (0, 424, 432))


def attend_kernel(qkv_ref, qm_ref, km_ref, out_ref, extra_ref):
    query, key, value = (qkv_ref[0, :, 128 * n : 128 * n + 128] for n in range(3))
    query_mask, key_mask = qm_ref[...], km_ref[...]
    lane = lax.broadcasted_iota(jnp.int32, query.shape, 1)
    even = lane < 64
    ones = jnp.ones_like(value)
    heads = (
        (jnp.where(even, query, query_mask), jnp.where(even, key, key_mask), jnp.where(even, value, ones)),
        (jnp.where(even, query_mask, query), jnp.where(even, key_mask, key), jnp.where(even, ones, value)),
    )
    for start, stop, keys in FORWARD_BLOCKS:
        sums = []
        for query_head, key_head, value_head in heads:
            scores = dot(query_head[start:stop], key_head[:keys], NT)
            sums.append(dot(jnp.exp(scores).astype(LOW), value_head[:keys]))
        side = even[start:stop]
        chosen = jnp.where(side, sums[0], sums[1])
        totals = jnp.where(side, sums[1], sums[0])
        out_ref[0, start:stop, :] = (chosen / pltpu.roll(totals, 64, 1)).astype(LOW)
        high, rest = two_parts(-jnp.log(totals))
        spare = lane[start:stop] & 63
        extra_ref[0, start:stop, :] = jnp.where(
            spare == 0, high, jnp.where(spare == 1, rest, query_mask[start:stop])
        )


def attend(qkv, query_mask, key_mask):
    items, length, triple = qkv.shape
    pairs = triple // 384
    block = pl.BlockSpec((1, length, 128), lambda i, p: (i, 0, p))
    table = pl.BlockSpec((length, 128), lambda i, p: (0, 0))
    return pl.pallas_call(
        attend_kernel,
        grid=(items, pairs),
        in_specs=[pl.BlockSpec((1, length, 384), lambda i, p: (i, 0, p)), table, table],
        out_specs=[block, block],
        out_shape=[jax.ShapeDtypeStruct((items, length, 128 * pairs), LOW)] * 2,
        compiler_params=pltpu.CompilerParams(vmem_limit_bytes=24 << 20),
        cost_estimate=LIGHT,
        name="attend",
    )(far(qkv), query_mask, key_mask)


def side_table(cross, size=128):
    first = lax.broadcasted_iota(jnp.int32, (size, size), 0) // 64
    second = lax.broadcasted_iota(jnp.int32, (size, size), 1) // 64
    return jnp.where((first != second) if cross else (first == second), 1.0, 0.0).astype(LOW)


def attend_back_kernel(
    qkv_ref, extra_ref, km_ref, out_ref, grad_ref, root_ref, gain_ref,
    grad_qkv_ref, head_ref, value_sum, key_sum, query_sum,
):
    query, key, value = (qkv_ref[0, :, 128 * n : 128 * n + 128] for n in range(3))
    key_mask, grad, extra = km_ref[...], grad_ref[0], extra_ref[0]
    lane = lax.broadcasted_iota(jnp.int32, query.shape, 1)
    even = lane < 64
    spare = lane & 63
    centre = dot((grad.astype(WIDE) * out_ref[0].astype(WIDE)).astype(LOW), side_table(True))
    high, rest = two_parts(-centre)
    grad_extra = jnp.where(spare == 0, high, jnp.where(spare == 1, rest, jnp.zeros_like(high)))
    ones = jnp.ones_like(value)
    key_rows = key.astype(WIDE).T.astype(LOW)
    heads = (
        (jnp.where(even, query, extra), jnp.where(even, key, key_mask),
         jnp.where(even, value, ones), jnp.where(even, grad, grad_extra)),
        (jnp.where(even, extra, query), jnp.where(even, key_mask, key),
         jnp.where(even, ones, value), jnp.where(even, grad_extra, grad)),
    )
    for number, (start, stop, keys) in enumerate(BACKWARD_BLOCKS):
        for head, (query_head, key_head, value_head, grad_head) in enumerate(heads):
            head_rows = key_rows[64 * head : 64 * head + 64]
            probs = jnp.exp(dot(key_head[:keys], query_head[start:stop], NT))
            grad_probs = dot(value_head[:keys], grad_head[start:stop], NT)
            grad_scores = (probs * grad_probs).astype(LOW)
            value_part = dot(probs.astype(LOW), grad[start:stop])
            key_part = dot(grad_scores, query[start:stop])
            if number == 0:
                value_sum[head] = value_part
                key_sum[head] = key_part
            else:
                value_sum[head, :keys] += value_part
                key_sum[head, :keys] += key_part
            query_sum[start:stop, 64 * head : 64 * head + 64] = dot(head_rows[:, :keys], grad_scores).T
    row = lax.broadcasted_iota(jnp.int32, (128, 128), 0)
    wanted = jnp.where(lax.broadcasted_iota(jnp.int32, (128, 128), 1) >= 64, 64, 0)
    roots = root_ref[0]
    root_query = dot(roots, jnp.where(row == wanted, 1.0, 0.0).astype(LOW))
    root_key = dot(roots, jnp.where(row == wanted + 32, 1.0, 0.0).astype(LOW))
    same = side_table(False)
    gain = gain_ref[...]
    grad_query = query_sum[...] * gain
    unit_query = query.astype(WIDE) / gain
    product = unit_query * grad_query
    head_ref[0] = jnp.sum(product, 0, keepdims=True)
    grad_qkv_ref[0, :, :128] = (
        root_query * (grad_query - unit_query * dot(product.astype(LOW), same))
    ).astype(LOW)
    grad_key = jnp.where(even, key_sum[0], key_sum[1])
    unit_key = key.astype(WIDE)
    grad_qkv_ref[0, :, 128:256] = (
        root_key * (grad_key - unit_key * dot((unit_key * grad_key).astype(LOW), same))
    ).astype(LOW)
    grad_qkv_ref[0, :, 256:] = jnp.where(even, value_sum[0], value_sum[1]).astype(LOW)


def attend_back(qkv, extra, key_mask, out, grad, roots, gain, first, pairs):
    items, length, _ = qkv.shape
    block = pl.BlockSpec((1, length, 128), lambda i, p: (i, 0, p + first))
    table = pl.BlockSpec((length, 128), lambda i, p: (0, 0))
    return pl.pallas_call(
        attend_back_kernel,
        grid=(items, pairs),
        in_specs=[pl.BlockSpec((1, length, 384), lambda i, p: (i, 0, p + first))]
        + [block, table, block, block, block, pl.BlockSpec((1, 128), lambda i, p: (0, p + first))],
        out_specs=[
            pl.BlockSpec((1, length, 384), lambda i, p: (i, 0, p)),
            pl.BlockSpec((1, 1, 128), lambda i, p: (i, 0, p)),
        ],
        out_shape=[
            jax.ShapeDtypeStruct((items, length, 384 * pairs), LOW),
            jax.ShapeDtypeStruct((items, 1, 128 * pairs), WIDE),
        ],
        scratch_shapes=[
            pltpu.VMEM((2, length, 128), WIDE),
            pltpu.VMEM((2, length, 128), WIDE),
            pltpu.VMEM((length, 128), WIDE),
        ],
        compiler_params=pltpu.CompilerParams(vmem_limit_bytes=24 << 20),
        cost_estimate=LIGHT,
        name="attend_back",
    )(far(qkv), far(extra), key_mask, far(out), far(grad), far(roots), gain)


def row_facts(lengths_ref, block_rows, length):
    row = pl.program_id(0) * block_rows + lax.broadcasted_iota(jnp.int32, (block_rows, 1), 0)
    second = row >= length
    end = jnp.where(second, length + lengths_ref[1], lengths_ref[0])
    return second, row < end


def per_row(ref, second):
    return jnp.where(second, ref[1:2, :], ref[0:1, :])


def add_sums(ref, second, values):
    count = values[0].shape[0]
    flags = pl.program_id(0) * count
    half = count * pl.num_programs(0) // 2
    split = (flags < half) & (flags + count > half)

    @pl.when(jnp.logical_not(split))
    def _():
        for number, value in enumerate(values):
            row = 2 * number + jnp.where(flags >= half, 1, 0)
            ref[pl.ds(row, 1), :] += jnp.sum(value, 0, keepdims=True)

    @pl.when(split)
    def _():
        for number, value in enumerate(values):
            later = jnp.sum(jnp.where(second, value, 0.0), 0, keepdims=True)
            ref[2 * number : 2 * number + 1, :] += jnp.sum(value, 0, keepdims=True) - later
            ref[2 * number + 1 : 2 * number + 2, :] += later


def normalize(values):
    centred = values - jnp.mean(values, -1, keepdims=True)
    scale = lax.rsqrt(jnp.mean(centred * centred, -1, keepdims=True) + EPS)
    return centred * scale, scale


def token_call(kernel, place, rows, length, lengths, blocked, full, weights, outs, sums, name):
    block_rows = 2 * length // 5
    grid = rows // block_rows
    parts, where = [], []
    for pieces, sources, _ in weights:
        start = len(parts)
        parts.extend(pieces)
        where.append((start, len(pieces), sources))
    shapes = [weight[2] for weight in weights]
    counts = [1 if count == 1 else 32 * len(sources) for _, count, sources in where]
    blocked_count, full_count, out_count, weight_count = len(blocked), len(full), len(outs), len(weights)

    def body(place_ref, lengths_ref, *refs):
        cursor = 0

        def take(count):
            nonlocal cursor
            cursor += count
            return refs[cursor - count : cursor]

        token_refs, full_refs, part_refs = take(blocked_count), take(full_count), take(len(parts))
        out_refs, sum_refs = take(out_count), take(sums)
        buffers, sems = take(weight_count), take(weight_count)
        first = pl.program_id(0) == 0

        def copies(number):
            start, count, sources = where[number]
            return weight_copies(
                place_ref, part_refs[start : start + count], sources, buffers[number], sems[number]
            )

        @pl.when(first)
        def _():
            for number in range(weight_count):
                for copy in copies(number):
                    copy.start()
            for ref in sum_refs:
                ref[...] = jnp.zeros_like(ref)

        def ready(number):
            @pl.when(first)
            def _():
                for copy in copies(number):
                    copy.wait()

            return buffers[number]

        second, real = row_facts(lengths_ref, block_rows, length)
        kernel(second, real, token_refs, full_refs, ready, out_refs, sum_refs)

    any_space = pl.BlockSpec(memory_space=pl.ANY)
    smem = pl.BlockSpec(memory_space=pltpu.SMEM)
    return pl.pallas_call(
        body,
        grid=(grid,),
        in_specs=[smem, smem]
        + [pl.BlockSpec((block_rows, v.shape[1]), lambda i: (i, 0)) for v in blocked]
        + [pl.BlockSpec(v.shape, lambda i: (0, 0)) for v in full]
        + [any_space] * len(parts),
        out_specs=[pl.BlockSpec((block_rows, width), lambda i: (i, 0)) for width, _ in outs]
        + [pl.BlockSpec((16, 1024), lambda i: (0, 0))] * sums,
        out_shape=[jax.ShapeDtypeStruct((rows, width), kind) for width, kind in outs]
        + [jax.ShapeDtypeStruct((16, 1024), WIDE)] * sums,
        scratch_shapes=[pltpu.VMEM(shape, LOW) for shape in shapes]
        + [pltpu.SemaphoreType.DMA((count,)) for count in counts],
        compiler_params=pltpu.CompilerParams(vmem_limit_bytes=VMEM_LIMIT),
        cost_estimate=LIGHT,
        name=name,
    )(place.table, lengths, *map(far, blocked), *full, *parts)


def project_kernel(second, real, tokens, full, ready, outs, sums):
    (x_ref,) = tokens
    scale, shift, gain = full
    h_ref, qkv_ref, root_ref = outs
    unit, _ = normalize(x_ref[...].astype(WIDE))
    hidden = (unit * (1.0 + per_row(scale, second)) + per_row(shift, second)).astype(LOW)
    h_ref[...] = hidden
    same = side_table(False, 256)
    first_half = (lax.broadcasted_iota(jnp.int32, (hidden.shape[0], 128), 1) & 32) == 0
    weight = ready(0)
    for pair in range(weight.shape[1] // 384):
        start = 384 * pair
        raw = dot(hidden, weight[:, start : start + 384])
        both = raw[:, :256]
        root = lax.rsqrt(dot((both * both).astype(LOW), same) + EPS)
        root_ref[:, 128 * pair : 128 * pair + 128] = jnp.where(
            first_half, root[:, :128], root[:, 128:]
        ).astype(LOW)
        query = raw[:, :128] * (root[:, :128] * gain[:, 128 * pair : 128 * pair + 128])
        qkv_ref[:, start : start + 128] = query.astype(LOW)
        qkv_ref[:, start + 128 : start + 256] = (raw[:, 128:256] * root[:, 128:]).astype(LOW)
        qkv_ref[:, start + 256 : start + 384] = raw[:, 256:].astype(LOW)


def block_kernel(second, real, tokens, full, ready, outs, sums):
    attended_ref, x_ref, cot_ref = tokens
    gamma_one_ref, gamma_two_ref, scale_ref, shift_ref = full
    out_ref, h_ref, act_ref, mlp_grad_ref, hidden_grad_ref, middle_ref, attn_grad_ref, attended_grad_ref = outs
    (sum_ref,) = sums
    gate_one, gate_two = per_row(gamma_one_ref, second), per_row(gamma_two_ref, second)
    scale = 1.0 + per_row(scale_ref, second)
    upstream = cot_ref[...].astype(WIDE)
    mlp_grad = jnp.where(real, gate_two * upstream, 0.0).astype(LOW)
    mlp_grad_ref[...] = mlp_grad
    proj = ready(0)
    attn = dot(attended_ref[...], proj[...])
    branch_one = jnp.where(real, gate_one * attn, 0.0)
    middle = x_ref[...].astype(WIDE) + branch_one
    unit, root = normalize(middle)
    hidden = (unit * scale + per_row(shift_ref, second)).astype(LOW)
    h_ref[...] = hidden
    mlp, grad = 0.0, 0.0
    width = 1024
    fc1, fc2 = ready(1), ready(2)
    for start in range(0, fc1.shape[1], width):
        span = slice(start, start + width)
        wide = dot(hidden, fc1[:, span])
        act_grad = dot(mlp_grad, fc2[span, :], NT)
        square = wide * wide
        lift = 0.5 + 0.5 * jnp.tanh(wide * (GELU_COEF + (GELU_COEF * 0.044715) * square))
        act = (wide * lift).astype(LOW)
        act_ref[:, span] = act
        bend = wide * (2.0 * GELU_COEF + (6.0 * 0.044715 * GELU_COEF) * square)
        hidden_grad = (act_grad * (lift * (1.0 + bend * (1.0 - lift)))).astype(LOW)
        hidden_grad_ref[:, span] = hidden_grad
        mlp = mlp + dot(act, fc2[span, :])
        grad = grad + dot(hidden_grad, fc1[:, span], NT)
    branch_two = jnp.where(real, gate_two * mlp, 0.0)
    stream = middle + branch_two
    out_ref[...] = stream.astype(LOW)
    scaled = grad * scale
    middle_grad = upstream + root * (
        scaled - jnp.mean(scaled, -1, keepdims=True) - unit * jnp.mean(scaled * unit, -1, keepdims=True)
    )
    middle_ref[...] = middle_grad.astype(LOW)
    attn_grad = jnp.where(real, gate_one * middle_grad, 0.0).astype(LOW)
    attn_grad_ref[...] = attn_grad
    attended_grad_ref[...] = dot(attn_grad, proj[...], NT).astype(LOW)
    add_sums(
        sum_ref,
        second,
        [
            jnp.where(real, stream * stream, 0.0),
            branch_one * branch_one,
            branch_two * branch_two,
            jnp.where(real, mlp * upstream, 0.0),
            jnp.where(real, attn * middle_grad, 0.0),
            grad * unit,
            grad,
        ],
    )


def token_back_kernel(second, real, tokens, full, ready, outs, sums):
    *grad_refs, x_ref, middle_ref = tokens
    (scale,) = full
    (out_ref,) = outs
    (sum_ref,) = sums
    unit, root = normalize(x_ref[...].astype(WIDE))
    weight = ready(0)
    grad, column = None, 0
    for ref in grad_refs:
        part = dot(ref[...], weight[:, column : column + ref.shape[1]], NT)
        grad = part if grad is None else grad + part
        column += ref.shape[1]
    add_sums(sum_ref, second, [grad * unit, grad])
    scaled = grad * (1.0 + per_row(scale, second))
    total = middle_ref[...].astype(WIDE) + root * (
        scaled - jnp.mean(scaled, -1, keepdims=True) - unit * jnp.mean(scaled * unit, -1, keepdims=True)
    )
    out_ref[...] = total.astype(LOW)


def outer_kernel(half_ref, left_ref, right_ref, out_ref):
    out_ref[...] = dot(left_ref[...], right_ref[...], TN).astype(LOW)


def outer(left, right, half):
    count, height = left.shape
    width = right.shape[1] // 2
    tall = min(height, 1024)
    wide = min(width, 1024 if width % 1024 == 0 else 768 if width % 768 == 0 else 512)
    steps = width // wide
    return pl.pallas_call(
        outer_kernel,
        grid_spec=pltpu.PrefetchScalarGridSpec(
            num_scalar_prefetch=1,
            grid=(height // tall, steps),
            in_specs=[
                pl.BlockSpec((count, tall), lambda i, j, h: (0, i)),
                pl.BlockSpec((count, wide), lambda i, j, h: (0, h[0] * steps + j)),
            ],
            out_specs=pl.BlockSpec((tall, wide), lambda i, j, h: (i, j)),
        ),
        out_shape=jax.ShapeDtypeStruct((height, width), LOW),
        compiler_params=pltpu.CompilerParams(vmem_limit_bytes=28 << 20),
        cost_estimate=LIGHT,
        name="outer",
    )(half.reshape(1).astype(jnp.int32), far(left), far(right))


def outer_joint(left, rights, other_left, other_right, half):
    count, height = left.shape
    rights = [*rights, other_right]
    widths = [right.shape[1] // 4 for right in rights]
    total = sum(widths)
    whole = lambda v: pl.BlockSpec(v.shape, lambda j, h: (0, 0))
    part = lambda width: pl.BlockSpec((count, width), lambda j, h: (0, 2 * h[0] + j))

    def body(half_ref, left_ref, other_ref, *refs):
        *right_refs, out_ref = refs
        column = 0
        for number, (ref, width) in enumerate(zip(right_refs, widths)):
            source = other_ref if number == len(widths) - 1 else left_ref
            out_ref[:, column : column + width] = dot(source[...], ref[...], TN).astype(LOW)
            column += width

    return pl.pallas_call(
        body,
        grid_spec=pltpu.PrefetchScalarGridSpec(
            num_scalar_prefetch=1,
            grid=(2,),
            in_specs=[whole(left), whole(other_left)] + [part(width) for width in widths],
            out_specs=pl.BlockSpec((height, total), lambda j, h: (0, j)),
        ),
        out_shape=jax.ShapeDtypeStruct((height, 2 * total), LOW),
        compiler_params=pltpu.CompilerParams(vmem_limit_bytes=40 << 20),
        cost_estimate=LIGHT,
        name="outer_joint",
    )(half.reshape(1).astype(jnp.int32), far(left), far(other_left), *map(far, rights))


def plain_sum(place, keep, send):
    flip = place.c == 1
    full = jnp.concatenate([jnp.where(flip, send, keep), jnp.where(flip, keep, send)], 1)
    part = lax.psum_scatter(full, "fsdp", scatter_dimension=0, tiled=True)
    return lax.psum(part, "dp").astype(WIDE)


def shards(place_counts, tokens, cond, stop_scale, w_ada, w_qkv, w_proj, w_fc1, w_fc2, head_log_scale, cotangent):
    place = Place(*place_counts)
    items, width = cond.shape
    rows = tokens.shape[0]
    length = rows // items
    heads = head_log_scale.shape[0]
    pairs = heads // 2
    hidden_width = w_fc1.shape[1]
    ends = jnp.asarray(np.cumsum([side * side for side in PATCHES]).astype(np.int32))
    lengths = jnp.sum(jnp.where(jnp.arange(len(PATCHES))[None, :] == stop_scale[:, None], ends[None, :], 0), 1)

    def by_pair(matrix):
        return jnp.swapaxes(matrix.reshape(matrix.shape[0], 3, pairs, 128), 1, 2).reshape(matrix.shape)

    def from_pair(matrix):
        return jnp.swapaxes(matrix.reshape(matrix.shape[0], pairs, 3, 128), 1, 2).reshape(matrix.shape)

    paired = by_pair(w_qkv)
    half = paired.shape[1] // 2
    cond_wide = cond.astype(WIDE)
    silu_cond = (cond_wide * jax.nn.sigmoid(cond_wide)).astype(LOW)
    ada_rows = w_ada.shape[0]
    group_count = items * place.fsdp_count
    ada_columns = (0, place.fsdp_index * ada_rows)

    def part_modulation(group_cond):
        return dot(lax.dynamic_slice(group_cond, ada_columns, (group_count, ada_rows)), w_ada)

    if place.grouped:
        unit_rows = w_qkv.shape[0]
        cond_stack = small_over_z(silu_cond)
        own_qkv, cond_stack = tie(own_quarter(place, paired), cond_stack)
        qkv = Gather(own_qkv)
        qkv.over_z()
        mixed = scatter_over_x(place, part_modulation(small_over_x(place, cond_stack)))
        qkv.stack, mixed = tie(qkv.stack, mixed)
        qkv.over_xy()
        modulation = scatter_over_z(place, mixed)
        own_rest = jnp.concatenate([own_quarter(place, w_proj), own_quarter(place, w_fc1)], 1)
        own_rest, modulation = tie(own_rest, modulation)
        rest = Gather(own_rest)
        rest.over_z()
        qkv.over_both()
        qkv.over_core_first()
        rest.stack, *qkv.from_both = tie(rest.stack, *qkv.from_both)
        qkv_parts = qkv.over_core()
        piece = w_fc2.shape[0] // place.dp_count
        fc2_piece = lax.dynamic_slice(w_fc2, (place.dp_index * piece, 0), (piece, width))
        fc2_piece, rest.stack = tie(fc2_piece, rest.stack)
        rest.over_xy()
        fc2_full = lax.all_gather(fc2_piece, ("fsdp", "dp"), axis=0, tiled=True)
        quarter = half // 2
        qkv_weight = (qkv_parts, [(0, quarter, unit_rows, 0)], (width, 2 * half))
        fc2_weight = ([fc2_full], 0, (hidden_width, width))
    else:
        qkv_weight, proj_weight, fc1_weight, fc2_weight = (
            ([lax.all_gather(w, "fsdp", axis=0, tiled=True)], 0, (w.shape[0] * place.fsdp_count, w.shape[1]))
            for w in (paired, w_proj, w_fc1, w_fc2)
        )
        modulation = lax.psum_scatter(
            part_modulation(gather_small(place, silu_cond, False)), "fsdp", scatter_dimension=0, tiled=True
        )
    gamma_one, gamma_two, scale_one, scale_two, shift_one, shift_two = [
        modulation[:, n * width : (n + 1) * width] for n in range(6)
    ]

    gain = jnp.repeat(jnp.exp(head_log_scale), width // heads)[None, :]
    normed_one, projected, roots = token_call(
        project_kernel, place, rows, length, lengths, [tokens], [scale_one, shift_one, gain],
        [qkv_weight], [(width, LOW), (3 * width, LOW), (width, LOW)], 0, "project",
    )
    if place.grouped:
        rest.from_x, rest.from_y, projected = tie(rest.from_x, rest.from_y, projected)
        rest.over_both()
        rest.over_core_first()
    cube = (items, length, width)
    projected, roots = projected.reshape(items, length, 3 * width), roots.reshape(cube)
    query_mask, key_mask = mask_tables(length)
    attended, extra = attend(projected, query_mask, key_mask)
    if place.grouped:
        attended, *rest.from_both = tie(attended, *rest.from_both)
        rest_parts = rest.over_core()
        proj_weight = (rest_parts, [(0, width // 4, unit_rows, 0)], (width, width))
        fc1_weight = (
            rest_parts, [(width // 4, hidden_width // 4, unit_rows, 0)], (width, hidden_width)
        )
    flat_attended = attended.reshape(rows, width)
    (
        result, normed_two, act, grad_mlp, grad_hidden, grad_middle, grad_attn, grad_attended, sum_one,
    ) = token_call(
        block_kernel, place, rows, length, lengths, [flat_attended, tokens, cotangent],
        [gamma_one, gamma_two, scale_two, shift_two], [proj_weight, fc1_weight, fc2_weight],
        [(width, LOW), (width, LOW), (hidden_width, LOW), (width, LOW), (hidden_width, LOW)]
        + [(width, LOW)] * 3, 1, "block",
    )

    def small_group(sum_four):
        head_terms = jnp.concatenate([heads_first, heads_second], 2).reshape(items, heads, width // heads).sum(2)
        head_parts = jnp.concatenate([*two_parts(head_terms), jnp.zeros((items, 128 - 2 * heads), LOW)], 1)
        grad_modulation = jnp.concatenate(
            [sum_one[8:10], sum_one[6:8], sum_four[0:2], sum_one[10:12], sum_four[2:4], sum_one[12:14]], 1
        ).astype(LOW)
        return jnp.concatenate([grad_modulation, head_parts, silu_cond], 1)

    def send_part(left, right):
        return outer(left, right, 1 - place.c)

    def keep_part(left, right):
        return outer(left, right, place.c)

    def heads_back(grad, first):
        out, sums = attend_back(
            projected, extra, key_mask, attended, grad.reshape(cube), roots, gain, first, pairs // 2
        )
        return out.reshape(rows, half), sums

    def token_back(first, second):
        return token_call(
            token_back_kernel, place, rows, length, lengths, [first, second, tokens, grad_middle],
            [scale_one], [qkv_weight], [(width, LOW)], 1, "token_back",
        )

    if place.grouped:
        quarter = width // 4
        fc2_send = send_part(act, grad_mlp)
        fc2_keep, arrived = beside(lambda g: keep_part(act, g), grad_mlp, [(fc2_send, {"dc": 1})])
        fc2 = RowSum(fc2_keep, arrived[0], w_fc2.shape[0], "mixed")
        (sums,) = add_blocks(place, [fc2.first()], "sums_a")

        (grad_first, heads_first), arrived = beside(
            lambda g: heads_back(g, 0), grad_attended, fc2.moves(sums)
        )
        (sums,) = add_blocks(place, [fc2.second(arrived)], "sums_b")

        fc1_send, fc2_arrived = beside(
            lambda g: send_part(normed_two, g), tie(grad_hidden, grad_first)[0], fc2.moves(sums)
        )
        fc1_keep, arrived = beside(lambda g: keep_part(normed_two, g), grad_hidden, [(fc1_send, {"dc": 1})])
        fc1 = RowSum(fc1_keep, arrived[0], unit_rows, "mixed")
        fc1_sums, fc2_sums = add_blocks(place, [fc1.first(), fc2.third(fc2_arrived)], "sums_c")

        (grad_second, heads_second), arrived = beside(
            lambda g: heads_back(g, pairs // 2), grad_attended, fc1.moves(fc1_sums) + fc2.moves(fc2_sums)
        )
        fc1_sums, (fc2_own,) = add_blocks(
            place, [fc1.second(arrived[:2]), fc2.last(arrived[2:])], "sums_d"
        )
        joint = functools.partial(outer_joint, normed_one, [grad_first, grad_second], flat_attended)
        last_send, (*fc1_arrived, fc2_y, fc2_c) = beside(
            lambda g: joint(g, 1 - place.c),
            tie(grad_attn, grad_second)[0],
            fc1.moves(fc1_sums) + [(fc2_own, {"dy": 1}), (fc2_own, {"dc": 1})],
        )
        last_keep, (arrived, fc2_both) = beside(
            lambda g: joint(g, place.c), grad_attn, [(last_send, {"dc": 1}), (fc2_y, {"dc": 1})]
        )
        last = RowSum(last_keep, arrived, unit_rows, "mixed")
        fc1_sums, last_sums = add_blocks(place, [fc1.third(fc1_arrived), last.first()], "sums_e")

        (grad_tokens, sum_four), arrived = beside(
            lambda g: token_back(grad_first, g), grad_second, last.moves(last_sums) + fc1.moves(fc1_sums)
        )
        last_sums, (fc1_own,) = add_blocks(place, [last.second(arrived[:2]), fc1.last(arrived[2:])], "sums_f")
        group = small_group(sum_four)
        moves = last.moves(last_sums)
        sent, group = tie(tuple(v for v, _ in moves), group)
        arrived = [hop(v, **axes) for v, (_, axes) in zip(sent, moves)]
        group_stack = small_over_z(group)
        arrived, group_stack = tie(arrived, group_stack)
        (last_sums,) = add_blocks(place, [last.third(arrived)], "sums_g")
        sent, group_stack = tie(tuple(last_sums), group_stack)
        arrived = [hop(v, **axes) for v, axes in last.moves(sent)]
        group = small_over_x(place, group_stack)
        fc1_y = hop(fc1_own, dy=1)
        ((last_own,),) = add_blocks(place, [last.last(arrived)], "sums_h")
        last_all = spread(last_own)
        fc1_core = [hop(fc1_own, dc=1), hop(fc1_y, dc=1)]
        (grad_fc2,) = lay_out(
            place, [fc2_own, fc2_y, fc2_c, fc2_both], [[(0, 0, quarter, 0, 0, quarter)]], [w_fc2.shape],
            "lay_out_fc2",
        )
        wide = hidden_width // 4
        (grad_fc1,) = lay_out(
            place, [fc1_own, fc1_y] + fc1_core, [[(0, 0, wide, 0, 0, wide)]], [w_fc1.shape], "lay_out_fc1"
        )
        layout = [
            (0, 384 * side + 128 * n, 128, 0, n * width + 512 * side, 128) for side in range(2) for n in range(3)
        ]
        layout.append((1, 768, quarter, 0, 0, quarter))
        grad_qkv, grad_proj = lay_out(
            place, last_all, [layout], [w_qkv.shape, w_proj.shape], "lay_out_last"
        )
    else:
        def whole_sum(left, right):
            return plain_sum(place, keep_part(left, right), send_part(left, right))

        grad_fc2 = whole_sum(act, grad_mlp)
        grad_fc1 = whole_sum(normed_two, grad_hidden)
        grad_proj = whole_sum(flat_attended, grad_attn)
        grad_first, heads_first = heads_back(grad_attended, 0)
        grad_second, heads_second = heads_back(grad_attended, pairs // 2)
        grad_qkv = from_pair(
            jnp.concatenate([whole_sum(normed_one, grad_first), whole_sum(normed_one, grad_second)], 1)
        )
        grad_tokens, sum_four = token_back(grad_first, grad_second)
        group = gather_small(place, small_group(sum_four), False)

    grad_columns = dot(group[:, : 6 * width], w_ada, NT)
    everything = over_dp(place, group)
    all_heads = everything[:, 6 * width : 6 * width + 2 * heads].astype(WIDE)
    grad_head = jnp.sum(all_heads[:, :heads] + all_heads[:, heads:], 0)
    all_slice = lax.dynamic_slice(
        everything, (0, 6 * width + 128 + place.fsdp_index * ada_rows), (everything.shape[0], ada_rows)
    )
    grad_ada = dot(all_slice, everything[:, : 6 * width], TN)
    grad_parts = gather_small(place, grad_columns[None], False)
    own_items = lax.dynamic_slice(
        grad_parts, (0, place.fsdp_index * items, 0), (grad_parts.shape[0], items, ada_rows)
    )
    grad_silu = jnp.swapaxes(own_items, 0, 1).reshape(items, width)
    gate = jax.nn.sigmoid(cond_wide)
    grad_cond = (grad_silu * gate * (1.0 + cond_wide * (1.0 - gate))).astype(LOW)

    counted = (lengths * width).astype(WIDE)
    squares = jnp.stack(
        [sum_one[0:2].sum(1), sum_one[2:4].sum(1), sum_one[4:6].sum(1)], 1
    )
    rms_rows = jnp.sqrt(squares / counted[:, None] + EPS)
    return (
        result, grad_tokens, grad_cond, grad_ada, grad_qkv, grad_proj, grad_fc1, grad_fc2,
        grad_head, rms_rows,
    )


def solution(mesh):
    both = P(("dp", "fsdp"), None)
    rows = P("fsdp", None)
    return jax.shard_map(
        functools.partial(shards, (mesh.shape["dp"], mesh.shape["fsdp"])),
        mesh=mesh,
        in_specs=(both, both, P(("dp", "fsdp")), rows, rows, rows, rows, rows, P(), both),
        out_specs=(both, both, both, rows, rows, rows, rows, rows, P(), both),
        check_vma=False,
    )
```
